32 devices in a mesh: seq: 2 (over x), ctx: 4 (over z), fsdp: 4 (over y, core).
Axes of the slice: x: 2, y: 2, z: 4, core: 2. Of those that a mesh axis runs over, the one named last changes fastest.
Arguments:
- tokens: bfloat16 [4096, 512], P(('seq', 'ctx', 'fsdp')), may hold values from -6 to 6
- lengths: int32 [2], P('seq'), may hold values from 1024 to 2048, as said below
- ln1_gain: bfloat16 [512], P('fsdp'), may hold values from 0.5 to 1.5
- ln1_bias: bfloat16 [512], P('fsdp'), may hold values from -1.1953125 to 1.1953125
- qkv_weight: bfloat16 [512, 1536], P('fsdp'), may hold values from -0.25 to 0.25
- out_weight: bfloat16 [512, 512], P('fsdp'), may hold values from -2 to 2
- ln2_gain: bfloat16 [512], P('fsdp'), may hold values from 0.5 to 1.5
- ln2_bias: bfloat16 [512], P('fsdp'), may hold values from -1.1953125 to 1.1953125
- up_weight: bfloat16 [512, 2048], P('fsdp'), may hold values from -0.25 to 0.25
- up_bias: bfloat16 [2048], P('fsdp'), may hold values from -2 to 2
- down_weight: bfloat16 [2048, 512], P('fsdp'), may hold values from -0.125 to 0.125
- down_bias: bfloat16 [512], P('fsdp'), may hold values from -1.1953125 to 1.1953125
- cotangent: bfloat16 [4096, 512], P(('seq', 'ctx', 'fsdp')), may hold values from -6 to 6
Outputs:
- layer_out: bfloat16 [4096, 512], P(('seq', 'ctx', 'fsdp'))
- input_grad: float32 [4096, 512], P(('seq', 'ctx', 'fsdp'))
- ln1_gain_grad: float32 [512], P('fsdp')
- ln1_bias_grad: float32 [512], P('fsdp')
- qkv_weight_grad: float32 [512, 1536], P('fsdp')
- out_weight_grad: float32 [512, 512], P('fsdp')
- ln2_gain_grad: float32 [512], P('fsdp')
- ln2_bias_grad: float32 [512], P('fsdp')
- up_weight_grad: float32 [512, 2048], P('fsdp')
- up_bias_grad: float32 [2048], P('fsdp')
- down_weight_grad: float32 [2048, 512], P('fsdp')
- down_bias_grad: float32 [512], P('fsdp')
- rms_stats: float32 [3], replicated
The draws below stay inside these ranges and needn't reach their ends.
Inputs may be any that keep to these rules, and one draw needn't show every extreme that they name: `lengths`: one sequence has all 2048 positions valid; the length of each other one is drawn between 1024 and 2048.
All inputs are finite; a program needn't handle non-finite values.
Results may differ from the reference program's by a relative error of at most 0.017.
Values may be sent and summed in bfloat16 or wider, within the bound.
A program may use at most 320 MiB of HBM per device.

```python
import math
import jax
import jax.numpy as jnp
from jax import lax

D = 512
HEADS = 8
HEAD_DIM = 64
FF = 2048
SEQS = 2
SEQLEN = 2048
ROWS = 4096


def draw_lengths(key, part):
    shorter = jax.random.randint(jax.random.fold_in(key, 11), (SEQS,), SEQLEN // 2, SEQLEN + 1)
    chosen = jax.random.randint(jax.random.fold_in(key, 12), (), 0, SEQS)
    return jnp.where(jnp.arange(SEQS) == chosen, SEQLEN, shorter).astype(jnp.int32)


def shard_levels(own_key, dims, cuts, least, top_value):
    factor_of, own = 1.0, jax.random.fold_in(own_key, 6)
    for dim, parts in cuts:
        heights = jnp.exp(jax.random.uniform(jax.random.fold_in(own, dim), (parts,), jnp.float32, least / len(cuts), top_value / len(cuts)))
        factor_of = factor_of * jnp.repeat(heights, dims[dim] // parts).reshape([-1 if axis == dim else 1 for axis in range(len(dims))])
    return factor_of


def scatter_about(rng, shape, scale, most, shards=(), kind=jnp.bfloat16):
    entries = scale * jax.random.normal(rng, shape, jnp.float32)
    if shards:
        entries = entries * shard_levels(rng, shape, shards, -0.22, 0.18)
    return jnp.clip(entries, -most, most).astype(kind)


def setup_inputs(seed: int = 0) -> dict:
    streams_of = jax.random.split(jax.random.key(seed), 14)
    tokens = scatter_about(streams_of[0], (ROWS, D), 1.0, 6.0, ((0, 32),))
    lengths = draw_lengths(jax.random.fold_in(streams_of[13], 71), 0)
    ln1_gain = jnp.clip(1.0 + 0.1 * jax.random.normal(streams_of[2], (D,), jnp.float32), 0.5, 1.5).astype(jnp.bfloat16)
    ln1_bias = scatter_about(streams_of[3], (D,), 0.3, 1.1953125, ((0, 4),))
    qkv_weight = scatter_about(streams_of[4], (D, 3 * D), D ** -0.5, 0.25, ((0, 4),))
    out_weight = scatter_about(streams_of[5], (D, D), (D // 64) ** -0.5, 2.0, ((0, 4),))
    ln2_gain = jnp.clip(1.0 + 0.1 * jax.random.normal(streams_of[6], (D,), jnp.float32), 0.5, 1.5).astype(jnp.bfloat16)
    ln2_bias = scatter_about(streams_of[7], (D,), 0.3, 1.1953125, ((0, 4),))
    up_weight = scatter_about(streams_of[8], (D, FF), D ** -0.5, 0.25, ((0, 4),))
    up_bias = scatter_about(streams_of[9], (FF,), 0.5, 2.0, ((0, 4),))
    down_weight = scatter_about(streams_of[10], (FF, D), FF ** -0.5, 0.125, ((0, 4),))
    down_bias = scatter_about(streams_of[11], (D,), 0.3, 1.1953125, ((0, 4),))
    cotangent = scatter_about(streams_of[12], (ROWS, D), 1.0, 6.0, ((0, 32),))
    return {"tokens": tokens, "lengths": lengths, "ln1_gain": ln1_gain, "ln1_bias": ln1_bias, "qkv_weight": qkv_weight, "out_weight": out_weight, "ln2_gain": ln2_gain, "ln2_bias": ln2_bias, "up_weight": up_weight, "up_bias": up_bias, "down_weight": down_weight, "down_bias": down_bias, "cotangent": cotangent}


@jax.custom_vjp
def low(v):
    return lax.optimization_barrier(v.astype(jnp.bfloat16)).astype(jnp.float32)

@jax.custom_vjp
def low_back(v):
    return v

def low_keep(v):
    return (low(v), None)

def low_pass(kept, grad):
    return (grad,)

def back_keep(v):
    return (v, None)

def back_low(kept, grad):
    return (low(grad),)
low.defvjp(low_keep, low_pass)
low_back.defvjp(back_keep, back_low)
highest = lax.Precision.HIGHEST
epsilon = 1e-05
masked_value = -1e+30

def layer_norm(values, gain, bias):
    center = lax.optimization_barrier(jnp.mean(values, axis=1, keepdims=True))
    shifted = values - center
    spread = lax.optimization_barrier(jnp.mean(shifted * shifted, axis=1, keepdims=True))
    return shifted * lax.rsqrt(spread + epsilon) * gain + bias

def causal_attention(query, keys, values, valid):
    total, width = query.shape
    block = math.gcd(total, 512)
    count = total // block
    key_heads = keys.reshape(total, HEADS, HEAD_DIM)
    value_heads = values.reshape(total, HEADS, HEAD_DIM)
    key_pos = jnp.arange(total, dtype=jnp.int32)

    def attend_block(pieces):
        query_block, first = pieces
        scores = low_back(jnp.einsum('qhe,khe->hqk', query_block, key_heads, precision=highest))
        query_pos = first + jnp.arange(block, dtype=jnp.int32)
        allowed = (key_pos[None, :] <= query_pos[:, None]) & (key_pos[None, :] < valid)
        scores = jnp.where(allowed[None], scores, masked_value)
        probs = low(jax.nn.softmax(scores, axis=2))
        return jnp.einsum('hqk,khe->qhe', probs, value_heads, precision=highest)
    blocks = lax.map(jax.checkpoint(attend_block), (query.reshape(count, block, HEADS, HEAD_DIM), jnp.arange(count, dtype=jnp.int32) * block))
    return blocks.reshape(total, width)

def forward(inputs, valid, gain_first, shift_first, joint_weight, out_proj, gain_second, shift_second, up_proj, up_shift, down_proj, down_shift):
    width = inputs.shape[1]
    scale = HEAD_DIM ** (-0.5)
    normed = low(layer_norm(inputs, gain_first, shift_first))
    projected = jnp.dot(normed, joint_weight, precision=highest)
    query = low(low_back(projected[:, :width] * scale))
    keys = low(low_back(projected[:, width:2 * width]))
    values = low(low_back(projected[:, 2 * width:]))
    attended = low(low_back(causal_attention(query, keys, values, valid)))
    attention_out = low_back(jnp.dot(attended, out_proj, precision=highest))
    middle = inputs + attention_out
    normed_two = low(layer_norm(middle, gain_second, shift_second))
    raised = low_back(jnp.dot(normed_two, up_proj, precision=highest) + up_shift)
    activated = low(jax.nn.gelu(raised, approximate=False))
    feed_out = low_back(jnp.dot(activated, down_proj, precision=highest) + down_shift)
    return (middle + feed_out, attention_out, feed_out)

def reference(tokens, lengths, ln1_gain, ln1_bias, qkv_weight, out_weight, ln2_gain, ln2_bias, up_weight, up_bias, down_weight, down_bias, cotangent):
    params = tuple((param.astype(jnp.float32) for param in (ln1_gain, ln1_bias, qkv_weight, out_weight, ln2_gain, ln2_bias, up_weight, up_bias, down_weight, down_bias)))
    width = tokens.shape[1]
    count = lengths.shape[0]
    inputs = tokens.astype(jnp.float32).reshape(count, SEQLEN, width)
    cotangents = cotangent.astype(jnp.float32).reshape(count, SEQLEN, width)

    def per_sequence(carry, pieces):
        sequence, grads_out, valid = pieces

        def apply(values, *weights):
            return forward(values, valid, *weights)
        outputs, pull = jax.vjp(apply, sequence, *params)
        final, attention_out, feed_out = outputs
        grads = pull((grads_out, jnp.zeros_like(attention_out), jnp.zeros_like(feed_out)))
        carry = tuple((before + after for before, after in zip(carry, grads[1:])))
        live = (jnp.arange(SEQLEN, dtype=jnp.int32) < valid)[:, None]
        squares = jnp.stack([jnp.sum(jnp.where(live, value * value, 0.0)) for value in outputs])
        return (carry, (final, grads[0], squares))
    start = tuple((jnp.zeros_like(param) for param in params))
    totals, (finals, input_grads, squares) = lax.scan(per_sequence, start, (inputs, cotangents, lengths))
    live_count = jnp.sum(lengths).astype(jnp.float32)
    rms_stats = jnp.sqrt(lax.optimization_barrier(jnp.sum(squares, axis=0)) / (live_count * width))
    return (finals.reshape(-1, width).astype(jnp.bfloat16), input_grads.reshape(-1, width), totals[0], totals[1], totals[2], totals[3], totals[4], totals[5], totals[6], totals[7], totals[8], totals[9], rms_stats)
```

```python
from functools import partial

import jax
import jax.numpy as jnp
from jax import lax
from jax.sharding import PartitionSpec as P

HEADS = 8
HEAD_DIM = 64


epsilon = 1e-05
masked_value = -1e30
block_limit = 2048


def layer_norm(values, gain, bias):
    center = jnp.mean(values, axis=1, keepdims=True)
    shifted = values - center
    spread = jnp.mean(shifted * shifted, axis=1, keepdims=True)
    return shifted * lax.rsqrt(spread + epsilon) * gain + bias


def block_rows(count):
    block = count
    while block > block_limit and block % 2 == 0:
        block = block // 2
    return block


def allowed_keys(query_pos, first, block, valid):
    key_pos = first + jnp.arange(block, dtype=jnp.int32)
    return (key_pos[None, :] <= query_pos[:, None]) & (key_pos[None, :] < valid)


def split_keys(keys, values, first):
    count = keys.shape[0]
    block = block_rows(count)
    turns = count // block
    key_blocks = keys.reshape(turns, block, HEADS, HEAD_DIM)
    value_blocks = values.reshape(turns, block, HEADS, HEAD_DIM)
    offsets = first + block * jnp.arange(turns, dtype=jnp.int32)
    return (block, key_blocks, value_blocks, offsets)


def attend_run(state, query_heads, query_pos, valid, keys, values, first):
    block, key_blocks, value_blocks, offsets = split_keys(keys, values, first)
    latest = query_pos[-1]

    def attend_advance(carry, pieces):
        key_block, value_block, begin = pieces

        def attend_update(current):
            running, weights, weighted = current
            allowed = allowed_keys(query_pos, begin, block, valid)[None]
            scores = jnp.einsum(
                "qhe,khe->hqk", query_heads, key_block, preferred_element_type=jnp.float32
            )
            scores = jnp.where(allowed, scores, masked_value)
            raised = jnp.maximum(running, jnp.max(scores, axis=2))
            probs = jnp.where(allowed, jnp.exp(scores - raised[:, :, None]), 0.0)
            fade = jnp.exp(running - raised)
            weights = weights * fade + jnp.sum(probs, axis=2)
            weighted = weighted * fade[:, :, None] + jnp.einsum(
                "hqk,khe->hqe",
                probs.astype(jnp.bfloat16),
                value_block,
                preferred_element_type=jnp.float32,
            )
            return (raised, weights, weighted)

        passed = (begin > latest) | (begin >= valid)
        return (lax.cond(passed, lambda current: current, attend_update, carry), None)

    state, _ = lax.scan(attend_advance, state, (key_blocks, value_blocks, offsets))
    return state


def grad_queries(query_heads, grad_heads, log_total, delta, query_pos, valid, keys, values):
    block, key_blocks, value_blocks, offsets = split_keys(keys, values, 0)
    latest = query_pos[-1]
    start = jnp.zeros(query_heads.shape[1:2] + (query_heads.shape[0], HEAD_DIM), jnp.float32)

    def grad_advance(carry, pieces):
        key_block, value_block, begin = pieces

        def grad_update(current):
            allowed = allowed_keys(query_pos, begin, block, valid)[None]
            scores = jnp.einsum(
                "qhe,khe->hqk", query_heads, key_block, preferred_element_type=jnp.float32
            )
            probs = jnp.where(allowed, jnp.exp(scores - log_total[:, :, None]), 0.0)
            grad_probs = jnp.einsum(
                "qhe,khe->hqk", grad_heads, value_block, preferred_element_type=jnp.float32
            )
            grad_scores = (probs * (grad_probs - delta[:, :, None])).astype(jnp.bfloat16)
            return current + jnp.einsum(
                "hqk,khe->hqe", grad_scores, key_block, preferred_element_type=jnp.float32
            )

        passed = (begin > latest) | (begin >= valid)
        return (lax.cond(passed, lambda current: current, grad_update, carry), None)

    result, _ = lax.scan(grad_advance, start, (key_blocks, value_blocks, offsets))
    return result


def key_gradients(query_heads, grad_heads, log_total, delta, query_pos, valid, keys, values, first):
    block, key_blocks, value_blocks, offsets = split_keys(keys, values, first)
    latest = query_pos[-1]
    width = keys.shape[1]

    def key_advance(carry, pieces):
        key_block, value_block, begin = pieces

        def key_update(blocks):
            key_part, value_part = blocks
            allowed = allowed_keys(query_pos, begin, block, valid)[None]
            scores = jnp.einsum(
                "qhe,khe->hqk", query_heads, key_part, preferred_element_type=jnp.float32
            )
            probs = jnp.where(allowed, jnp.exp(scores - log_total[:, :, None]), 0.0)
            grad_probs = jnp.einsum(
                "qhe,khe->hqk", grad_heads, value_part, preferred_element_type=jnp.float32
            )
            grad_scores = (probs * (grad_probs - delta[:, :, None])).astype(jnp.bfloat16)
            value_grad = jnp.einsum(
                "hqk,qhe->khe",
                probs.astype(jnp.bfloat16),
                grad_heads,
                preferred_element_type=jnp.float32,
            )
            key_grad = jnp.einsum(
                "hqk,qhe->khe", grad_scores, query_heads, preferred_element_type=jnp.float32
            )
            return jnp.concatenate(
                [key_grad.reshape(block, width), value_grad.reshape(block, width)], axis=1
            )

        def nothing(blocks):
            return jnp.zeros((block, 2 * width), jnp.float32)

        passed = (begin > latest) | (begin >= valid)
        return (carry, lax.cond(passed, nothing, key_update, (key_block, value_block)))

    _, parts = lax.scan(key_advance, 0, (key_blocks, value_blocks, offsets))
    return parts.reshape(keys.shape[0], 2 * width)


def on_device(
    tokens,
    lengths,
    ln1_gain,
    ln1_bias,
    qkv_weight,
    out_weight,
    ln2_gain,
    ln2_bias,
    up_weight,
    up_bias,
    down_weight,
    down_bias,
    cotangent,
):
    local_rows, width = tokens.shape
    scale = HEAD_DIM ** (-0.5)
    offset = lax.axis_index(("ctx", "fsdp")) * local_rows
    valid = lengths[0]
    query_pos = offset + jnp.arange(local_rows, dtype=jnp.int32)
    gathered = (
        lax.all_gather(ln1_gain, "fsdp", axis=0, tiled=True),
        lax.all_gather(ln1_bias, "fsdp", axis=0, tiled=True),
        lax.all_gather(qkv_weight, "fsdp", axis=0, tiled=True),
        lax.all_gather(out_weight, "fsdp", axis=0, tiled=True),
        lax.all_gather(ln2_gain, "fsdp", axis=0, tiled=True),
        lax.all_gather(ln2_bias, "fsdp", axis=0, tiled=True),
        lax.all_gather(up_weight, "fsdp", axis=0, tiled=True),
        lax.all_gather(up_bias, "fsdp", axis=0, tiled=True),
        lax.all_gather(down_weight, "fsdp", axis=0, tiled=True),
        lax.all_gather(down_bias, "fsdp", axis=0, tiled=True),
    )
    (
        gain_low,
        shift_low,
        joint_weight,
        out_proj,
        gain_high,
        shift_high,
        up_proj,
        up_low,
        down_proj,
        down_low,
    ) = gathered
    gain_first = gain_low.astype(jnp.float32)
    shift_first = shift_low.astype(jnp.float32)
    gain_second = gain_high.astype(jnp.float32)
    shift_second = shift_high.astype(jnp.float32)
    up_shift = up_low.astype(jnp.float32)
    down_shift = down_low.astype(jnp.float32)
    inputs = tokens.astype(jnp.float32)
    normed = layer_norm(inputs, gain_first, shift_first).astype(jnp.bfloat16)
    projected = jnp.dot(normed, joint_weight, preferred_element_type=jnp.float32)
    query = (projected[:, :width] * scale).astype(jnp.bfloat16)
    key_rows = projected[:, width : 2 * width].astype(jnp.bfloat16)
    value_rows = projected[:, 2 * width :].astype(jnp.bfloat16)
    query_heads = query.reshape(local_rows, HEADS, HEAD_DIM)
    start_state = (
        jnp.full((HEADS, local_rows), masked_value, jnp.float32),
        jnp.zeros((HEADS, local_rows), jnp.float32),
        jnp.zeros((HEADS, local_rows, HEAD_DIM), jnp.float32),
    )
    state = attend_run(
        start_state,
        query_heads,
        query_pos,
        valid,
        lax.all_gather(key_rows, ("ctx", "fsdp"), axis=0, tiled=True),
        lax.all_gather(value_rows, ("ctx", "fsdp"), axis=0, tiled=True),
        jnp.int32(0),
    )
    running, weights, weighted = state
    log_total = running + jnp.log(weights)
    attended = jnp.transpose(weighted / weights[:, :, None], (1, 0, 2)).reshape(local_rows, width)
    attended_low = attended.astype(jnp.bfloat16)
    attention_out = jnp.dot(attended_low, out_proj, preferred_element_type=jnp.float32)
    middle = inputs + attention_out
    normed_two = layer_norm(middle, gain_second, shift_second).astype(jnp.bfloat16)
    raised = jnp.dot(normed_two, up_proj, preferred_element_type=jnp.float32) + up_shift
    activated = jax.nn.gelu(raised, approximate=False).astype(jnp.bfloat16)
    feed_out = jnp.dot(activated, down_proj, preferred_element_type=jnp.float32) + down_shift
    final = middle + feed_out
    live = (query_pos < valid).astype(jnp.float32)[:, None]
    totals = lax.psum(
        (
            jnp.sum(live * final * final),
            jnp.sum(live * attention_out * attention_out),
            jnp.sum(live * feed_out * feed_out),
            jnp.sum(live),
        ),
        ("seq", "ctx", "fsdp"),
    )
    rms_stats = jnp.sqrt(jnp.stack([totals[0], totals[1], totals[2]]) / (totals[3] * width))
    grad_final = cotangent.astype(jnp.float32)
    down_bias_grad = jnp.sum(grad_final, axis=0)
    down_weight_grad = jnp.einsum(
        "rf,rd->fd", activated, cotangent, preferred_element_type=jnp.float32
    )
    grad_act = jnp.einsum("rd,fd->rf", cotangent, down_proj, preferred_element_type=jnp.float32)
    _, gelu_pull = jax.vjp(partial(jax.nn.gelu, approximate=False), raised)
    grad_raised = gelu_pull(grad_act)[0].astype(jnp.bfloat16)
    up_bias_grad = jnp.sum(grad_raised, axis=0, dtype=jnp.float32)
    up_weight_grad = jnp.einsum(
        "rd,rf->df", normed_two, grad_raised, preferred_element_type=jnp.float32
    )
    grad_normed_two = jnp.einsum(
        "rf,df->rd", grad_raised, up_proj, preferred_element_type=jnp.float32
    )
    _, second_pull = jax.vjp(layer_norm, middle, gain_second, shift_second)
    grad_middle_norm, gain_two_grad, shift_two_grad = second_pull(grad_normed_two)
    grad_middle = grad_final + grad_middle_norm
    grad_branch = grad_middle.astype(jnp.bfloat16)
    out_weight_grad = jnp.einsum(
        "rd,re->de", attended_low, grad_branch, preferred_element_type=jnp.float32
    )
    grad_attended = jnp.einsum(
        "re,de->rd", grad_branch, out_proj, preferred_element_type=jnp.float32
    ).astype(jnp.bfloat16)
    grad_heads = grad_attended.reshape(local_rows, HEADS, HEAD_DIM)
    delta = jnp.transpose(
        jnp.sum(
            (grad_attended.astype(jnp.float32) * attended).reshape(local_rows, HEADS, HEAD_DIM),
            axis=2,
        )
    )
    back_keys, back_values = (
        lax.all_gather(key_rows, ("ctx", "fsdp"), axis=0, tiled=True),
        lax.all_gather(value_rows, ("ctx", "fsdp"), axis=0, tiled=True),
    )
    query_grad = grad_queries(
        query_heads, grad_heads, log_total, delta, query_pos, valid, back_keys, back_values
    )
    query_low = (
        jnp.transpose(query_grad, (1, 0, 2)).reshape(local_rows, width).astype(jnp.bfloat16) * scale
    )
    pair_grad = lax.psum_scatter(
        key_gradients(
            query_heads,
            grad_heads,
            log_total,
            delta,
            query_pos,
            valid,
            back_keys,
            back_values,
            jnp.int32(0),
        ),
        ("ctx", "fsdp"),
        scatter_dimension=0,
        tiled=True,
    )
    grad_projected = jnp.concatenate([query_low, pair_grad.astype(jnp.bfloat16)], axis=1)
    qkv_weight_grad = jnp.einsum(
        "rd,rc->dc", normed, grad_projected, preferred_element_type=jnp.float32
    )
    grad_normed = jnp.einsum(
        "rc,dc->rd", grad_projected, joint_weight, preferred_element_type=jnp.float32
    )
    _, first_pull = jax.vjp(layer_norm, inputs, gain_first, shift_first)
    grad_input_norm, gain_one_grad, shift_one_grad = first_pull(grad_normed)
    input_grad = grad_middle + grad_input_norm
    grads = (
        gain_one_grad,
        shift_one_grad,
        qkv_weight_grad,
        out_weight_grad,
        gain_two_grad,
        shift_two_grad,
        up_weight_grad,
        up_bias_grad,
        down_weight_grad,
        down_bias_grad,
    )
    mats = (grads[2], grads[3], grads[6], grads[8])
    wide = [m.astype(jnp.bfloat16).reshape(4, -1, 512) for m in mats]
    sizes = [w.shape[1] for w in wide]
    joined = jnp.concatenate(wide, axis=1).reshape(-1, 512)
    part = lax.psum_scatter(joined, "fsdp", scatter_dimension=0, tiled=True)
    part = lax.psum(part, ("seq", "ctx"))
    vecs = (grads[0], grads[1], grads[4], grads[5], grads[7], grads[9])
    vsum = lax.psum(jnp.concatenate(vecs), ("seq", "ctx", "fsdp"))
    place = lax.axis_index("fsdp")
    pieces = []
    at = 0
    for v in vecs:
        span = v.shape[0] // 4
        pieces.append(lax.dynamic_slice_in_dim(vsum, at + place * span, span, 0))
        at += v.shape[0]
    outs = []
    at = 0
    for m, size in zip(mats, sizes):
        outs.append(part[at : at + size].astype(jnp.float32).reshape(m.shape[0] // 4, m.shape[1]))
        at += size
    shares = (
        pieces[0], pieces[1], outs[0], outs[1], pieces[2], pieces[3], outs[2], pieces[4], outs[3], pieces[5],
    )
    return (
        final.astype(jnp.bfloat16),
        input_grad,
        shares[0],
        shares[1],
        shares[2],
        shares[3],
        shares[4],
        shares[5],
        shares[6],
        shares[7],
        shares[8],
        shares[9],
        rms_stats,
    )


def solution(mesh):
    return jax.shard_map(
        on_device,
        mesh=mesh,
        in_specs=(
            P(("seq", "ctx", "fsdp"), None),
            P("seq"),
            P("fsdp"),
            P("fsdp"),
            P("fsdp", None),
            P("fsdp", None),
            P("fsdp"),
            P("fsdp"),
            P("fsdp", None),
            P("fsdp"),
            P("fsdp", None),
            P("fsdp"),
            P(("seq", "ctx", "fsdp"), None),
        ),
        out_specs=(
            P(("seq", "ctx", "fsdp"), None),
            P(("seq", "ctx", "fsdp"), None),
            P("fsdp"),
            P("fsdp"),
            P("fsdp", None),
            P("fsdp", None),
            P("fsdp"),
            P("fsdp"),
            P("fsdp", None),
            P("fsdp"),
            P("fsdp", None),
            P("fsdp"),
            P(),
        ),
        check_vma=False,
    )
```

```python
from functools import partial
import itertools

import jax
import jax.numpy as jnp
from jax import lax
from jax.experimental import pallas as pl
from jax.experimental.pallas import tpu as pltpu
from jax.sharding import PartitionSpec as P

HEADS = 8
HEAD_DIM = 64
EPS = 1e-05
NEG = -1e30
F32 = jnp.float32
BF16 = jnp.bfloat16
MESH = pl.DeviceIdType.MESH
ROWS = 128
KEYS = 512

ERF_TOP = (
    0.00022905065861350646,
    0.0034082910107109506,
    0.050955695062380861,
    0.18520832239976145,
    1.128379143519084,
)
ERF_LOW = (
    -1.1791602954361697e-7,
    0.000023547966471313185,
    0.0010179625278914885,
    0.014070470171167667,
    0.11098505178285362,
    0.49746925110067538,
    1.0,
)


def mm(a, b, ca=1, cb=0):
    return lax.dot_general(a, b, (((ca,), (cb,)), ((), ())), preferred_element_type=F32)


def erf(x):
    x = jnp.clip(x, -3.832506856900711, 3.832506856900711)
    s = x * x
    top = jnp.full_like(s, ERF_TOP[0])
    for c in ERF_TOP[1:]:
        top = top * s + c
    low = jnp.full_like(s, ERF_LOW[0])
    for c in ERF_LOW[1:]:
        low = low * s + c
    return x * top / low


def row_norm(x):
    center = jnp.mean(x, axis=1, keepdims=True)
    shifted = x - center
    spread = jnp.mean(shifted * shifted, axis=1, keepdims=True)
    r = lax.rsqrt(spread + EPS)
    return shifted * r, r


class Plan:
    def __init__(self, seqs, ctx, fsdp):
        self.S, self.C, self.F = seqs, ctx, fsdp
        self.N = ctx * fsdp
        self.G = self.N // HEADS
        self.bits = []
        b = 1
        while b < ctx:
            self.bits.append(b)
            b *= 2

    def split(self, dev):
        s, c, f = dev
        p = c * self.F + f
        return p // self.G, p % self.G

    def at(self, s, p):
        return (s, p // self.F, p % self.F)

    def head_peer(self, dev, k):
        h, g = self.split(dev)
        return self.at(dev[0], ((h + k) % HEADS) * self.G + g)

    def flip_peer(self, dev):
        h, g = self.split(dev)
        return self.at(dev[0], (h + 1 - 2 * (h % 2)) * self.G + g)

    def sibling(self, dev, k):
        h, g = self.split(dev)
        return self.at(dev[0], h * self.G + (g + k) % self.G)

    def fsdp_low(self, dev):
        s, c, f = dev
        return (s, c, f + 1 - 2 * (f % 2))

    def fsdp_high(self, dev):
        s, c, f = dev
        return (s, c, (f + 2) % self.F)

    def seq_peer(self, dev):
        s, c, f = dev
        return ((s + 1) % self.S, c, f)

    def ctx_peer(self, dev, b):
        s, c, f = dev
        return (s, c + b - 2 * b * ((c // b) % 2), f)

    def greeted(self):
        base = [partial(self._head, k) for k in range(1, HEADS)]
        base += [partial(self._sib, k) for k in range(1, self.G)]
        base += [self.seq_peer]
        more = [self.fsdp_low, self.fsdp_high] + [partial(self._ctx, b) for b in self.bits]
        devs = list(itertools.product(range(self.S), range(self.C), range(self.F)))
        for extra in more:
            if not all(extra(d) in [p(d) for p in base] for d in devs):
                base.append(extra)
        return base

    def _head(self, k, dev):
        return self.head_peer(dev, k)

    def _sib(self, k, dev):
        return self.sibling(dev, k)

    def _ctx(self, b, dev):
        return self.ctx_peer(dev, b)


def body(plan, count_rows, lens, smalls, tok_in, cot_in, wq_in, wo_in, wu_in, wd_in,
         out_y, out_dx, out_dq, out_r, out_v, out_v1,
         small, tok, cot, wq, wo, wu, wd,
         msg_kv, msg_q, kv, kvt, qb, o_send, o_recv, ot, lse, do_send, do_recv,
         dkv, dkvs, dkvr, dkv_red, dkv_recv, dq_send, dq_recv, nall,
         gp, gr1, gs, gr2, gt, gr,
         v1, v1r, v1s, v1r2, v1t, v1r3, v0, vrecv, vacc,
         mid, act, graw, ra, sa, rb, sb, rc, sc, lsem, ssem, rsem, rfull):
    G, F, N = plan.G, plan.F, plan.N
    Gm = min(G, F)
    seq, ctx, fs = (lax.axis_index(a) for a in ("seq", "ctx", "fsdp"))
    me = (seq, ctx, fs)
    h, g = plan.split(me)
    fl, fh = fs % 2, fs // 2
    D = tok.shape[2]
    FF = wu.shape[1]
    valid = lens[0]
    counter = itertools.count()
    locals_ = itertools.count()

    greet = plan.greeted()
    bar = pltpu.get_barrier_semaphore()
    for peer in greet:
        pl.semaphore_signal(bar, inc=1, device_id=peer(me), device_id_type=MESH)
    pl.semaphore_wait(bar, len(greet))

    sent = []

    def send(src, dst, dev):
        n = next(counter)
        copy = pltpu.make_async_remote_copy(
            src_ref=src, dst_ref=dst, send_sem=ssem.at[n], recv_sem=rsem.at[n],
            device_id=dev, device_id_type=MESH)
        copy.start()
        sent.append(copy)
        return copy

    def local(src, dst):
        copy = pltpu.make_async_copy(src, dst, lsem.at[next(locals_)])
        copy.start()
        return copy

    low, high = plan.fsdp_low(me), plan.fsdp_high(me)
    fhigh = (fs + 2) % F
    head_dev = {k: plan.head_peer(me, k) for k in range(1, HEADS)}
    head_idx = {k: (h + k) % HEADS for k in range(1, HEADS)}
    sib_dev = {k: plan.sibling(me, k) for k in range(1, G)}
    sib_idx = {k: (g + k) % G for k in range(1, G)}

    l_small = local(smalls, small.at[fs])
    l_tok = local(tok_in, tok.at[h])
    sm_low = send(smalls, small.at[fs], low)
    sm_high = send(smalls, small.at[fs], high)
    shards = ((wq_in, wq, 128), (wo_in, wo, 128), (wu_in, wu, 128), (wd_in, wd, FF // F))

    def rows_of(w, step, which):
        return w.at[pl.ds(pl.multiple_of(which * step, step), step), :]

    w_high = [send(wq_in, rows_of(wq, 128, fs), high)]
    w_low = [send(wq_in, rows_of(wq, 128, fs), low)]
    tok_copies = [send(tok_in, tok.at[h], head_dev[k]) for k in (2, 4, 6)]
    for src, dst, step in shards[1:]:
        w_high.append(send(src, rows_of(dst, step, fs), high))
    for src, dst, step in shards[1:]:
        w_low.append(send(src, rows_of(dst, step, fs), low))
    l_w = [local(src, rows_of(dst, step, fs)) for src, dst, step in shards]
    l_cot = local(cot_in, cot)

    l_small.wait()
    sm_low.wait_recv()
    sm_high.wait_recv()
    sm_fwd = send(small.at[fhigh], small.at[fhigh], low)
    l_tok.wait()
    inputs = tok[h].astype(F32)
    n_one, r_one = row_norm(inputs)
    sm_fwd.wait_recv()

    def vec(first, many=1):
        return jnp.concatenate(
            [small[q, first + r : first + r + 1, :] for q in range(F) for r in range(many)], axis=1)

    gain1, bias1, gain2, bias2 = vec(0), vec(1), vec(2), vec(3)
    down_bias = vec(8)
    normed = (n_one * gain1 + bias1).astype(BF16)
    nall[h] = normed
    l_w[0].wait()
    w_low[0].wait_recv()
    base = pl.multiple_of(fh * 256, 256)
    other = pl.multiple_of((1 - fh) * 256, 256)
    part = mm(nall[h, :, pl.ds(base, 256)], wq[pl.ds(base, 256), :])
    w_high[0].wait_recv()
    f_q = send(rows_of(wq, 128, fhigh), rows_of(wq, 128, fhigh), low)
    f_q.wait_recv()
    proj = part + mm(nall[h, :, pl.ds(other, 256)], wq[pl.ds(other, 256), :])

    lane = lax.broadcasted_iota(jnp.int32, (ROWS, 128), 1)
    left = lane < 64
    for i in range(HEADS // 2):
        kb = proj[:, D + 128 * i : D + 128 * (i + 1)]
        vb = proj[:, 2 * D + 128 * i : 2 * D + 128 * (i + 1)]
        msg_kv[2 * i] = jnp.where(left, kb, pltpu.roll(vb, 64, 1)).astype(BF16)
        msg_kv[2 * i + 1] = jnp.where(left, pltpu.roll(kb, 64, 1), vb).astype(BF16)
        qt = (proj[:, 128 * i : 128 * (i + 1)] * (HEAD_DIM ** -0.5)).T.astype(BF16)
        msg_q[2 * i] = qt[:64]
        msg_q[2 * i + 1] = qt[64:]
    kv_in, q_in = {}, {}
    for k in range(1, HEADS):
        kv_in[k] = send(msg_kv.at[head_idx[k]], kv.at[h, g], head_dev[k])
    for k in range(1, HEADS):
        q_in[k] = send(msg_q.at[head_idx[k]], qb.at[h], head_dev[k])
    kv[h, g] = msg_kv[h]
    qb[h] = msg_q[h]
    for k in range(1, HEADS):
        kv_in[k].wait_recv()
    kv_sib = {k: send(kv.at[:, g], kv.at[:, g], sib_dev[k]) for k in range(1, G)}
    w_high[1].wait_recv()
    fwd_w = {1: send(rows_of(wo, 128, fhigh), rows_of(wo, 128, fhigh), low)}
    for k in range(1, HEADS):
        q_in[k].wait_recv()
    for k in range(1, G):
        kv_sib[k].wait_recv()

    tiles = HEADS // 2
    per = 2 * G * ROWS // KEYS
    blocks = KEYS // ROWS

    def chunk_of(ref, kc):
        if G >= blocks:
            b0 = kc * blocks
            return ref.at[b0 // G, pl.ds(lax.rem(b0, G), blocks)]
        return ref.at[pl.ds(kc * (blocks // G), blocks // G)]

    def limits(i):
        col = lax.broadcasted_iota(jnp.int32, (1, 2 * ROWS), 1)
        pos = ((2 * i + col // ROWS) * G + g) * ROWS + col % ROWS
        return jnp.minimum(pos + 1, valid)

    key_iota = lax.broadcasted_iota(jnp.int32, (KEYS, 2 * ROWS), 0)
    nothing = jnp.zeros((HEAD_DIM, 2 * ROWS), BF16)

    @pl.loop(0, N * ROWS // KEYS)
    def _(kc):
        piece = chunk_of(kv, kc)[...].reshape(KEYS, 128)
        kvt[kc] = piece.astype(F32).T.astype(BF16)

    @pl.loop(0, tiles)
    def _(i):
        qt = jnp.concatenate([qb[2 * i], qb[2 * i + 1]], axis=1)
        stacked = jnp.concatenate([qt, nothing], axis=0)
        limit = limits(i)

        def step(kc, carry):
            m, l, acc = carry
            piece = chunk_of(kv, kc)[...].reshape(KEYS, 128)
            st = mm(piece, stacked)
            st = jnp.where(key_iota < limit - kc * KEYS, st, NEG)
            mn = jnp.maximum(m, jnp.max(st, axis=0, keepdims=True))
            e = jnp.exp(st - mn)
            al = jnp.exp(m - mn)
            l = l * al + jnp.sum(e, axis=0, keepdims=True)
            acc = acc * al + mm(kvt[kc, 64:128, :], e.astype(BF16))
            return mn, l, acc

        m, l, acc = lax.fori_loop(
            0, (i + 1) * per, step,
            (jnp.full((1, 2 * ROWS), NEG, F32), jnp.zeros((1, 2 * ROWS), F32),
             jnp.zeros((HEAD_DIM, 2 * ROWS), F32)))
        o = acc / l
        ot[i] = o
        lse[i] = m + jnp.log(l)
        o_send[2 * i] = o[:, :ROWS].astype(BF16)
        o_send[2 * i + 1] = o[:, ROWS:].astype(BF16)

    o_in = {k: send(o_send.at[head_idx[k]], o_recv.at[h], head_dev[k]) for k in range(1, HEADS)}
    o_recv[h] = o_send[h]

    w_high[2].wait_recv()
    fwd_w[2] = send(rows_of(wu, 128, fhigh), rows_of(wu, 128, fhigh), low)
    parity = h % 2
    flip = plan.flip_peer(me)
    for copy in tok_copies:
        copy.wait_recv()
    tok4 = lambda ref, q: ref.at[:, q]
    tok_flip = send(tok4(tok.reshape(HEADS // 2, 2, ROWS, D), parity),
                    tok4(tok.reshape(HEADS // 2, 2, ROWS, D), parity), flip)
    for k in range(1, HEADS):
        o_in[k].wait_recv()

    for q in range(1, 4):
        l_w[q].wait()
        w_low[q].wait_recv()
    l_cot.wait()
    fwd_w[1].wait_recv()
    at_t = o_recv[...].reshape(D, ROWS)
    attention_out = mm(at_t, wo[...], 0, 0)
    middle = tok[h].astype(F32) + attention_out
    n_two, r_two = row_norm(middle)
    normed_two = (n_two * gain2 + bias2).astype(BF16)
    fwd_w[2].wait_recv()
    w_high[3].wait_recv()
    fwd_w[3] = send(rows_of(wd, FF // F, fhigh), rows_of(wd, FF // F, fhigh), low)
    mid[...] = jnp.zeros_like(mid)
    fwd_w[3].wait_recv()
    cots = cot[...]
    span = FF // F

    gnt = jnp.zeros((ROWS, D), F32)
    feed = jnp.zeros((ROWS, D), F32)
    for q in range(F):
        cols = slice(q * span, (q + 1) * span)
        bias = jnp.concatenate([small[q, 4 + r : 5 + r, :] for r in range(span // 128)], axis=1)
        raised = mm(normed_two, wu[:, cols]) + bias
        cdf = 0.5 * (1.0 + erf(raised * (0.5 ** 0.5)))
        pdf = jnp.exp(-0.5 * raised * raised) * 0.3989422804014327
        a = (raised * cdf).astype(BF16)
        act[:, cols] = a
        grad = (mm(cots, wd[cols, :], 1, 1) * (cdf + raised * pdf)).astype(BF16)
        graw[:, cols] = grad
        gnt = gnt + mm(grad, wu[:, cols], 1, 1)
        feed = feed + mm(a, wd[cols, :])
        v0[q, 2:6, :] = jnp.concatenate(
            [jnp.sum(grad[:, 128 * r : 128 * (r + 1)].astype(F32), axis=0, keepdims=True)
             for r in range(span // 128)], axis=0)

    def scatter_row(ref, row, x):
        for q in range(F):
            ref[q, row : row + 1, :] = x[:, 128 * q : 128 * (q + 1)]

    grad_final = cots.astype(F32)
    e2 = gnt * gain2
    grad_middle = grad_final + r_two * (
        e2 - jnp.mean(e2, axis=1, keepdims=True) - n_two * jnp.mean(e2 * n_two, axis=1, keepdims=True))
    mid[...] = grad_middle
    gb = grad_middle.astype(BF16)
    ga = mm(wo[...], gb, 1, 1).astype(BF16)
    do_send[...] = ga.reshape(HEADS, HEAD_DIM, ROWS)
    do_in = {k: send(do_send.at[head_idx[k]], do_recv.at[h], head_dev[k]) for k in range(1, HEADS)}
    do_recv[h] = do_send[h]

    for q in range(F):
        cols = slice(q * span, (q + 1) * span)
        rfull[q // 2, q % 2, 0:512, :] = mm(act[:, cols], cots, 0, 0).astype(BF16)
    for q in range(F):
        cols = slice(q * span, (q + 1) * span)
        u = mm(normed_two, graw[:, cols], 0, 0).astype(BF16)
        for p in range(F):
            rfull[p // 2, p % 2, 512 + 128 * q : 640 + 128 * q, :] = u[128 * p : 128 * (p + 1)]
    og = mm(at_t, gb).astype(BF16)
    for p in range(F):
        rfull[p // 2, p % 2, 1024:1152, :] = og[128 * p : 128 * (p + 1)]

    feed_out = feed + down_bias
    final = middle + feed_out
    out_y[...] = final.astype(BF16)
    scatter_row(v0, 0, jnp.sum(gnt * n_two, axis=0, keepdims=True))
    scatter_row(v0, 1, jnp.sum(gnt, axis=0, keepdims=True))
    scatter_row(v0, 6, jnp.sum(grad_final, axis=0, keepdims=True))
    place = (ctx * F + fs) * ROWS
    row = lax.broadcasted_iota(jnp.int32, (ROWS, 1), 0) + place
    live = (row < valid).astype(F32)

    def total(x):
        return jnp.sum(jnp.sum(x, axis=1, keepdims=True) * live, axis=0, keepdims=True)

    lane1 = lax.broadcasted_iota(jnp.int32, (1, 128), 1)
    stats = jnp.where(lane1 == 0, total(final * final), 0.0)
    stats = jnp.where(lane1 == 1, total(attention_out * attention_out), stats)
    stats = jnp.where(lane1 == 2, total(feed_out * feed_out), stats)
    stats = jnp.where(lane1 == 3, jnp.sum(live, axis=0, keepdims=True), stats)
    for q in range(F):
        v0[q, 7:8, :] = stats

    def add_rows(dst, a, b, rows):
        block = 32 if rows % 32 == 0 else 16

        @pl.loop(0, rows // block)
        def _(t):
            at = pl.ds(pl.multiple_of(t * block, block), block)
            dst[at, :] = (a[at, :].astype(F32) + b[at, :].astype(F32)).astype(BF16)

    class Part:
        def __init__(self, first, rows):
            self.first, self.rows, self.stage, self.copy = first, rows, -1, None
            self.steps = [(plan.seq_peer(me), seq)] if plan.S == 2 else []
            self.steps += [(plan.ctx_peer(me, b), (ctx // b) % 2) for b in plan.bits]

        def rng(self):
            return pl.ds(self.first, self.rows)

        def pump(self):
            self.stage += 1
            t = self.stage
            r = self.rng()
            if t == 0:
                self.copy = send(rfull.at[:, 1 - fl, r, :], ra.at[:, r, :], low)
                return
            if t == 1:
                self.copy.wait_recv()
                for y in range(2):
                    add_rows(sa.at[y, r, :], rfull.at[y, fl, r, :], ra.at[y, r, :], self.rows)
                self.copy = send(sa.at[1 - fh, r, :], rb.at[r, :], high)
                return
            if t == 2:
                self.copy.wait_recv()
                add_rows(sb.at[r, :], sa.at[fh, r, :], rb.at[r, :], self.rows)
                self.piece, self.n, self.off, self.used = sb.at[r, :], self.rows, self.first, 0
                self.trail = []
                self.begin(0)
                return
            n_steps = len(self.steps)
            if t < 3 + n_steps:
                self.finish(t - 3)
                if t - 3 + 1 < n_steps:
                    self.begin(t - 3 + 1)
                else:
                    self.spread(len(self.trail) - 1)
                return
            self.copy.wait_recv()
            k = self.back
            self.off, self.n = self.trail[k][1], self.trail[k][2]
            self.spread(k - 1)

        def begin(self, k):
            dev, bit = self.steps[k]
            self.halve = self.n % 32 == 0
            start = self.first + self.used
            if self.halve:
                half = self.n // 2
                src = self.piece.at[pl.ds(pl.multiple_of((1 - bit) * half, 16), half), :]
                self.into = rc.at[pl.ds(start, half), :]
            else:
                src = self.piece
                self.into = rc.at[pl.ds(start, self.n), :]
            self.copy = send(src, self.into, dev)

        def finish(self, k):
            dev, bit = self.steps[k]
            self.copy.wait_recv()
            last = k + 1 == len(self.steps)
            if self.halve:
                half = self.n // 2
                self.trail.append((dev, self.off, self.n))
                mine = self.piece.at[pl.ds(pl.multiple_of(bit * half, 16), half), :]
                self.off = self.off + bit * half
                size = half
            else:
                mine, size = self.piece, self.n
            start = self.first + self.used
            self.used += size
            if last:
                dst = out_r.at[pl.ds(pl.multiple_of(self.off, 16), size), :]
            else:
                dst = sc.at[pl.ds(start, size), :]
            add_rows(dst, mine, self.into, size)
            self.piece, self.n = dst, size

        def spread(self, k):
            self.back = k
            if k < 0:
                self.copy = None
                return
            dev = self.trail[k][0]
            region = out_r.at[pl.ds(pl.multiple_of(self.off, 16), self.n), :]
            self.copy = send(region, region, dev)

        @property
        def done(self):
            return self.stage >= 3 and self.copy is None

    parts = [Part(0, 512), Part(512, 640)]

    class Vectors:
        def __init__(self):
            self.steps = [low, high] + ([plan.seq_peer(me)] if plan.S == 2 else [])
            self.steps += [plan.ctx_peer(me, b) for b in plan.bits]
            self.t = 0
            self.copy = send(v0, vrecv.at[0], self.steps[0])

        def pump(self):
            if self.t == len(self.steps):
                return
            t = self.t
            self.copy.wait_recv()
            src = v0[...] if t == 0 else vacc[t - 1]
            vacc[t] = src + vrecv[t]
            self.t += 1
            if self.t < len(self.steps):
                self.copy = send(vacc.at[t], vrecv.at[self.t], self.steps[self.t])

    vectors = Vectors()
    for p in parts:
        p.pump()

    tok_flip.wait_recv()

    @pl.loop(0, HEADS)
    def _(j):
        n, _ = row_norm(tok[j].astype(F32))
        nall[j] = (n * gain1 + bias1).astype(BF16)

    for k in range(1, HEADS):
        do_in[k].wait_recv()
    for p in parts:
        p.pump()
    vectors.pump()

    dkv[...] = jnp.zeros_like(dkv)

    @pl.loop(0, tiles)
    def _(t):
        i = tiles - 1 - t
        qt = jnp.concatenate([qb[2 * i], qb[2 * i + 1]], axis=1)
        dt = jnp.concatenate([do_recv[2 * i], do_recv[2 * i + 1]], axis=1)
        stacked = jnp.concatenate(
            [jnp.concatenate([qt, nothing], axis=1), jnp.concatenate([nothing, dt], axis=1)], axis=0)
        delta = jnp.sum(dt.astype(F32) * ot[i], axis=0, keepdims=True)
        level = lse[i]
        limit = limits(i)

        def step(kc, acc):
            piece = chunk_of(kv, kc)[...].reshape(KEYS, 128)
            both = mm(piece, stacked)
            st = jnp.where(key_iota < limit - kc * KEYS, both[:, : 2 * ROWS], NEG)
            p = jnp.exp(st - level)
            ds = (p * (both[:, 2 * ROWS :] - delta)).astype(BF16)
            pair = jnp.concatenate([ds, p.astype(BF16)], axis=1)
            spot = chunk_of(dkv, kc)
            spot[...] += mm(pair, stacked, 1, 1).reshape(spot.shape)
            return acc + mm(kvt[kc, 0:64, :], ds)

        acc = lax.fori_loop(0, (i + 1) * per, step, jnp.zeros((HEAD_DIM, 2 * ROWS), F32))
        low_dq = (acc.astype(BF16).astype(F32) * (HEAD_DIM ** -0.5)).astype(BF16)
        dq_send[2 * i] = low_dq[:, :ROWS]
        dq_send[2 * i + 1] = low_dq[:, ROWS:]

    dq_in = {k: send(dq_send.at[head_idx[k]], dq_recv.at[h], head_dev[k]) for k in range(1, HEADS)}
    dq_recv[h] = dq_send[h]
    dkv_sib = {}
    for k in range(1, G):
        @pl.loop(0, HEADS)
        def _(j, k=k):
            dkvs[k - 1, j] = dkv[j, sib_idx[k]].astype(BF16)

        dkv_sib[k] = send(dkvs.at[k - 1], dkvr.at[k - 1], sib_dev[k])
    for k in range(1, G):
        dkv_sib[k].wait_recv()

    @pl.loop(0, HEADS)
    def _(j):
        x = dkv[j, g]
        for k in range(1, G):
            x = x + dkvr[k - 1, j].astype(F32)
        dkv_red[j] = x.astype(BF16)

    dkv_in = {k: send(dkv_red.at[head_idx[k]], dkv_recv.at[h], head_dev[k]) for k in range(1, HEADS)}
    dkv_recv[h] = dkv_red[h]

    dq_cat = jnp.concatenate([dq_send[j] for j in range(HEADS)], axis=1)
    dkv_cat = jnp.concatenate([dkv_red[j].astype(F32).T.astype(BF16) for j in range(HEADS)], axis=1)
    heads_t = jnp.concatenate([dq_cat, dkv_cat], axis=0)
    gw = mm(heads_t, nall[...].reshape(HEADS * ROWS, D)).astype(BF16)
    for q in range(F):
        gp[q // Gm, q % Gm] = gw[:, 128 * q : 128 * (q + 1)]
    g_sib = {k: send(gp.at[:, sib_idx[k] % Gm], gr1.at[k - 1], sib_dev[k]) for k in range(1, G)}
    for p in parts:
        p.pump()
    vectors.pump()
    for k in range(1, G):
        g_sib[k].wait_recv()
    own = gp[:, g % Gm].astype(F32)
    for k in range(1, G):
        own = own + gr1[k - 1].astype(F32)
    gs[...] = own.astype(BF16)
    if plan.S == 2:
        g_seq = send(gs, gr2, plan.seq_peer(me))
        g_seq.wait_recv()
        gt[...] = (gs[...].astype(F32) + gr2[...].astype(F32)).astype(BF16)
    else:
        gt[...] = gs[...]
    g_in = {}
    for k in range(1, HEADS):
        there = (head_idx[k] * G + g) % F
        g_in[k] = send(gt.at[there // Gm], gr.at[h], head_dev[k])
    gr[h] = gt[fs // Gm]

    for k in range(1, HEADS):
        dq_in[k].wait_recv()
    for k in range(1, HEADS):
        dkv_in[k].wait_recv()
    cols = [[], []]
    for i in range(HEADS // 2):
        a = dkv_recv[2 * i].astype(F32)
        b = dkv_recv[2 * i + 1].astype(F32)
        cols[0].append(jnp.where(left, a, pltpu.roll(b, 64, 1)))
        cols[1].append(jnp.where(left, pltpu.roll(a, 64, 1), b))
    kv_cols = jnp.concatenate(cols[0] + cols[1], axis=1).astype(BF16)
    grad_normed = mm(kv_cols, wq[:, D:], 1, 1) + mm(dq_recv[...].reshape(D, ROWS), wq[:, :D], 0, 1)
    n_one, r_one = row_norm(tok[h].astype(F32))
    scatter_row(v1, 0, jnp.sum(grad_normed * n_one, axis=0, keepdims=True))
    scatter_row(v1, 1, jnp.sum(grad_normed, axis=0, keepdims=True))
    v1_sib = {k: send(v1, v1r.at[k - 1], sib_dev[k]) for k in range(1, G)}
    e1 = grad_normed * gain1
    out_dx[...] = mid[...] + r_one * (
        e1 - jnp.mean(e1, axis=1, keepdims=True) - n_one * jnp.mean(e1 * n_one, axis=1, keepdims=True))
    for k in range(1, G):
        v1_sib[k].wait_recv()
    acc1 = v1[...]
    for k in range(1, G):
        acc1 = acc1 + v1r[k - 1]
    v1s[...] = acc1
    if plan.S == 2:
        v1_seq = send(v1s, v1r2, plan.seq_peer(me))
        for p in parts:
            p.pump()
        vectors.pump()
        v1_seq.wait_recv()
        v1t[...] = v1s[...] + v1r2[...]
    else:
        v1t[...] = v1s[...]
    v1_in = {}
    for k in range(1, HEADS):
        there = (head_idx[k] * G + g) % F
        v1_in[k] = send(v1t.at[there], v1r3.at[h], head_dev[k])
    v1r3[h] = v1t[fs]
    while not all(p.done for p in parts):
        for p in parts:
            if not p.done:
                p.pump()
        vectors.pump()
    while vectors.t < len(vectors.steps):
        vectors.pump()
    out_v[...] = vacc[len(vectors.steps) - 1, fs]

    for k in range(1, HEADS):
        g_in[k].wait_recv()
    for i in range(HEADS // 2):
        for part_no in range(3):
            lo, hi = 64 * part_no, 64 * (part_no + 1)
            x = jnp.concatenate([gr[2 * i, lo:hi, :], gr[2 * i + 1, lo:hi, :]], axis=0)
            out_dq[:, D * part_no + 128 * i : D * part_no + 128 * (i + 1)] = x.astype(F32).T
    for k in range(1, HEADS):
        v1_in[k].wait_recv()
    out_v1[...] = jnp.sum(v1r3[...], axis=0)
    for copy in sent:
        copy.wait_send()


def layer(plan, lengths, smalls, tokens, cotangent, qkv_weight, out_weight, up_weight, down_weight):
    G, F, N = plan.G, plan.F, plan.N
    Gm = min(G, F)
    D = tokens.shape[1]
    FF = up_weight.shape[1]
    nv = 2 + (plan.S == 2) + len(plan.bits)
    shard = FF // F + 4 * 128 + 128
    anyw = pl.BlockSpec(memory_space=pl.ANY)
    vm = pl.BlockSpec(memory_space=pltpu.VMEM)
    V = pltpu.VMEM
    sib = max(G - 1, 1)
    nsem = 128 + 4 * G
    scratch = [
        V((F, 16, 128), F32),
        V((HEADS, ROWS, D), BF16),
        V((ROWS, D), BF16),
        V((D, 3 * D), BF16), V((D, D), BF16), V((D, FF), BF16), V((FF, D), BF16),
        V((HEADS, ROWS, 128), BF16), V((HEADS, HEAD_DIM, ROWS), BF16),
        V((HEADS, G, ROWS, 128), BF16),
        V((N * ROWS // KEYS, 128, KEYS), BF16),
        V((HEADS, HEAD_DIM, ROWS), BF16),
        V((HEADS, HEAD_DIM, ROWS), BF16), V((HEADS, HEAD_DIM, ROWS), BF16),
        V((HEADS // 2, HEAD_DIM, 2 * ROWS), F32), V((HEADS // 2, 1, 2 * ROWS), F32),
        V((HEADS, HEAD_DIM, ROWS), BF16), V((HEADS, HEAD_DIM, ROWS), BF16),
        V((HEADS, G, ROWS, 128), F32),
        V((sib, HEADS, ROWS, 128), BF16), V((sib, HEADS, ROWS, 128), BF16),
        V((HEADS, ROWS, 128), BF16), V((HEADS, ROWS, 128), BF16),
        V((HEADS, HEAD_DIM, ROWS), BF16), V((HEADS, HEAD_DIM, ROWS), BF16),
        V((HEADS, ROWS, D), BF16),
        V((F // Gm, Gm, 192, 128), BF16), V((sib, F // Gm, 192, 128), BF16),
        V((F // Gm, 192, 128), BF16), V((F // Gm, 192, 128), BF16), V((F // Gm, 192, 128), BF16),
        V((HEADS, 192, 128), BF16),
        V((F, 8, 128), F32), V((sib, F, 8, 128), F32), V((F, 8, 128), F32), V((F, 8, 128), F32),
        V((F, 8, 128), F32), V((HEADS, 8, 128), F32),
        V((F, 8, 128), F32), V((nv, F, 8, 128), F32), V((nv, F, 8, 128), F32),
        V((ROWS, D), F32),
        V((ROWS, FF), BF16), V((ROWS, FF), BF16),
        V((2, shard, D), BF16), V((2, shard, D), BF16), V((shard, D), BF16), V((shard, D), BF16),
        V((2 * shard, D), BF16), V((2 * shard, D), BF16),
        pltpu.SemaphoreType.DMA((8,)), pltpu.SemaphoreType.DMA((nsem,)), pltpu.SemaphoreType.DMA((nsem,)),
        V((2, 2, shard, D), BF16),
    ]
    S = jax.ShapeDtypeStruct
    return pl.pallas_call(
        partial(body, plan, N * ROWS),
        out_shape=(S((ROWS, D), BF16), S((ROWS, D), F32), S((ROWS, 3 * D), F32),
                   S((shard, D), BF16), S((8, 128), F32), S((8, 128), F32)),
        in_specs=[pl.BlockSpec(memory_space=pltpu.SMEM)] + [anyw] * 7,
        out_specs=(vm,) * 6,
        scratch_shapes=scratch,
        compiler_params=pltpu.CompilerParams(
            collective_id=0, has_side_effects=True, vmem_limit_bytes=60 << 20),
    )(lengths, smalls, tokens, cotangent, qkv_weight, out_weight, up_weight, down_weight)


def on_device(plan, tokens, lengths, ln1_gain, ln1_bias, qkv_weight, out_weight, ln2_gain, ln2_bias,
              up_weight, up_bias, down_weight, down_bias, cotangent):
    D = tokens.shape[1]
    F = plan.F
    smalls = jnp.concatenate(
        [ln1_gain, ln1_bias, ln2_gain, ln2_bias, up_bias, down_bias,
         jnp.zeros((16 * 128 - 5 * 128 - up_bias.shape[0],), BF16)]).astype(F32).reshape(16, 128)
    y, dx, dqkv, r, v, v1 = layer(
        plan, lengths, smalls, tokens, cotangent, qkv_weight, out_weight, up_weight, down_weight)
    r = r.astype(F32)
    down_grad = r[0:512]
    up_grad = r[512:1024].reshape(4, 128, 512).transpose(1, 0, 2).reshape(128, 2048)
    out_grad = r[1024:1152]
    stats = v[7]
    rms = jnp.sqrt(stats[:3] / (stats[3] * D))
    return (y, dx, v1[0], v1[1], dqkv, out_grad, v[0], v[1], up_grad, v[2:6].reshape(512), down_grad,
            v[6], rms)


def solution(mesh):
    plan = Plan(mesh.shape["seq"], mesh.shape["ctx"], mesh.shape["fsdp"])
    rows = P(("seq", "ctx", "fsdp"), None)
    f1, f2 = P("fsdp"), P("fsdp", None)
    return jax.shard_map(
        partial(on_device, plan),
        mesh=mesh,
        in_specs=(rows, P("seq"), f1, f1, f2, f2, f1, f1, f2, f1, f2, f1, rows),
        out_specs=(rows, rows, f1, f1, f2, f2, f1, f1, f2, f1, f2, f1, P()),
        check_vma=False,
    )
```

```python
from functools import partial
import itertools

import jax
import jax.numpy as jnp
from jax import lax
from jax.experimental import pallas as pl
from jax.experimental.pallas import tpu as pltpu
from jax.sharding import PartitionSpec as P

HEADS = 8
HEAD_DIM = 64
EPS = 1e-05
NEG = -1e30
F32 = jnp.float32
BF16 = jnp.bfloat16
MESH = pl.DeviceIdType.MESH
ROWS = 128
KEYS = 512

ERF_TOP = (
    0.00022905065861350646,
    0.0034082910107109506,
    0.050955695062380861,
    0.18520832239976145,
    1.128379143519084,
)
ERF_LOW = (
    -1.1791602954361697e-7,
    0.000023547966471313185,
    0.0010179625278914885,
    0.014070470171167667,
    0.11098505178285362,
    0.49746925110067538,
    1.0,
)


def mm(a, b, ca=1, cb=0):
    return lax.dot_general(a, b, (((ca,), (cb,)), ((), ())), preferred_element_type=F32)


def erf(x):
    x = jnp.clip(x, -3.832506856900711, 3.832506856900711)
    s = x * x
    top = jnp.full_like(s, ERF_TOP[0])
    for c in ERF_TOP[1:]:
        top = top * s + c
    low = jnp.full_like(s, ERF_LOW[0])
    for c in ERF_LOW[1:]:
        low = low * s + c
    return x * top / low


def row_norm(x):
    center = jnp.mean(x, axis=1, keepdims=True)
    shifted = x - center
    spread = jnp.mean(shifted * shifted, axis=1, keepdims=True)
    r = lax.rsqrt(spread + EPS)
    return shifted * r, r


class Plan:
    def __init__(self, seqs, ctx, fsdp):
        self.S, self.C, self.F = seqs, ctx, fsdp
        self.N = ctx * fsdp
        self.G = self.N // HEADS
        self.bits = []
        b = 1
        while b < ctx:
            self.bits.append(b)
            b *= 2

    def split(self, dev):
        s, c, f = dev
        p = c * self.F + f
        return p // self.G, p % self.G

    def at(self, s, p):
        return (s, p // self.F, p % self.F)

    def head_peer(self, dev, k):
        h, g = self.split(dev)
        return self.at(dev[0], ((h + k) % HEADS) * self.G + g)

    def flip_peer(self, dev):
        h, g = self.split(dev)
        return self.at(dev[0], (h + 1 - 2 * (h % 2)) * self.G + g)

    def sibling(self, dev, k):
        h, g = self.split(dev)
        return self.at(dev[0], h * self.G + (g + k) % self.G)

    def fsdp_low(self, dev):
        s, c, f = dev
        return (s, c, f + 1 - 2 * (f % 2))

    def fsdp_high(self, dev):
        s, c, f = dev
        return (s, c, (f + 2) % self.F)

    def seq_peer(self, dev):
        s, c, f = dev
        return ((s + 1) % self.S, c, f)

    def ctx_peer(self, dev, b):
        s, c, f = dev
        return (s, c + b - 2 * b * ((c // b) % 2), f)

    def greeted(self):
        base = [partial(self._head, k) for k in range(1, HEADS)]
        base += [partial(self._sib, k) for k in range(1, self.G)]
        base += [self.seq_peer]
        more = [self.fsdp_low, self.fsdp_high] + [partial(self._ctx, b) for b in self.bits]
        devs = list(itertools.product(range(self.S), range(self.C), range(self.F)))
        for extra in more:
            if not all(extra(d) in [p(d) for p in base] for d in devs):
                base.append(extra)
        return base

    def _head(self, k, dev):
        return self.head_peer(dev, k)

    def _sib(self, k, dev):
        return self.sibling(dev, k)

    def _ctx(self, b, dev):
        return self.ctx_peer(dev, b)


def body(plan, lens, g1_in, b1_in, g2_in, b2_in, ub_in, db_in, tok_in, cot_in, wq_in, wo_in, wu_in, wd_in,
         out_y, out_dx, out_dq, out_r, out_v, out_v1,
         raw, rawu, small, tok, wq, wo, wu, wd,
         msg_kv, msg_q, kv, kvt, qb, o_send, at2, ot, lse, do_send, do_recv,
         dkv, dkvs, dkvr, dkv_red, dkv_recv, dq_send, dq_recv, nall,
         gp, gr1, gs, gr2, gt, gr,
         v1, v1r, v1s, v1r2, v1t, v1r3, v0, vrecv, vacc,
         mid, slope, actb, xa, c2, n2, g2, gb2, sa, into, sums, lsem, ssem, rsem):
    G, F, N = plan.G, plan.F, plan.N
    Gm = min(G, F)
    seq, ctx, fs = (lax.axis_index(a) for a in ("seq", "ctx", "fsdp"))
    me = (seq, ctx, fs)
    h, g = plan.split(me)
    fl, fh = fs % 2, fs // 2
    D = tok.shape[2]
    FF = wu.shape[1]
    span = FF // F
    valid = lens[0]
    counter = itertools.count()
    locals_ = itertools.count()

    def local(src, dst):
        copy = pltpu.make_async_copy(src, dst, lsem.at[next(locals_)])
        copy.start()
        return copy

    l_raw = [local(x, raw.at[i]) for i, x in enumerate((g1_in, b1_in, g2_in, b2_in, db_in))]
    l_raw.append(local(ub_in, rawu))
    l_tok = local(tok_in, tok.at[h])
    greet = plan.greeted()
    bar = pltpu.get_barrier_semaphore()
    for peer in greet:
        pl.semaphore_signal(bar, inc=1, device_id=peer(me), device_id_type=MESH)
    for copy in l_raw:
        copy.wait()
    own = [raw[i].astype(F32) for i in range(4)] + [rawu[...].astype(F32), raw[4].astype(F32)]
    used = 5 + span // 128
    small[fs] = jnp.concatenate(own + [jnp.zeros((16 - used, 128), F32)], axis=0)
    pl.semaphore_wait(bar, len(greet))

    sent = []

    def send(src, dst, dev):
        n = next(counter)
        copy = pltpu.make_async_remote_copy(
            src_ref=src, dst_ref=dst, send_sem=ssem.at[n], recv_sem=rsem.at[n],
            device_id=dev, device_id_type=MESH)
        copy.start()
        sent.append(copy)
        return copy

    low, high = plan.fsdp_low(me), plan.fsdp_high(me)
    fhigh = (fs + 2) % F
    head_dev = {k: plan.head_peer(me, k) for k in range(1, HEADS)}
    head_idx = {k: (h + k) % HEADS for k in range(1, HEADS)}
    sib_dev = {k: plan.sibling(me, k) for k in range(1, G)}
    sib_idx = {k: (g + k) % G for k in range(1, G)}

    far = plan.seq_peer(me)
    sm_low = send(small.at[fs], small.at[fs], low)
    sm_high = send(small.at[fs], small.at[fs], high)
    shards = ((wq_in, wq, 128), (wo_in, wo, 128), (wu_in, wu, 128), (wd_in, wd, span))

    def rows_of(w, step, which, part=None):
        if part is None:
            return w.at[pl.ds(pl.multiple_of(which * step, step), step), :]
        return w.at[pl.ds(pl.multiple_of(which * step + part * (step // 2), step // 2), step // 2), :]

    w_high = [send(wq_in, rows_of(wq, 128, fs), high)]
    w_low = [send(wq_in, rows_of(wq, 128, fs), low)]
    tok_copies = [send(tok_in, tok.at[h], head_dev[k]) for k in (2, 4, 6)]
    for src, dst, step in shards[1:]:
        half = src.at[pl.ds(pl.multiple_of(seq * (step // 2), step // 2), step // 2), :]
        w_high.append(send(half, rows_of(dst, step, fs, seq), high))
    for src, dst, step in shards[1:]:
        w_low.append(send(src, rows_of(dst, step, fs), low))
    l_w = [local(src, rows_of(dst, step, fs)) for src, dst, step in shards]
    l_cot = local(cot_in, c2.at[0])
    crossed, passed = {}, {}

    def cross(q):
        w_high[q].wait_recv()
        _, dst, step = shards[q]
        piece = rows_of(dst, step, fhigh, seq)
        crossed[q] = send(piece, piece, far)

    def hand_on(q):
        crossed[q].wait_recv()
        _, dst, step = shards[q]
        piece = rows_of(dst, step, fhigh)
        passed[q] = send(piece, piece, low)

    sm_low.wait_recv()
    sm_high.wait_recv()
    sm_fwd = send(small.at[fhigh], small.at[fhigh], low)
    l_tok.wait()
    inputs = tok[h].astype(F32)
    n_one, r_one = row_norm(inputs)
    sm_fwd.wait_recv()

    def vec(first, many=1):
        return jnp.concatenate(
            [small[q, first + r : first + r + 1, :] for q in range(F) for r in range(many)], axis=1)

    gain1, bias1, gain2, bias2 = vec(0), vec(1), vec(2), vec(3)
    down_bias = vec(4 + span // 128)
    normed = (n_one * gain1 + bias1).astype(BF16)
    nall[h] = normed
    l_w[0].wait()
    w_low[0].wait_recv()
    base = pl.multiple_of(fh * 256, 256)
    other = pl.multiple_of((1 - fh) * 256, 256)
    part = mm(nall[h, :, pl.ds(base, 256)], wq[pl.ds(base, 256), :])
    w_high[0].wait_recv()
    f_q = send(rows_of(wq, 128, fhigh), rows_of(wq, 128, fhigh), low)
    f_q.wait_recv()
    proj = part + mm(nall[h, :, pl.ds(other, 256)], wq[pl.ds(other, 256), :])

    lane = lax.broadcasted_iota(jnp.int32, (ROWS, 128), 1)
    left = lane < 64
    for i in range(HEADS // 2):
        kb = proj[:, D + 128 * i : D + 128 * (i + 1)]
        vb = proj[:, 2 * D + 128 * i : 2 * D + 128 * (i + 1)]
        msg_kv[2 * i] = jnp.where(left, kb, pltpu.roll(vb, 64, 1)).astype(BF16)
        msg_kv[2 * i + 1] = jnp.where(left, pltpu.roll(kb, 64, 1), vb).astype(BF16)
        qt = (proj[:, 128 * i : 128 * (i + 1)] * (HEAD_DIM ** -0.5)).T.astype(BF16)
        msg_q[2 * i] = qt[:64]
        msg_q[2 * i + 1] = qt[64:]
    kv_in, q_in = {}, {}
    for k in range(1, HEADS):
        kv_in[k] = send(msg_kv.at[head_idx[k]], kv.at[h, g], head_dev[k])
    for k in range(1, HEADS):
        q_in[k] = send(msg_q.at[head_idx[k]], qb.at[h], head_dev[k])
    kv[h, g] = msg_kv[h]
    qb[h] = msg_q[h]
    cross(1)
    for k in range(1, HEADS):
        kv_in[k].wait_recv()
    kv_sib = {k: send(kv.at[:, g], kv.at[:, g], sib_dev[k]) for k in range(1, G)}
    cross(2)
    hand_on(1)
    for k in range(1, HEADS):
        q_in[k].wait_recv()
    for k in range(1, G):
        kv_sib[k].wait_recv()

    tiles = HEADS // 2
    per = 2 * G * ROWS // KEYS
    blocks = KEYS // ROWS

    def chunk_of(ref, kc):
        if G >= blocks:
            b0 = kc * blocks
            return ref.at[b0 // G, pl.ds(lax.rem(b0, G), blocks)]
        return ref.at[pl.ds(kc * (blocks // G), blocks // G)]

    def limits(i):
        col = lax.broadcasted_iota(jnp.int32, (1, 2 * ROWS), 1)
        pos = ((2 * i + col // ROWS) * G + g) * ROWS + col % ROWS
        return jnp.minimum(pos + 1, valid)

    key_iota = lax.broadcasted_iota(jnp.int32, (KEYS, 2 * ROWS), 0)
    nothing = jnp.zeros((HEAD_DIM, 2 * ROWS), BF16)

    @pl.loop(0, N * ROWS // KEYS)
    def _(kc):
        piece = chunk_of(kv, kc)[...].reshape(KEYS, 128)
        kvt[kc] = piece.astype(F32).T.astype(BF16)

    def attend(i):
        qt = jnp.concatenate([qb[2 * i], qb[2 * i + 1]], axis=1)
        stacked = jnp.concatenate([qt, nothing], axis=0)
        limit = limits(i)

        def step(kc, carry):
            m, l, acc = carry
            piece = chunk_of(kv, kc)[...].reshape(KEYS, 128)
            st = mm(piece, stacked)
            st = jnp.where(key_iota < limit - kc * KEYS, st, NEG)
            mn = jnp.maximum(m, jnp.max(st, axis=0, keepdims=True))
            e = jnp.exp(st - mn)
            al = jnp.exp(m - mn)
            l = l * al + jnp.sum(e, axis=0, keepdims=True)
            acc = acc * al + mm(kvt[kc, 64:128, :], e.astype(BF16))
            return mn, l, acc

        m, l, acc = lax.fori_loop(
            0, (i + 1) * per, step,
            (jnp.full((1, 2 * ROWS), NEG, F32), jnp.zeros((1, 2 * ROWS), F32),
             jnp.zeros((HEAD_DIM, 2 * ROWS), F32)))
        o = acc / l
        ot[i] = o
        lse[i] = m + jnp.log(l)
        o_send[2 * i] = o[:, :ROWS].astype(BF16)
        o_send[2 * i + 1] = o[:, ROWS:].astype(BF16)

    for i in range(tiles):
        attend(i)
        if i == 2:
            cross(3)
    o_in = {k: send(o_send.at[head_idx[k]], at2.at[0, h], head_dev[k]) for k in range(1, HEADS)}
    at2[0, h] = o_send[h]
    hand_on(2)
    parity = h % 2
    flip = plan.flip_peer(me)
    for copy in tok_copies:
        copy.wait_recv()
    l_cot.wait()
    sib_c = send(c2.at[0], c2.at[1], low)
    tok4 = tok.reshape(HEADS // 2, 2, ROWS, D)
    tok_flip = send(tok4.at[:, parity], tok4.at[:, parity], flip)
    for k in range(1, HEADS):
        o_in[k].wait_recv()
    sib_at = send(at2.at[0], at2.at[1], low)

    for q in range(1, 4):
        l_w[q].wait()
        w_low[q].wait_recv()
    passed[1].wait_recv()
    at_t = at2[0].reshape(D, ROWS)
    attention_out = mm(at_t, wo[...], 0, 0)
    middle = tok[h].astype(F32) + attention_out
    n_two, r_two = row_norm(middle)
    normed_two = (n_two * gain2 + bias2).astype(BF16)
    n2[0] = normed_two
    sib_n = send(n2.at[0], n2.at[1], low)
    passed[2].wait_recv()
    hand_on(3)
    for q in range(F):
        cols = slice(q * span, (q + 1) * span)
        bias = jnp.concatenate([small[q, 4 + r : 5 + r, :] for r in range(span // 128)], axis=1)
        raised = mm(normed_two, wu[:, cols]) + bias
        cdf = 0.5 * (1.0 + erf(raised * (0.5 ** 0.5)))
        pdf = jnp.exp(-0.5 * raised * raised) * 0.3989422804014327
        actb[q // 2, q % 2] = (raised * cdf).astype(BF16)
        slope[q] = cdf + raised * pdf
    sib_a = send(actb.at[:, 1 - fl], xa, low)
    passed[3].wait_recv()
    cots = c2[0]
    gnt = jnp.zeros((ROWS, D), F32)
    for q in range(F):
        cols = slice(q * span, (q + 1) * span)
        grad = (mm(cots, wd[cols, :], 1, 1) * slope[q]).astype(BF16)
        g2[0, :, cols] = grad
        gnt = gnt + mm(grad, wu[:, cols], 1, 1)
    sib_g = send(g2.at[0], g2.at[1], low)

    def scatter_row(ref, row, x):
        for q in range(F):
            ref[q, row : row + 1, :] = x[:, 128 * q : 128 * (q + 1)]

    grad_final = cots.astype(F32)
    e2 = gnt * gain2
    grad_middle = grad_final + r_two * (
        e2 - jnp.mean(e2, axis=1, keepdims=True) - n_two * jnp.mean(e2 * n_two, axis=1, keepdims=True))
    mid[...] = grad_middle
    gb = grad_middle.astype(BF16)
    gb2[0] = gb
    sib_b = send(gb2.at[0], gb2.at[1], low)
    ga = mm(wo[...], gb, 1, 1).astype(BF16)
    do_send[...] = ga.reshape(HEADS, HEAD_DIM, ROWS)
    do_in = {k: send(do_send.at[head_idx[k]], do_recv.at[h], head_dev[k]) for k in range(1, HEADS)}
    do_recv[h] = do_send[h]

    sib_c.wait_recv()
    sib_a.wait_recv()
    both_c = c2[...].reshape(2 * ROWS, D)
    for y in range(2):
        a = jnp.concatenate([actb[y, fl], xa[y]], axis=0)
        sa[y, 0:span, :] = mm(a, both_c, 0, 0).astype(BF16)
    sib_n.wait_recv()
    sib_g.wait_recv()
    for y in range(2):
        spot = pl.ds(pl.multiple_of((2 * y + fl) * 128, 128), 128)
        a = n2[:, :, spot].reshape(2 * ROWS, 128)
        for q in range(F):
            cols = slice(q * span, (q + 1) * span)
            sa[y, span + 128 * q : span + 128 * (q + 1), :] = mm(
                a, g2[:, :, cols].reshape(2 * ROWS, span), 0, 0).astype(BF16)
    sib_at.wait_recv()
    sib_b.wait_recv()
    for y in range(2):
        x = jnp.zeros((128, D), F32)
        for p in range(2):
            rows = at2[p, pl.ds(pl.multiple_of((2 * y + fl) * 2, 2), 2)].reshape(128, ROWS)
            x = x + mm(rows, gb2[p])
        sa[y, span + 512 : span + 640, :] = x.astype(BF16)

    feed_out = down_bias
    for q in range(F):
        cols = slice(q * span, (q + 1) * span)
        feed_out = feed_out + mm(actb[q // 2, q % 2], wd[cols, :])
        grad = g2[0, :, cols].astype(F32)
        v0[q, 2 : 2 + span // 128, :] = jnp.concatenate(
            [jnp.sum(grad[:, 128 * r : 128 * (r + 1)], axis=0, keepdims=True)
             for r in range(span // 128)], axis=0)
    final = middle + feed_out
    out_y[...] = final.astype(BF16)
    scatter_row(v0, 0, jnp.sum(gnt * n_two, axis=0, keepdims=True))
    scatter_row(v0, 1, jnp.sum(gnt, axis=0, keepdims=True))
    scatter_row(v0, 2 + span // 128, jnp.sum(grad_final, axis=0, keepdims=True))
    place = (ctx * F + fs) * ROWS
    row = lax.broadcasted_iota(jnp.int32, (ROWS, 1), 0) + place
    live = (row < valid).astype(F32)

    def total(x):
        return jnp.sum(jnp.sum(x, axis=1, keepdims=True) * live, axis=0, keepdims=True)

    lane1 = lax.broadcasted_iota(jnp.int32, (1, 128), 1)
    stats = jnp.where(lane1 == 0, total(final * final), 0.0)
    stats = jnp.where(lane1 == 1, total(attention_out * attention_out), stats)
    stats = jnp.where(lane1 == 2, total(feed_out * feed_out), stats)
    stats = jnp.where(lane1 == 3, jnp.sum(live, axis=0, keepdims=True), stats)
    for q in range(F):
        v0[q, 3 + span // 128 : 4 + span // 128, :] = stats

    def add_rows(dst, a, b, rows):
        block = 32 if rows % 32 == 0 else 16

        @pl.loop(0, rows // block)
        def _(t):
            at = pl.ds(pl.multiple_of(t * block, block), block)
            dst[at, :] = (a[at, :].astype(F32) + b[at, :].astype(F32)).astype(BF16)

    pool = {"into": 0, "sums": 0}

    def take(name, rows):
        first = pool[name]
        pool[name] += rows
        ref = {"into": into, "sums": sums}[name]
        return ref.at[pl.ds(first, rows), :]

    class Part:
        def __init__(self, first, rows, y_first):
            self.rows, self.off, self.n = rows, first, rows
            self.pair = sa.at[:, pl.ds(first, rows), :]
            self.piece = None
            x = ("halve", far, seq)
            y = ("pick", high, fh)
            self.steps = [y, x] if y_first else [x, y]
            self.steps += [("halve", plan.ctx_peer(me, b), (ctx // b) % 2) for b in plan.bits]
            self.trail = []
            self.t = -1
            self.done = False

        def pump(self):
            if self.done:
                return
            if self.t >= 0:
                self.copy.wait_recv()
                if self.t < len(self.steps):
                    self.finish()
                else:
                    self.off, self.n = self.region
            self.t += 1
            if self.t < len(self.steps):
                self.begin()
            elif self.trail:
                dev, off, n = self.trail.pop()
                region = out_r.at[pl.ds(pl.multiple_of(self.off, 16), self.n), :]
                self.copy = send(region, region, dev)
                self.region = off, n
            else:
                self.done = True

        def part_of(self, ref, bit, half):
            return ref.at[pl.ds(pl.multiple_of(bit * half, 16), half), :]

        def begin(self):
            kind, dev, bit = self.steps[self.t]
            n = self.n
            self.size = n // 2 if kind == "halve" and n % 32 == 0 else n
            other = 1 - bit
            if self.piece is None and kind == "halve":
                self.got = take("into", 2 * self.size).reshape(2, self.size, D)
                src = self.pair.at[:, pl.ds(pl.multiple_of(other * self.size, 16), self.size), :]
            else:
                self.got = take("into", self.size)
                if kind == "pick":
                    src = self.pair.at[other]
                elif self.size < n:
                    src = self.part_of(self.piece, other, self.size)
                else:
                    src = self.piece
            self.copy = send(src, self.got, dev)

        def finish(self):
            kind, dev, bit = self.steps[self.t]
            n, size = self.n, self.size
            last = self.t + 1 == len(self.steps)
            if size < n:
                self.trail.append((dev, self.off, n))
                self.off = self.off + bit * size
            if self.piece is None and kind == "halve":
                dst = take("sums", 2 * size).reshape(2, size, D)
                for y in range(2):
                    add_rows(dst.at[y], self.part_of(self.pair.at[y], bit, size), self.got.at[y], size)
                self.pair = dst
            else:
                if last:
                    dst = out_r.at[pl.ds(pl.multiple_of(self.off, 16), size), :]
                else:
                    dst = take("sums", size)
                if kind == "pick":
                    mine = self.pair.at[bit]
                elif size < n:
                    mine = self.part_of(self.piece, bit, size)
                else:
                    mine = self.piece
                add_rows(dst, mine, self.got, size)
                self.piece = dst
            self.n = size

    parts = [Part(0, span // 2, True), Part(span // 2, span // 2, True),
             Part(span, 256, False), Part(span + 256, 384, False)]

    class Vectors:
        def __init__(self):
            self.steps = [low, high] + ([plan.seq_peer(me)] if plan.S > 1 else [])
            self.steps += [plan.ctx_peer(me, b) for b in plan.bits]
            self.t = 0
            self.copy = send(v0, vrecv.at[0], self.steps[0])

        def pump(self):
            if self.t == len(self.steps):
                return
            t = self.t
            self.copy.wait_recv()
            src = v0[...] if t == 0 else vacc[t - 1]
            vacc[t] = src + vrecv[t]
            self.t += 1
            if self.t < len(self.steps):
                self.copy = send(vacc.at[t], vrecv.at[self.t], self.steps[self.t])

    vectors = Vectors()
    for p in parts:
        p.pump()

    tok_flip.wait_recv()

    @pl.loop(0, HEADS)
    def _(j):
        n, _ = row_norm(tok[j].astype(F32))
        nall[j] = (n * gain1 + bias1).astype(BF16)

    for k in range(1, HEADS):
        do_in[k].wait_recv()
    vectors.pump()

    dkv[...] = jnp.zeros_like(dkv)

    def attend_back(i):
        qt = jnp.concatenate([qb[2 * i], qb[2 * i + 1]], axis=1)
        dt = jnp.concatenate([do_recv[2 * i], do_recv[2 * i + 1]], axis=1)
        stacked = jnp.concatenate(
            [jnp.concatenate([qt, nothing], axis=1), jnp.concatenate([nothing, dt], axis=1)], axis=0)
        delta = jnp.sum(dt.astype(F32) * ot[i], axis=0, keepdims=True)
        level = lse[i]
        limit = limits(i)

        def step(kc, acc):
            piece = chunk_of(kv, kc)[...].reshape(KEYS, 128)
            both = mm(piece, stacked)
            st = jnp.where(key_iota < limit - kc * KEYS, both[:, : 2 * ROWS], NEG)
            p = jnp.exp(st - level)
            ds = (p * (both[:, 2 * ROWS :] - delta)).astype(BF16)
            pair = jnp.concatenate([ds, p.astype(BF16)], axis=1)
            spot = chunk_of(dkv, kc)
            spot[...] += mm(pair, stacked, 1, 1).reshape(spot.shape)
            return acc + mm(kvt[kc, 0:64, :], ds)

        acc = lax.fori_loop(0, (i + 1) * per, step, jnp.zeros((HEAD_DIM, 2 * ROWS), F32))
        low_dq = (acc.astype(BF16).astype(F32) * (HEAD_DIM ** -0.5)).astype(BF16)
        dq_send[2 * i] = low_dq[:, :ROWS]
        dq_send[2 * i + 1] = low_dq[:, ROWS:]

    for i in reversed(range(tiles)):
        attend_back(i)
        if i == 1:
            parts[0].pump()
            parts[2].pump()
            vectors.pump()
    dq_in = {k: send(dq_send.at[head_idx[k]], dq_recv.at[h], head_dev[k]) for k in range(1, HEADS)}
    dq_recv[h] = dq_send[h]
    dkv_sib = {}
    for k in range(1, G):
        @pl.loop(0, HEADS)
        def _(j, k=k):
            dkvs[k - 1, j] = dkv[j, sib_idx[k]].astype(BF16)

        dkv_sib[k] = send(dkvs.at[k - 1], dkvr.at[k - 1], sib_dev[k])
    parts[1].pump()
    parts[3].pump()
    vectors.pump()
    for k in range(1, G):
        dkv_sib[k].wait_recv()

    @pl.loop(0, HEADS)
    def _(j):
        x = dkv[j, g]
        for k in range(1, G):
            x = x + dkvr[k - 1, j].astype(F32)
        dkv_red[j] = x.astype(BF16)

    dkv_in = {k: send(dkv_red.at[head_idx[k]], dkv_recv.at[h], head_dev[k]) for k in range(1, HEADS)}
    dkv_recv[h] = dkv_red[h]

    dq_cat = jnp.concatenate([dq_send[j] for j in range(HEADS)], axis=1)
    dkv_cat = jnp.concatenate([dkv_red[j].astype(F32).T.astype(BF16) for j in range(HEADS)], axis=1)
    heads_t = jnp.concatenate([dq_cat, dkv_cat], axis=0)
    gw = mm(heads_t, nall[...].reshape(HEADS * ROWS, D)).astype(BF16)
    for q in range(F):
        gp[q // Gm, q % Gm] = gw[:, 128 * q : 128 * (q + 1)]
    g_sib = {k: send(gp.at[:, sib_idx[k] % Gm], gr1.at[k - 1], sib_dev[k]) for k in range(1, G)}
    for p in parts:
        p.pump()
    vectors.pump()
    for k in range(1, G):
        g_sib[k].wait_recv()
    own = gp[:, g % Gm].astype(F32)
    for k in range(1, G):
        own = own + gr1[k - 1].astype(F32)
    gs[...] = own.astype(BF16)
    if plan.S > 1:
        g_seq = send(gs, gr2, plan.seq_peer(me))
        g_seq.wait_recv()
        gt[...] = (gs[...].astype(F32) + gr2[...].astype(F32)).astype(BF16)
    else:
        gt[...] = gs[...]
    g_in = {}
    for k in range(1, HEADS):
        there = (head_idx[k] * G + g) % F
        g_in[k] = send(gt.at[there // Gm], gr.at[h], head_dev[k])
    gr[h] = gt[fs // Gm]

    for k in range(1, HEADS):
        dq_in[k].wait_recv()
    for k in range(1, HEADS):
        dkv_in[k].wait_recv()
    cols = [[], []]
    for i in range(HEADS // 2):
        a = dkv_recv[2 * i].astype(F32)
        b = dkv_recv[2 * i + 1].astype(F32)
        cols[0].append(jnp.where(left, a, pltpu.roll(b, 64, 1)))
        cols[1].append(jnp.where(left, pltpu.roll(a, 64, 1), b))
    kv_cols = jnp.concatenate(cols[0] + cols[1], axis=1).astype(BF16)
    grad_normed = mm(kv_cols, wq[:, D:], 1, 1) + mm(dq_recv[...].reshape(D, ROWS), wq[:, :D], 0, 1)
    n_one, r_one = row_norm(tok[h].astype(F32))
    scatter_row(v1, 0, jnp.sum(grad_normed * n_one, axis=0, keepdims=True))
    scatter_row(v1, 1, jnp.sum(grad_normed, axis=0, keepdims=True))
    v1_sib = {k: send(v1, v1r.at[k - 1], sib_dev[k]) for k in range(1, G)}
    e1 = grad_normed * gain1
    out_dx[...] = mid[...] + r_one * (
        e1 - jnp.mean(e1, axis=1, keepdims=True) - n_one * jnp.mean(e1 * n_one, axis=1, keepdims=True))
    for k in range(1, G):
        v1_sib[k].wait_recv()
    acc1 = v1[...]
    for k in range(1, G):
        acc1 = acc1 + v1r[k - 1]
    v1s[...] = acc1
    if plan.S > 1:
        v1_seq = send(v1s, v1r2, plan.seq_peer(me))
        for p in parts:
            p.pump()
        vectors.pump()
        v1_seq.wait_recv()
        v1t[...] = v1s[...] + v1r2[...]
    else:
        v1t[...] = v1s[...]
    v1_in = {}
    for k in range(1, HEADS):
        there = (head_idx[k] * G + g) % F
        v1_in[k] = send(v1t.at[there], v1r3.at[h], head_dev[k])
    v1r3[h] = v1t[fs]
    while not all(p.done for p in parts):
        for p in parts:
            p.pump()
        vectors.pump()
    while vectors.t < len(vectors.steps):
        vectors.pump()
    out_v[...] = vacc[len(vectors.steps) - 1, fs]

    for k in range(1, HEADS):
        g_in[k].wait_recv()
    for i in range(HEADS // 2):
        for part_no in range(3):
            lo, hi = 64 * part_no, 64 * (part_no + 1)
            x = jnp.concatenate([gr[2 * i, lo:hi, :], gr[2 * i + 1, lo:hi, :]], axis=0)
            out_dq[:, D * part_no + 128 * i : D * part_no + 128 * (i + 1)] = x.astype(F32).T
    for k in range(1, HEADS):
        v1_in[k].wait_recv()
    out_v1[...] = jnp.sum(v1r3[...], axis=0)
    for copy in sent:
        copy.wait_send()


def layer(plan, lengths, vectors, tokens, cotangent, qkv_weight, out_weight, up_weight, down_weight):
    G, F, N = plan.G, plan.F, plan.N
    Gm = min(G, F)
    D = tokens.shape[1]
    FF = up_weight.shape[1]
    span = FF // F
    nv = 3 + len(plan.bits)
    shard = span + 4 * 128 + 128
    anyw = pl.BlockSpec(memory_space=pl.ANY)
    vm = pl.BlockSpec(memory_space=pltpu.VMEM)
    V = pltpu.VMEM
    sib = max(G - 1, 1)
    nsem = 128 + 4 * G
    heads = lambda: V((HEADS, HEAD_DIM, ROWS), BF16)
    scratch = [
        V((5, 1, 128), BF16), V((span // 128, 128), BF16), V((F, 16, 128), F32),
        V((HEADS, ROWS, D), BF16),
        V((D, 3 * D), BF16), V((D, D), BF16), V((D, FF), BF16), V((FF, D), BF16),
        V((HEADS, ROWS, 128), BF16), heads(),
        V((HEADS, G, ROWS, 128), BF16),
        V((N * ROWS // KEYS, 128, KEYS), BF16),
        heads(), heads(), V((2, HEADS, HEAD_DIM, ROWS), BF16),
        V((HEADS // 2, HEAD_DIM, 2 * ROWS), F32), V((HEADS // 2, 1, 2 * ROWS), F32),
        heads(), heads(),
        V((HEADS, G, ROWS, 128), F32),
        V((sib, HEADS, ROWS, 128), BF16), V((sib, HEADS, ROWS, 128), BF16),
        V((HEADS, ROWS, 128), BF16), V((HEADS, ROWS, 128), BF16),
        heads(), heads(),
        V((HEADS, ROWS, D), BF16),
        V((F // Gm, Gm, 192, 128), BF16), V((sib, F // Gm, 192, 128), BF16),
        V((F // Gm, 192, 128), BF16), V((F // Gm, 192, 128), BF16), V((F // Gm, 192, 128), BF16),
        V((HEADS, 192, 128), BF16),
        V((F, 8, 128), F32), V((sib, F, 8, 128), F32), V((F, 8, 128), F32), V((F, 8, 128), F32),
        V((F, 8, 128), F32), V((HEADS, 8, 128), F32),
        V((F, 8, 128), F32), V((nv, F, 8, 128), F32), V((nv, F, 8, 128), F32),
        V((ROWS, D), F32),
        V((F, ROWS, span), F32),
        V((2, 2, ROWS, span), BF16), V((2, ROWS, span), BF16),
        V((2, ROWS, D), BF16), V((2, ROWS, D), BF16), V((2, ROWS, FF), BF16), V((2, ROWS, D), BF16),
        V((2, shard, D), BF16),
        V((3 * shard, D), BF16), V((3 * shard, D), BF16),
        pltpu.SemaphoreType.DMA((16,)), pltpu.SemaphoreType.DMA((nsem,)), pltpu.SemaphoreType.DMA((nsem,)),
    ]
    S = jax.ShapeDtypeStruct
    return pl.pallas_call(
        partial(body, plan),
        out_shape=(S((ROWS, D), BF16), S((ROWS, D), F32), S((ROWS, 3 * D), F32),
                   S((shard, D), BF16), S((8, 128), F32), S((8, 128), F32)),
        in_specs=[pl.BlockSpec(memory_space=pltpu.SMEM)] + [anyw] * 12,
        out_specs=(vm,) * 6,
        scratch_shapes=scratch,
        compiler_params=pltpu.CompilerParams(
            collective_id=0, has_side_effects=True, vmem_limit_bytes=60 << 20),
    )(lengths, *vectors, tokens, cotangent, qkv_weight, out_weight, up_weight, down_weight)


def finish(y, dx, dq, r, v, v1, o_y, o_dx, o_g1, o_b1, o_dq, o_out, o_g2, o_b2, o_up, o_ub, o_down, o_db, o_rms):
    D = dx.shape[1]
    span = o_down.shape[0]
    n = span // 128
    o_y[...] = y[...]
    o_dx[...] = dx[...]
    o_dq[...] = dq[...]
    o_down[...] = r[0:span, :].astype(F32)
    for q in range(o_up.shape[1] // span):
        o_up[:, q * span : (q + 1) * span] = r[span + 128 * q : span + 128 * (q + 1), :].astype(F32)
    o_out[...] = r[span + 512 : span + 640, :].astype(F32)
    o_g1[...] = v1[0:1, :]
    o_b1[...] = v1[1:2, :]
    o_g2[...] = v[0:1, :]
    o_b2[...] = v[1:2, :]
    o_ub[...] = v[2 : 2 + n, :]
    o_db[...] = v[2 + n : 3 + n, :]
    stats = v[3 + n : 4 + n, :]
    o_rms[...] = jnp.sqrt(stats[:, 0:3] / (stats[:, 3:4] * D))


def on_device(plan, tokens, lengths, ln1_gain, ln1_bias, qkv_weight, out_weight, ln2_gain, ln2_bias,
              up_weight, up_bias, down_weight, down_bias, cotangent):
    D = tokens.shape[1]
    F = plan.F
    span = up_weight.shape[1] // F
    vectors = [x.reshape(-1, 128) for x in (ln1_gain, ln1_bias, ln2_gain, ln2_bias, up_bias, down_bias)]
    results = layer(
        plan, lengths, vectors, tokens, cotangent, qkv_weight, out_weight, up_weight, down_weight)
    S = jax.ShapeDtypeStruct
    vec = S((1, 128), F32)
    vm = pl.BlockSpec(memory_space=pltpu.VMEM)
    outs = pl.pallas_call(
        finish,
        out_shape=(S((ROWS, D), BF16), S((ROWS, D), F32), vec, vec, S((ROWS, 3 * D), F32), S((128, D), F32),
                   vec, vec, S((128, F * span), F32), S((span // 128, 128), F32), S((span, D), F32), vec,
                   S((1, 3), F32)),
        in_specs=[vm] * 6,
        out_specs=(vm,) * 13,
        compiler_params=pltpu.CompilerParams(vmem_limit_bytes=20 << 20),
    )(*results)
    outs = list(outs)
    for i in (2, 3, 6, 7, 9, 11, 12):
        outs[i] = outs[i].reshape(-1)
    return tuple(outs)


def solution(mesh):
    plan = Plan(mesh.shape["seq"], mesh.shape["ctx"], mesh.shape["fsdp"])
    rows = P(("seq", "ctx", "fsdp"), None)
    f1, f2 = P("fsdp"), P("fsdp", None)
    return jax.shard_map(
        partial(on_device, plan),
        mesh=mesh,
        in_specs=(rows, P("seq"), f1, f1, f2, f2, f1, f1, f2, f1, f2, f1, rows),
        out_specs=(rows, rows, f1, f1, f2, f2, f1, f1, f2, f1, f2, f1, P()),
        check_vma=False,
    )
```

```python
from functools import partial
import itertools

import jax
import jax.numpy as jnp
from jax import lax
from jax.experimental import pallas as pl
from jax.experimental.pallas import tpu as pltpu
from jax.sharding import PartitionSpec as P

HEADS = 8
HEAD_DIM = 64
EPS = 1e-05
NEG = -1e30
F32 = jnp.float32
BF16 = jnp.bfloat16
MESH = pl.DeviceIdType.MESH
ROWS = 128
KEYS = 512
KEYS_BACK = 512
PARTS = [(0, 256, False, False), (256, 256, False, False), (512, 128, False, False), (640, 256, False, False), (896, 128, False, False), (1024, 128, False, False)]
EVENTS = [0, 1, 2, 3, 4, 5, 6, 0, 6, 1, 0, 6, 2, 0, 1, 6, 3, 2, 1, 0, 4, 2, 3, 5, 4, 1, 6, 2, 3, 5, 4, 0, 5, 1, 2, 0, 3, 4, 5, 1, 2, 0, 3, 4, 5, 1, 3, 4, 2, 5, 3, 4, 5]
TICKS = [2, 3, 1, 0, 2, 1, 3, 1, 3, 0, 6, 10, 0, 6, 3, 0, 2, 1, 0, 0, 0]

ERF_TOP = (
    0.00022905065861350646,
    0.0034082910107109506,
    0.050955695062380861,
    0.18520832239976145,
    1.128379143519084,
)
ERF_LOW = (
    -1.1791602954361697e-7,
    0.000023547966471313185,
    0.0010179625278914885,
    0.014070470171167667,
    0.11098505178285362,
    0.49746925110067538,
    1.0,
)


def mm(a, b, ca=1, cb=0):
    return lax.dot_general(a, b, (((ca,), (cb,)), ((), ())), preferred_element_type=F32)


def erf(x):
    x = jnp.clip(x, -3.832506856900711, 3.832506856900711)
    s = x * x
    top = jnp.full_like(s, ERF_TOP[0])
    for c in ERF_TOP[1:]:
        top = top * s + c
    low = jnp.full_like(s, ERF_LOW[0])
    for c in ERF_LOW[1:]:
        low = low * s + c
    return x * top / low


def row_norm(x):
    center = jnp.mean(x, axis=1, keepdims=True)
    shifted = x - center
    spread = jnp.mean(shifted * shifted, axis=1, keepdims=True)
    r = lax.rsqrt(spread + EPS)
    return shifted * r, r


class Plan:
    def __init__(self, seqs, ctx, fsdp):
        self.S, self.C, self.F = seqs, ctx, fsdp
        self.N = ctx * fsdp
        self.G = self.N // HEADS
        self.bits = []
        b = 1
        while b < ctx:
            self.bits.append(b)
            b *= 2

    def split(self, dev):
        s, c, f = dev
        p = c * self.F + f
        return p // self.G, p % self.G

    def at(self, s, p):
        return (s, p // self.F, p % self.F)

    def head_peer(self, dev, k):
        h, g = self.split(dev)
        return self.at(dev[0], ((h + k) % HEADS) * self.G + g)

    def flip_peer(self, dev):
        h, g = self.split(dev)
        return self.at(dev[0], (h + 1 - 2 * (h % 2)) * self.G + g)

    def sibling(self, dev, k):
        h, g = self.split(dev)
        return self.at(dev[0], h * self.G + (g + k) % self.G)

    def fsdp_low(self, dev):
        s, c, f = dev
        return (s, c, f + 1 - 2 * (f % 2))

    def fsdp_high(self, dev):
        s, c, f = dev
        return (s, c, (f + 2) % self.F)

    def seq_peer(self, dev):
        s, c, f = dev
        return ((s + 1) % self.S, c, f)

    def ctx_peer(self, dev, b):
        s, c, f = dev
        return (s, c + b - 2 * b * ((c // b) % 2), f)

    def quad_peer(self, dev, b, k):
        s, c, f = dev
        return (s, (c // (4 * b)) * (4 * b) + ((c // b + k) % 4) * b + c % b, f)

    def greeted(self):
        base = [partial(self._head, k) for k in range(1, HEADS)]
        base += [partial(self._sib, k) for k in range(1, self.G)]
        base += [self.seq_peer]
        more = [self.fsdp_low, self.fsdp_high] + [partial(self._ctx, b) for b in self.bits]
        more += [partial(self._quad, b, k) for b in self.bits[:-1:2] for k in (1, 2, 3)]
        devs = list(itertools.product(range(self.S), range(self.C), range(self.F)))
        for extra in more:
            if not all(extra(d) in [p(d) for p in base] for d in devs):
                base.append(extra)
        return base

    def _head(self, k, dev):
        return self.head_peer(dev, k)

    def _sib(self, k, dev):
        return self.sibling(dev, k)

    def _quad(self, b, k, dev):
        return self.quad_peer(dev, b, k)

    def _ctx(self, b, dev):
        return self.ctx_peer(dev, b)


def body(plan, lens, g1_in, b1_in, g2_in, b2_in, ub_in, db_in, tok_in, cot_in, wq_in, wo_in, wu_in, wd_in,
         out_y, out_dx, out_dq, out_r, out_v, out_v1,
         raw, rawu, small, tok, wq, wo, wu, wd,
         msg, kvb, kvn, kvw, qb, o_send, at2, ot, lse, do_send, do_recv,
         dkv, dkvs, dkvr, dkv_red, dkv_recv, dq_send, dq_recv, nall,
         gp, gr1, gs, gr2, gt, gr,
         v1, v1r, v1s, v1r2, v1t, v1r3, v0, vrecv, vacc,
         mid, slope, actb, xa, c2, n2, g2, gb2, sa, into, sums, lsem, ssem, rsem):
    G, F, N = plan.G, plan.F, plan.N
    Gm = min(G, F)
    seq, ctx, fs = (lax.axis_index(a) for a in ("seq", "ctx", "fsdp"))
    me = (seq, ctx, fs)
    h, g = plan.split(me)
    fl, fh = fs % 2, fs // 2
    D = tok.shape[2]
    FF = wu.shape[1]
    span = FF // F
    valid = lens[0]
    counter = itertools.count()
    locals_ = itertools.count()

    def local(src, dst):
        copy = pltpu.make_async_copy(src, dst, lsem.at[next(locals_)])
        copy.start()
        return copy

    l_raw = [local(x, raw.at[i]) for i, x in enumerate((g1_in, b1_in, g2_in, b2_in, db_in))]
    l_raw.append(local(ub_in, rawu))
    l_tok = local(tok_in, tok.at[h])
    greet = plan.greeted()
    bar = pltpu.get_barrier_semaphore()
    for peer in greet:
        pl.semaphore_signal(bar, inc=1, device_id=peer(me), device_id_type=MESH)
    for copy in l_raw:
        copy.wait()
    own = [raw[i].astype(F32) for i in range(4)] + [rawu[...].astype(F32), raw[4].astype(F32)]
    used = 5 + span // 128
    small[fs] = jnp.concatenate(own + [jnp.zeros((16 - used, 128), F32)], axis=0)
    pl.semaphore_wait(bar, len(greet))

    sent = []

    def send(src, dst, dev):
        n = next(counter)
        copy = pltpu.make_async_remote_copy(
            src_ref=src, dst_ref=dst, send_sem=ssem.at[n], recv_sem=rsem.at[n],
            device_id=dev, device_id_type=MESH)
        copy.start()
        sent.append(copy)
        return copy

    posted = []

    def new_group():
        first = next(counter)
        for _ in range(HEADS - 1):
            next(counter)
        return first

    def post(group, to, src, dst):
        copy = pltpu.make_async_remote_copy(
            src_ref=src, dst_ref=dst, send_sem=ssem.at[group + to], recv_sem=rsem.at[group + h],
            device_id=plan.at(seq, to * G + g), device_id_type=MESH)

        @pl.when(h != to)
        def _():
            copy.start()

        posted.append((to, copy))

    def arrived(group, ref):
        for source in range(HEADS):
            copy = pltpu.make_async_remote_copy(
                src_ref=ref.at[source], dst_ref=ref.at[source], send_sem=ssem.at[group + source],
                recv_sem=rsem.at[group + source], device_id=plan.at(seq, source * G + g), device_id_type=MESH)

            @pl.when(h != source)
            def _():
                copy.wait_recv()

    low, high = plan.fsdp_low(me), plan.fsdp_high(me)
    fhigh = (fs + 2) % F
    head_dev = {k: plan.head_peer(me, k) for k in range(1, HEADS)}
    head_idx = {k: (h + k) % HEADS for k in range(1, HEADS)}
    sib_dev = {k: plan.sibling(me, k) for k in range(1, G)}
    sib_idx = {k: (g + k) % G for k in range(1, G)}

    far = plan.seq_peer(me)
    sm_low = send(small.at[fs], small.at[fs], low)
    sm_high = send(small.at[fs], small.at[fs], high)
    shards = ((wq_in, wq, 128), (wo_in, wo, 128), (wu_in, wu, 128), (wd_in, wd, span))

    def rows_of(w, first, count):
        return w.at[pl.ds(pl.multiple_of(first, count), count), :]

    def group_of(ref, which, c):
        return ref.at[pl.ds(pl.multiple_of(which * 128, 128), 128), c * D : (c + 1) * D]

    order = (1, 2, 0)
    q_high = {c: send(wq_in.at[:, c * D : (c + 1) * D], group_of(wq, fs, c), high) for c in order}
    q_low = {c: send(wq_in.at[:, c * D : (c + 1) * D], group_of(wq, fs, c), low) for c in order}
    half_rows = ROWS // 2

    def tokens_out(part):
        rows = slice(part * half_rows, (part + 1) * half_rows)
        return [send(tok_in.at[rows, :], tok.at[h, rows, :], head_dev[k]) for k in (2, 4, 6)]

    tok_copies = tokens_out(0)
    w_high, w_low = {}, {}
    for q in range(1, 4):
        src, dst, step = shards[q]
        w_low[q] = send(src, rows_of(dst, fs * step, step), low)
    l_w = [local(src, rows_of(dst, fs * step, step)) for src, dst, step in shards]
    l_cot = local(cot_in, c2.at[0])

    crossed, passed = {}, {}
    cuts = {1: 1, 2: 2, 3: 2}

    def slice_of(q, owner, p):
        count = shards[q][2] // (2 * cuts[q])
        first = (seq * cuts[q] + p) * count
        return count, first, owner * shards[q][2] + first

    def fetch(q):
        src, dst, step = shards[q]
        for p in range(cuts[q]):
            count, first, at = slice_of(q, fs, p)
            w_high[q, p] = send(rows_of(src, first, count), rows_of(dst, at, count), high)

    def cross(q, p):
        w_high[q, p].wait_recv()
        count, _, at = slice_of(q, fhigh, p)
        piece = rows_of(shards[q][1], at, count)
        crossed[q, p] = send(piece, piece, far)

    def hand_on(q):
        for p in range(cuts[q]):
            crossed[q, p].wait_recv()
        _, dst, step = shards[q]
        piece = rows_of(dst, fhigh * step, step)
        passed[q] = send(piece, piece, low)

    sm_low.wait_recv()
    sm_high.wait_recv()
    sm_fwd = send(small.at[fhigh], small.at[fhigh], low)
    l_tok.wait()
    inputs = tok[h].astype(F32)
    n_one, r_one = row_norm(inputs)
    sm_fwd.wait_recv()

    def vec(first, many=1):
        return jnp.concatenate(
            [small[q, first + r : first + r + 1, :] for q in range(F) for r in range(many)], axis=1)

    gain1, bias1, gain2, bias2 = vec(0), vec(1), vec(2), vec(3)
    down_bias = vec(4 + span // 128)
    normed = (n_one * gain1 + bias1).astype(BF16)
    nall[h] = normed
    l_w[0].wait()
    qkv_in = {}
    for c in order:
        q_low[c].wait_recv()
        q_high[c].wait_recv()
        piece = group_of(wq, fhigh, c)
        handed = send(piece, piece, low)
        handed.wait_recv()
        proj = mm(normed, wq[:, c * D : (c + 1) * D])
        if c == 0:
            proj = proj * (HEAD_DIM ** -0.5)
        msg[c] = proj.T.astype(BF16).reshape(HEADS, HEAD_DIM, ROWS)
        for k in range(1, HEADS):
            dst = qb.at[h] if c == 0 else kvb.at[h, g, (c - 1) * 64 : c * 64]
            qkv_in[c, k] = send(msg.at[c, head_idx[k]], dst, head_dev[k])
        if c == 0:
            qb[h] = msg[c, h]
        else:
            kvb[h, g, (c - 1) * 64 : c * 64] = msg[c, h]
    fetch(1)
    fetch(2)
    fetch(3)
    tok_copies += tokens_out(1)
    for c in (1, 2):
        for k in range(1, HEADS):
            qkv_in[c, k].wait_recv()
    kv_sib = {k: send(kvb.at[:, g], kvb.at[:, g], sib_dev[k]) for k in range(1, G)}

    def spread_block(hp, gg):
        at = pl.multiple_of((hp * G + gg) * ROWS, ROWS)
        block = kvb[hp, gg]
        kvw[:, pl.ds(at, ROWS)] = block
        kvn[pl.ds(at, ROWS), :] = block.astype(F32).T.astype(BF16)

    @pl.loop(0, HEADS)
    def _(hp):
        spread_block(hp, g)

    for k in range(1, G):
        kv_sib[k].wait_recv()
    for k in range(1, G):
        @pl.loop(0, HEADS)
        def _(hp, k=k):
            spread_block(hp, sib_idx[k])
    cross(1, 0)
    for k in range(1, HEADS):
        qkv_in[0, k].wait_recv()

    tiles = HEADS // 2

    def span_of(i, most):
        keys = (i + 1) * 2 * G * ROWS
        count = 1
        while keys % count or keys // count > most:
            count += 1
        return keys // count, count

    def over(count, step, start):
        return step(0, start) if count == 1 else lax.fori_loop(0, count, step, start)

    def keys_at(kc, size):
        return pl.ds(pl.multiple_of(kc * size, size), size) if not isinstance(kc, int) else slice(0, size)

    def key_iota(size):
        return lax.broadcasted_iota(jnp.int32, (size, 2 * ROWS), 0)

    def limits(i):
        col = lax.broadcasted_iota(jnp.int32, (1, 2 * ROWS), 1)
        pos = ((2 * i + col // ROWS) * G + g) * ROWS + col % ROWS
        return jnp.minimum(pos + 1, valid)

    nothing = jnp.zeros((HEAD_DIM, 2 * ROWS), BF16)

    def attend(i):
        qt = jnp.concatenate([qb[2 * i], qb[2 * i + 1]], axis=1)
        stacked = jnp.concatenate([qt, nothing], axis=0)
        limit = limits(i)

        size, count = span_of(i, KEYS)

        def step(kc, carry):
            at = keys_at(kc, size)
            st = mm(kvn[at, :], stacked)
            st = jnp.where(key_iota(size) < limit - kc * size, st, NEG)
            mn = jnp.max(st, axis=0, keepdims=True)
            if carry is not None:
                m, l, acc = carry
                mn = jnp.maximum(m, mn)
            e = jnp.exp(st - mn)
            total_e = jnp.sum(e, axis=0, keepdims=True)
            out = mm(kvw[64:128, at], e.astype(BF16))
            if carry is not None:
                al = jnp.exp(m - mn)
                total_e, out = l * al + total_e, acc * al + out
            return mn, total_e, out

        first = None if count == 1 else (
            jnp.full((1, 2 * ROWS), NEG, F32), jnp.zeros((1, 2 * ROWS), F32),
            jnp.zeros((HEAD_DIM, 2 * ROWS), F32))
        m, l, acc = over(count, step, first)
        o = acc / l
        ot[i] = o
        lse[i] = m + jnp.log(l)
        for p in range(2):
            o_send[2 * i + p] = o[:, p * ROWS : (p + 1) * ROWS].astype(BF16)
            post(o_group, 2 * i + p, o_send.at[2 * i + p], at2.at[0, h])

    o_group = new_group()
    for i in range(tiles):
        attend(i)
        if i == 1:
            cross(2, 0)
        if i == 2:
            cross(2, 1)
            hand_on(1)
    at2[0, h] = o_send[h]
    cross(3, 0)
    parity = h % 2
    flip = plan.flip_peer(me)
    for copy in tok_copies:
        copy.wait_recv()
    l_cot.wait()
    sib_c = send(c2.at[0], c2.at[1], low)
    tok4 = tok.reshape(HEADS // 2, 2, ROWS, D)
    tok_flip = send(tok4.at[:, parity], tok4.at[:, parity], flip)
    hand_on(2)
    cross(3, 1)
    arrived(o_group, at2.at[0])
    sib_at = send(at2.at[0], at2.at[1], low)

    def add_rows(dst, refs, rows):
        block = 32 if rows % 32 == 0 else 16

        @pl.loop(0, rows // block)
        def _(t):
            at = pl.ds(pl.multiple_of(t * block, block), block)
            x = refs[0][at, :].astype(F32)
            for ref in refs[1:]:
                x = x + ref[at, :].astype(F32)
            dst[at, :] = x.astype(BF16)

    pool = {"into": 0, "sums": 0}

    def take(name, rows):
        first = pool[name]
        pool[name] += rows
        ref = {"into": into, "sums": sums}[name]
        return ref.at[pl.ds(first, rows), :]

    class Part:
        def __init__(self, first, rows, y_first, quads):
            self.off, self.n = first, rows
            self.pair = sa.at[:, pl.ds(first, rows), :]
            self.piece = None
            x = ("cut", [far], 2, seq)
            y = ("pick", [high], 2, fh)
            self.steps = [y, x] if y_first else [x, y]
            n, bits = rows // 2, list(plan.bits)
            while bits:
                b = bits[0]
                if quads and len(bits) > 1 and n % 64 == 0:
                    peers = [plan.quad_peer(me, b, k) for k in (1, 2, 3)]
                    self.steps.append(("cut", peers, 4, (ctx // b) % 4))
                    bits, n = bits[2:], n // 4
                else:
                    kind = "cut" if n % 32 == 0 else "whole"
                    self.steps.append((kind, [plan.ctx_peer(me, b)], 2, (ctx // b) % 2))
                    bits, n = bits[1:], n // 2 if kind == "cut" else n
            self.trail = []
            self.t = -1
            self.done = False

        def pump(self):
            if self.done:
                return
            if self.t >= 0:
                for copy in self.copies:
                    copy.wait_recv()
                if self.t < len(self.steps):
                    self.finish()
                else:
                    self.off, self.n = self.region
            self.t += 1
            if self.t < len(self.steps):
                self.begin()
            elif self.trail:
                peers, off, n = self.trail.pop()
                region = out_r.at[pl.ds(pl.multiple_of(self.off, 16), self.n), :]
                self.copies = [send(region, region, dev) for dev in peers]
                self.region = off, n
            else:
                self.done = True

        def slot(self, ref, which, size):
            return ref.at[pl.ds(pl.multiple_of(which * size, 16), size), :]

        def begin(self):
            kind, peers, ways, mine = self.steps[self.t]
            self.size = self.n // ways if kind == "cut" else self.n
            self.got, self.copies = [], []
            for k, dev in enumerate(peers):
                there = (mine + k + 1) % ways
                if self.piece is None and kind == "cut":
                    got = take("into", 2 * self.size).reshape(2, self.size, D)
                    src = self.pair.at[:, pl.ds(pl.multiple_of(there * self.size, 16), self.size), :]
                else:
                    got = take("into", self.size)
                    if kind == "pick":
                        src = self.pair.at[there]
                    elif kind == "cut":
                        src = self.slot(self.piece, there, self.size)
                    else:
                        src = self.piece
                self.got.append(got)
                self.copies.append(send(src, got, dev))

        def finish(self):
            kind, peers, ways, mine = self.steps[self.t]
            size = self.size
            if kind == "cut":
                self.trail.append((peers, self.off, self.n))
                self.off = self.off + mine * size
            if self.piece is None and kind == "cut":
                dst = take("sums", 2 * size).reshape(2, size, D)
                for y in range(2):
                    add_rows(dst.at[y], [self.slot(self.pair.at[y], mine, size)] + [got.at[y] for got in self.got], size)
                self.pair = dst
            else:
                if self.t + 1 == len(self.steps):
                    dst = out_r.at[pl.ds(pl.multiple_of(self.off, 16), size), :]
                else:
                    dst = take("sums", size)
                if kind == "pick":
                    own = self.pair.at[mine]
                elif kind == "cut":
                    own = self.slot(self.piece, mine, size)
                else:
                    own = self.piece
                add_rows(dst, [own] + self.got, size)
                self.piece = dst
            self.n = size

    class Vectors:
        def __init__(self):
            self.steps = [([p], 2, None) for p in (low, high)]
            bits = list(plan.bits)
            while bits:
                b = bits[0]
                if len(bits) > 1:
                    self.steps.append(([plan.quad_peer(me, b, k) for k in (1, 2, 3)], 4, (ctx // b) % 4))
                    bits = bits[2:]
                else:
                    self.steps.append(([plan.ctx_peer(me, b)], 2, None))
                    bits = bits[1:]
            self.steps.append(([far], 2, None))
            self.t = -1
            self.done = False

        def begin(self, src):
            peers, ways, mine = self.steps[self.t]
            if ways == 2:
                self.copies = [send(src, vrecv.at[self.t, 0], peers[0])]
            else:
                vrecv[self.t, mine] = src[...]
                self.copies = [send(src, vrecv.at[self.t, mine], dev) for dev in peers]

        def pump(self):
            if self.done:
                return
            t = self.t
            if t < 0:
                self.t = 0
                self.begin(v0)
                return
            for copy in self.copies:
                copy.wait_recv()
            if self.steps[t][1] == 2:
                vacc[t] = (v0[...] if t == 0 else vacc[t - 1]) + vrecv[t, 0]
            else:
                vacc[t] = (vrecv[t, 0] + vrecv[t, 1]) + (vrecv[t, 2] + vrecv[t, 3])
            self.t += 1
            if self.t < len(self.steps):
                self.begin(vacc.at[t])
            else:
                self.done = True

    events, parts = [], []

    turns = iter(TICKS)

    def step_parts(count):
        for _ in range(min(count, len(events))):
            parts[events.pop(0)].pump()

    def tick():
        step_parts(next(turns))

    for q in range(1, 4):
        l_w[q].wait()
        w_low[q].wait_recv()
    passed[1].wait_recv()
    at_t = at2[0].reshape(D, ROWS)
    attention_out = mm(at_t, wo[...], 0, 0)
    middle = tok[h].astype(F32) + attention_out
    n_two, r_two = row_norm(middle)
    normed_two = (n_two * gain2 + bias2).astype(BF16)
    n2[0] = normed_two
    sib_n = send(n2.at[0], n2.at[1], low)
    passed[2].wait_recv()
    for q in range(F):
        cols = slice(q * span, (q + 1) * span)
        bias = jnp.concatenate([small[q, 4 + r : 5 + r, :] for r in range(span // 128)], axis=1)
        raised = mm(normed_two, wu[:, cols]) + bias
        cdf = 0.5 * (1.0 + erf(raised * (0.5 ** 0.5)))
        pdf = jnp.exp(-0.5 * raised * raised) * 0.3989422804014327
        actb[q // 2, q % 2] = (raised * cdf).astype(BF16)
        slope[q] = cdf + raised * pdf
    sib_a = send(actb.at[:, 1 - fl], xa, low)
    cots = c2[0]
    gnt = jnp.zeros((ROWS, D), F32)

    def back_block(step, gnt):
        q = (2 * fh + step) % F
        cols = pl.ds(pl.multiple_of(q * span, span), span)
        grad = (mm(cots, wd[cols, :], 1, 1) * slope[q]).astype(BF16)
        g2[0, :, cols] = grad
        return gnt + mm(grad, wu[:, cols], 1, 1)

    def share_blocks(y):
        cols = pl.ds(pl.multiple_of(y * 2 * span, 2 * span), 2 * span)
        return send(g2.at[0, :, cols], g2.at[1, :, cols], low)

    for step in range(F // 2):
        gnt = back_block(step, gnt)
    sib_g = [share_blocks(fh)]
    hand_on(3)
    sib_c.wait_recv()
    sib_a.wait_recv()
    both_c = c2[...].reshape(2 * ROWS, D)
    for y in range(2):
        a = jnp.concatenate([actb[y, fl], xa[y]], axis=0)
        sa[y, 0:span, :] = mm(a, both_c, 0, 0).astype(BF16)
    parts += [Part(*p) for p in PARTS]
    events += EVENTS
    tick()
    passed[3].wait_recv()
    for step in range(F // 2, F):
        gnt = back_block(step, gnt)
    sib_g.append(share_blocks(1 - fh))

    def scatter_row(ref, row, x):
        for q in range(F):
            ref[q, row : row + 1, :] = x[:, 128 * q : 128 * (q + 1)]

    grad_final = cots.astype(F32)
    e2 = gnt * gain2
    grad_middle = grad_final + r_two * (
        e2 - jnp.mean(e2, axis=1, keepdims=True) - n_two * jnp.mean(e2 * n_two, axis=1, keepdims=True))
    mid[...] = grad_middle
    gb = grad_middle.astype(BF16)
    gb2[0] = gb
    sib_b = send(gb2.at[0], gb2.at[1], low)
    ga = mm(wo[...], gb, 1, 1).astype(BF16)
    do_send[...] = ga.reshape(HEADS, HEAD_DIM, ROWS)
    do_in = {k: send(do_send.at[head_idx[k]], do_recv.at[h], head_dev[k]) for k in range(1, HEADS)}
    do_recv[h] = do_send[h]

    sib_n.wait_recv()
    for copy in sib_g:
        copy.wait_recv()
    for y in range(2):
        spot = pl.ds(pl.multiple_of((2 * y + fl) * 128, 128), 128)
        a = n2[:, :, spot].reshape(2 * ROWS, 128)
        for q in range(F):
            cols = slice(q * span, (q + 1) * span)
            sa[y, span + 128 * q : span + 128 * (q + 1), :] = mm(
                a, g2[:, :, cols].reshape(2 * ROWS, span), 0, 0).astype(BF16)
    tick()
    sib_at.wait_recv()
    sib_b.wait_recv()
    for y in range(2):
        x = jnp.zeros((128, D), F32)
        for p in range(2):
            rows = at2[p, pl.ds(pl.multiple_of((2 * y + fl) * 2, 2), 2)].reshape(128, ROWS)
            x = x + mm(rows, gb2[p])
        sa[y, span + 512 : span + 640, :] = x.astype(BF16)

    tick()

    feed_out = down_bias
    for q in range(F):
        cols = slice(q * span, (q + 1) * span)
        feed_out = feed_out + mm(actb[q // 2, q % 2], wd[cols, :])
        grad = g2[0, :, cols].astype(F32)
        v0[q, 2 : 2 + span // 128, :] = jnp.concatenate(
            [jnp.sum(grad[:, 128 * r : 128 * (r + 1)], axis=0, keepdims=True)
             for r in range(span // 128)], axis=0)
    final = middle + feed_out
    out_y[...] = final.astype(BF16)
    scatter_row(v0, 0, jnp.sum(gnt * n_two, axis=0, keepdims=True))
    scatter_row(v0, 1, jnp.sum(gnt, axis=0, keepdims=True))
    scatter_row(v0, 2 + span // 128, jnp.sum(grad_final, axis=0, keepdims=True))
    place = (ctx * F + fs) * ROWS
    row = lax.broadcasted_iota(jnp.int32, (ROWS, 1), 0) + place
    live = (row < valid).astype(F32)

    def total(x):
        return jnp.sum(jnp.sum(x, axis=1, keepdims=True) * live, axis=0, keepdims=True)

    lane1 = lax.broadcasted_iota(jnp.int32, (1, 128), 1)
    stats = jnp.where(lane1 == 0, total(final * final), 0.0)
    stats = jnp.where(lane1 == 1, total(attention_out * attention_out), stats)
    stats = jnp.where(lane1 == 2, total(feed_out * feed_out), stats)
    stats = jnp.where(lane1 == 3, jnp.sum(live, axis=0, keepdims=True), stats)
    for q in range(F):
        v0[q, 3 + span // 128 : 4 + span // 128, :] = stats

    parts.append(Vectors())
    tick()
    for k in range(1, HEADS):
        do_in[k].wait_recv()
    tick()

    dq_group, dkv_group = new_group(), new_group()
    dkv_sib = {}

    def attend_back(i):
        qt = jnp.concatenate([qb[2 * i], qb[2 * i + 1]], axis=1)
        dt = jnp.concatenate([do_recv[2 * i], do_recv[2 * i + 1]], axis=1)
        stacked = jnp.concatenate(
            [jnp.concatenate([qt, nothing], axis=1), jnp.concatenate([nothing, dt], axis=1)], axis=0)
        delta = jnp.sum(dt.astype(F32) * ot[i], axis=0, keepdims=True)
        level = lse[i]
        limit = limits(i)

        size, count = span_of(i, KEYS_BACK)

        def step(kc, acc):
            at = keys_at(kc, size)
            both = mm(kvn[at, :], stacked)
            st = jnp.where(key_iota(size) < limit - kc * size, both[:, : 2 * ROWS], NEG)
            p = jnp.exp(st - level)
            ds = (p * (both[:, 2 * ROWS :] - delta)).astype(BF16)
            pair = jnp.concatenate([ds, p.astype(BF16)], axis=1)
            more = mm(pair, stacked, 1, 1)
            if i == tiles - 1:
                dkv[at, :] = more
            else:
                dkv[at, :] += more
            out = mm(kvw[0:64, at], ds)
            return out if acc is None else acc + out

        acc = over(count, step, None if count == 1 else jnp.zeros((HEAD_DIM, 2 * ROWS), F32))
        low_dq = (acc.astype(BF16).astype(F32) * (HEAD_DIM ** -0.5)).astype(BF16)
        for p in range(2):
            j = 2 * i + p
            dq_send[j] = low_dq[:, p * ROWS : (p + 1) * ROWS]
            post(dq_group, j, dq_send.at[j], dq_recv.at[h])
            for k in range(1, G):
                spot = pl.multiple_of((j * G + sib_idx[k]) * ROWS, ROWS)
                dkvs[k - 1, j] = dkv[pl.ds(spot, ROWS), :].astype(BF16)
        for k in range(1, G):
            pairs = slice(2 * i, 2 * i + 2)
            dkv_sib[i, k] = send(dkvs.at[k - 1, pairs], dkvr.at[k - 1, pairs], sib_dev[k])

    def give_back(i):
        for k in range(1, G):
            dkv_sib[i, k].wait_recv()
        for j in (2 * i, 2 * i + 1):
            x = dkv[pl.ds(pl.multiple_of((j * G + g) * ROWS, ROWS), ROWS), :]
            for k in range(1, G):
                x = x + dkvr[k - 1, j].astype(F32)
            dkv_red[j] = x.astype(BF16)
            post(dkv_group, j, dkv_red.at[j], dkv_recv.at[h])

    for i in reversed(range(tiles)):
        attend_back(i)
        if i < tiles - 1:
            give_back(i + 1)
        tick()
    give_back(0)
    dq_recv[h] = dq_send[h]
    dkv_recv[h] = dkv_red[h]
    tick()

    tok_flip.wait_recv()

    @pl.loop(0, HEADS)
    def _(j):
        n, _ = row_norm(tok[j].astype(F32))
        nall[j] = (n * gain1 + bias1).astype(BF16)

    dq_cat = jnp.concatenate([dq_send[j] for j in range(HEADS)], axis=1)
    dkv_cat = jnp.concatenate([dkv_red[j].astype(F32).T.astype(BF16) for j in range(HEADS)], axis=1)
    heads_t = jnp.concatenate([dq_cat, dkv_cat], axis=0)
    gw = mm(heads_t, nall[...].reshape(HEADS * ROWS, D)).astype(BF16)
    for q in range(F):
        gp[q // Gm, q % Gm] = gw[:, 128 * q : 128 * (q + 1)]
    g_sib = {k: send(gp.at[:, sib_idx[k] % Gm], gr1.at[k - 1], sib_dev[k]) for k in range(1, G)}
    tick()
    for k in range(1, G):
        g_sib[k].wait_recv()
    own = gp[:, g % Gm].astype(F32)
    for k in range(1, G):
        own = own + gr1[k - 1].astype(F32)
    gs[...] = own.astype(BF16)
    if plan.S > 1:
        g_seq = send(gs, gr2, far)
    tick()

    arrived(dq_group, dq_recv)
    arrived(dkv_group, dkv_recv)
    tick()
    lane = lax.broadcasted_iota(jnp.int32, (ROWS, 128), 1)
    left = lane < 64
    cols = [[], []]
    for i in range(HEADS // 2):
        a = dkv_recv[2 * i].astype(F32)
        b = dkv_recv[2 * i + 1].astype(F32)
        cols[0].append(jnp.where(left, a, pltpu.roll(b, 64, 1)))
        cols[1].append(jnp.where(left, pltpu.roll(a, 64, 1), b))
    kv_cols = jnp.concatenate(cols[0] + cols[1], axis=1).astype(BF16)
    grad_normed = mm(kv_cols, wq[:, D:], 1, 1) + mm(dq_recv[...].reshape(D, ROWS), wq[:, :D], 0, 1)
    n_one, r_one = row_norm(tok[h].astype(F32))
    scatter_row(v1, 0, jnp.sum(grad_normed * n_one, axis=0, keepdims=True))
    scatter_row(v1, 1, jnp.sum(grad_normed, axis=0, keepdims=True))
    v1_sib = {k: send(v1, v1r.at[k - 1], sib_dev[k]) for k in range(1, G)}
    e1 = grad_normed * gain1
    out_dx[...] = mid[...] + r_one * (
        e1 - jnp.mean(e1, axis=1, keepdims=True) - n_one * jnp.mean(e1 * n_one, axis=1, keepdims=True))
    tick()
    for k in range(1, G):
        v1_sib[k].wait_recv()
    acc1 = v1[...]
    for k in range(1, G):
        acc1 = acc1 + v1r[k - 1]
    v1s[...] = acc1
    if plan.S > 1:
        v1_seq = send(v1s, v1r2, far)
    tick()
    if plan.S > 1:
        g_seq.wait_recv()
        gt[...] = (gs[...].astype(F32) + gr2[...].astype(F32)).astype(BF16)
    else:
        gt[...] = gs[...]
    gr[h] = gt[fs // Gm]
    g_in = {}
    for k in range(1, HEADS):
        there = (head_idx[k] * G + g) % F
        g_in[k] = send(gt.at[there // Gm], gr.at[h], head_dev[k])
        if k % 2 == 0:
            tick()
    if plan.S > 1:
        v1_seq.wait_recv()
        v1t[...] = v1s[...] + v1r2[...]
    else:
        v1t[...] = v1s[...]
    v1_in = {}
    for k in range(1, HEADS):
        there = (head_idx[k] * G + g) % F
        v1_in[k] = send(v1t.at[there], v1r3.at[h], head_dev[k])
    v1r3[h] = v1t[fs]
    step_parts(len(events))
    while not all(p.done for p in parts):
        for p in parts:
            p.pump()
    out_v[...] = vacc[len(parts[-1].steps) - 1, fs]

    for k in range(1, HEADS):
        g_in[k].wait_recv()
    for i in range(HEADS // 2):
        for part_no in range(3):
            lo, hi = 64 * part_no, 64 * (part_no + 1)
            x = jnp.concatenate([gr[2 * i, lo:hi, :], gr[2 * i + 1, lo:hi, :]], axis=0)
            out_dq[:, D * part_no + 128 * i : D * part_no + 128 * (i + 1)] = x.astype(F32).T
    for k in range(1, HEADS):
        v1_in[k].wait_recv()
    out_v1[...] = jnp.sum(v1r3[...], axis=0)
    for copy in sent:
        copy.wait_send()
    for to, copy in posted:
        @pl.when(h != to)
        def _(copy=copy):
            copy.wait_send()


def layer(plan, lengths, vectors, tokens, cotangent, qkv_weight, out_weight, up_weight, down_weight):
    G, F, N = plan.G, plan.F, plan.N
    Gm = min(G, F)
    D = tokens.shape[1]
    FF = up_weight.shape[1]
    span = FF // F
    nv = 3 + len(plan.bits)
    shard = span + 4 * 128 + 128
    anyw = pl.BlockSpec(memory_space=pl.ANY)
    vm = pl.BlockSpec(memory_space=pltpu.VMEM)
    V = pltpu.VMEM
    sib = max(G - 1, 1)
    nsem = 192 + 8 * G
    heads = lambda: V((HEADS, HEAD_DIM, ROWS), BF16)
    scratch = [
        V((5, 1, 128), BF16), V((span // 128, 128), BF16), V((F, 16, 128), F32),
        V((HEADS, ROWS, D), BF16),
        V((D, 3 * D), BF16), V((D, D), BF16), V((D, FF), BF16), V((FF, D), BF16),
        V((3, HEADS, HEAD_DIM, ROWS), BF16),
        V((HEADS, G, 128, ROWS), BF16),
        V((N * ROWS, 128), BF16), V((128, N * ROWS), BF16),
        heads(), heads(), V((2, HEADS, HEAD_DIM, ROWS), BF16),
        V((HEADS // 2, HEAD_DIM, 2 * ROWS), F32), V((HEADS // 2, 1, 2 * ROWS), F32),
        heads(), heads(),
        V((N * ROWS, 128), F32),
        V((sib, HEADS, ROWS, 128), BF16), V((sib, HEADS, ROWS, 128), BF16),
        V((HEADS, ROWS, 128), BF16), V((HEADS, ROWS, 128), BF16),
        heads(), heads(),
        V((HEADS, ROWS, D), BF16),
        V((F // Gm, Gm, 192, 128), BF16), V((sib, F // Gm, 192, 128), BF16),
        V((F // Gm, 192, 128), BF16), V((F // Gm, 192, 128), BF16), V((F // Gm, 192, 128), BF16),
        V((HEADS, 192, 128), BF16),
        V((F, 8, 128), F32), V((sib, F, 8, 128), F32), V((F, 8, 128), F32), V((F, 8, 128), F32),
        V((F, 8, 128), F32), V((HEADS, 8, 128), F32),
        V((F, 8, 128), F32), V((nv, 4, F, 8, 128), F32), V((nv, F, 8, 128), F32),
        V((ROWS, D), F32),
        V((F, ROWS, span), F32),
        V((2, 2, ROWS, span), BF16), V((2, ROWS, span), BF16),
        V((2, ROWS, D), BF16), V((2, ROWS, D), BF16), V((2, ROWS, FF), BF16), V((2, ROWS, D), BF16),
        V((2, shard, D), BF16),
        V((3 * shard, D), BF16), V((3 * shard, D), BF16),
        pltpu.SemaphoreType.DMA((16,)), pltpu.SemaphoreType.DMA((nsem,)), pltpu.SemaphoreType.DMA((nsem,)),
    ]
    S = jax.ShapeDtypeStruct
    return pl.pallas_call(
        partial(body, plan),
        out_shape=(S((ROWS, D), BF16), S((ROWS, D), F32), S((ROWS, 3 * D), F32),
                   S((shard, D), BF16), S((8, 128), F32), S((8, 128), F32)),
        in_specs=[pl.BlockSpec(memory_space=pltpu.SMEM)] + [anyw] * 12,
        out_specs=(vm,) * 6,
        scratch_shapes=scratch,
        compiler_params=pltpu.CompilerParams(
            collective_id=0, has_side_effects=True, vmem_limit_bytes=60 << 20),
    )(lengths, *vectors, tokens, cotangent, qkv_weight, out_weight, up_weight, down_weight)


def finish(y, dx, dq, r, v, v1, o_y, o_dx, o_g1, o_b1, o_dq, o_out, o_g2, o_b2, o_up, o_ub, o_down, o_db, o_rms,
           rv, vv, vv1, down, up, out, qv, xv, yv, sem):
    D = dx.shape[1]
    span = o_down.shape[0]
    n = span // 128

    def go(i, src, dst):
        copy = pltpu.make_async_copy(src, dst, sem.at[i])
        copy.start()
        return copy

    l_r = go(0, r, rv)
    l_v, l_v1 = go(1, v, vv), go(2, v1, vv1)
    through = [go(3, dq, qv), go(4, dx, xv), go(5, y, yv)]
    outs = []
    l_v.wait()
    l_v1.wait()
    o_g1[...] = vv1[0:1, :]
    o_b1[...] = vv1[1:2, :]
    o_g2[...] = vv[0:1, :]
    o_b2[...] = vv[1:2, :]
    o_ub[...] = vv[2 : 2 + n, :]
    o_db[...] = vv[2 + n : 3 + n, :]
    stats = vv[3 + n : 4 + n, :]
    o_rms[...] = jnp.sqrt(stats[:, 0:3] / (stats[:, 3:4] * D))
    for i, (copy, src, dst) in enumerate(zip(through, (qv, xv, yv), (o_dq, o_dx, o_y))):
        copy.wait()
        outs.append(go(9 + i, src, dst))
    l_r.wait()
    down[...] = rv[0:span, :].astype(F32)
    outs.append(go(6, down, o_down))
    for q in range(o_up.shape[1] // span):
        up[:, q * span : (q + 1) * span] = rv[span + 128 * q : span + 128 * (q + 1), :].astype(F32)
    outs.append(go(7, up, o_up))
    out[...] = rv[span + 512 : span + 640, :].astype(F32)
    outs.append(go(8, out, o_out))
    for copy in outs:
        copy.wait()


def on_device(plan, tokens, lengths, ln1_gain, ln1_bias, qkv_weight, out_weight, ln2_gain, ln2_bias,
              up_weight, up_bias, down_weight, down_bias, cotangent):
    D = tokens.shape[1]
    F = plan.F
    span = up_weight.shape[1] // F
    vectors = [x.reshape(-1, 128) for x in (ln1_gain, ln1_bias, ln2_gain, ln2_bias, up_bias, down_bias)]
    results = layer(
        plan, lengths, vectors, tokens, cotangent, qkv_weight, out_weight, up_weight, down_weight)
    S = jax.ShapeDtypeStruct
    vec = S((1, 128), F32)
    vm = pl.BlockSpec(memory_space=pltpu.VMEM)
    hbm = pl.BlockSpec(memory_space=pl.ANY)
    outs = pl.pallas_call(
        finish,
        out_shape=(S((ROWS, D), BF16), S((ROWS, D), F32), vec, vec, S((ROWS, 3 * D), F32), S((128, D), F32),
                   vec, vec, S((128, F * span), F32), S((span // 128, 128), F32), S((span, D), F32), vec,
                   S((1, 3), F32)),
        in_specs=[hbm] * 6,
        out_specs=(hbm, hbm, vm, vm, hbm, hbm, vm, vm, hbm, vm, hbm, vm, vm),
        scratch_shapes=[
            pltpu.VMEM(results[3].shape, BF16), pltpu.VMEM((8, 128), F32), pltpu.VMEM((8, 128), F32),
            pltpu.VMEM((span, D), F32), pltpu.VMEM((128, F * span), F32), pltpu.VMEM((128, D), F32),
            pltpu.VMEM((128, 3 * D), F32), pltpu.VMEM((ROWS, D), F32), pltpu.VMEM((ROWS, D), BF16),
            pltpu.SemaphoreType.DMA((12,))],
        compiler_params=pltpu.CompilerParams(vmem_limit_bytes=60 << 20),
    )(*results)
    outs = list(outs)
    for i in (2, 3, 6, 7, 9, 11, 12):
        outs[i] = outs[i].reshape(-1)
    return tuple(outs)


def solution(mesh):
    plan = Plan(mesh.shape["seq"], mesh.shape["ctx"], mesh.shape["fsdp"])
    rows = P(("seq", "ctx", "fsdp"), None)
    f1, f2 = P("fsdp"), P("fsdp", None)
    return jax.shard_map(
        partial(on_device, plan),
        mesh=mesh,
        in_specs=(rows, P("seq"), f1, f1, f2, f2, f1, f1, f2, f1, f2, f1, rows),
        out_specs=(rows, rows, f1, f1, f2, f2, f1, f1, f2, f1, f2, f1, P()),
        check_vma=False,
    )
```

```python
from functools import partial
import itertools

import jax
import jax.numpy as jnp
from jax import lax
from jax.experimental import pallas as pl
from jax.experimental.pallas import tpu as pltpu
from jax.sharding import PartitionSpec as P

HEADS = 8
HEAD_DIM = 64
EPS = 1e-05
NEG = -1e30
F32 = jnp.float32
BF16 = jnp.bfloat16
MESH = pl.DeviceIdType.MESH
ROWS = 128
KEYS = 512
KEYS_BACK = 512
PARTS = [(0, 256, False, False), (256, 128, False, False), (384, 128, False, False), (512, 256, False, False), (768, 128, False, False), (896, 128, False, False), (1024, 128, True, True)]
EVENTS = [0, 1, 2, 3, 4, 5, 6, 7, 0, 7, 1, 6, 2, 0, 7, 1, 0, 3, 2, 1, 7, 4, 2, 5, 3, 0, 1, 6, 4, 2, 5, 7, 3, 0, 1, 4, 5, 6, 2, 0, 3, 1, 4, 5, 2, 6, 0, 3, 4, 1, 5, 2, 6, 3, 4, 5, 3, 4, 5]
TICKS = [3, 3, 1, 0, 2, 3, 0, 2, 1, 1, 1, 3, 8, 11, 6, 0, 0, 6, 0, 0, 0]

ERF_TOP = (
    0.00022905065861350646,
    0.0034082910107109506,
    0.050955695062380861,
    0.18520832239976145,
    1.128379143519084,
)
ERF_LOW = (
    -1.1791602954361697e-7,
    0.000023547966471313185,
    0.0010179625278914885,
    0.014070470171167667,
    0.11098505178285362,
    0.49746925110067538,
    1.0,
)


def mm(a, b, ca=1, cb=0):
    return lax.dot_general(a, b, (((ca,), (cb,)), ((), ())), preferred_element_type=F32)


def erf(x):
    x = jnp.clip(x, -3.832506856900711, 3.832506856900711)
    s = x * x
    top = jnp.full_like(s, ERF_TOP[0])
    for c in ERF_TOP[1:]:
        top = top * s + c
    low = jnp.full_like(s, ERF_LOW[0])
    for c in ERF_LOW[1:]:
        low = low * s + c
    return x * top / low


def row_norm(x):
    center = jnp.mean(x, axis=1, keepdims=True)
    shifted = x - center
    spread = jnp.mean(shifted * shifted, axis=1, keepdims=True)
    r = lax.rsqrt(spread + EPS)
    return shifted * r, r


class Plan:
    def __init__(self, seqs, ctx, fsdp):
        self.S, self.C, self.F = seqs, ctx, fsdp
        self.N = ctx * fsdp
        self.G = self.N // HEADS
        self.bits = []
        b = 1
        while b < ctx:
            self.bits.append(b)
            b *= 2

    def split(self, dev):
        s, c, f = dev
        p = c * self.F + f
        return p // self.G, p % self.G

    def at(self, s, p):
        return (s, p // self.F, p % self.F)

    def head_peer(self, dev, k):
        h, g = self.split(dev)
        return self.at(dev[0], ((h + k) % HEADS) * self.G + g)

    def flip_peer(self, dev):
        h, g = self.split(dev)
        return self.at(dev[0], (h + 1 - 2 * (h % 2)) * self.G + g)

    def sibling(self, dev, k):
        h, g = self.split(dev)
        return self.at(dev[0], h * self.G + (g + k) % self.G)

    def fsdp_low(self, dev):
        s, c, f = dev
        return (s, c, f + 1 - 2 * (f % 2))

    def fsdp_high(self, dev):
        s, c, f = dev
        return (s, c, (f + 2) % self.F)

    def seq_peer(self, dev):
        s, c, f = dev
        return ((s + 1) % self.S, c, f)

    def ctx_peer(self, dev, b):
        s, c, f = dev
        return (s, c + b - 2 * b * ((c // b) % 2), f)

    def quad_peer(self, dev, b, k):
        s, c, f = dev
        return (s, (c // (4 * b)) * (4 * b) + ((c // b + k) % 4) * b + c % b, f)

    def greeted(self):
        base = [partial(self._head, k) for k in range(1, HEADS)]
        base += [partial(self._sib, k) for k in range(1, self.G)]
        base += [self.seq_peer]
        more = [self.fsdp_low, self.fsdp_high] + [partial(self._ctx, b) for b in self.bits]
        more += [partial(self._quad, b, k) for b in self.bits[:-1:2] for k in (1, 2, 3)]
        devs = list(itertools.product(range(self.S), range(self.C), range(self.F)))
        for extra in more:
            if not all(extra(d) in [p(d) for p in base] for d in devs):
                base.append(extra)
        return base

    def _head(self, k, dev):
        return self.head_peer(dev, k)

    def _sib(self, k, dev):
        return self.sibling(dev, k)

    def _quad(self, b, k, dev):
        return self.quad_peer(dev, b, k)

    def _ctx(self, b, dev):
        return self.ctx_peer(dev, b)


def body(plan, lens, g1_in, b1_in, g2_in, b2_in, ub_in, db_in, tok_in, cot_in, wq_in, wo_in, wu_in, wd_in,
         out_y, out_dx, out_dq, out_r, out_v, out_v1,
         raw, rawu, small, tok, wq, wo, wu, wd,
         msg, kvb, kvn, kvw, qb, o_send, at2, ot, lse, do_send, do_recv,
         dkv, dkvs, dkvr, dkv_red, dkv_recv, dq_send, dq_recv, nall,
         gp, gr1, gs, gr2, gt, gr,
         v1, v1r, v1s, v1r2, v1t, v1r3, v0, vrecv, vacc,
         mid, slope, actb, xa, c2, n2, g2, gb2, sa, into, sums, lsem, ssem, rsem):
    G, F, N = plan.G, plan.F, plan.N
    Gm = min(G, F)
    seq, ctx, fs = (lax.axis_index(a) for a in ("seq", "ctx", "fsdp"))
    me = (seq, ctx, fs)
    h, g = plan.split(me)
    fl, fh = fs % 2, fs // 2
    D = tok.shape[2]
    FF = wu.shape[1]
    span = FF // F
    valid = lens[0]
    counter = itertools.count()
    locals_ = itertools.count()

    def local(src, dst):
        copy = pltpu.make_async_copy(src, dst, lsem.at[next(locals_)])
        copy.start()
        return copy

    l_raw = [local(x, raw.at[i]) for i, x in enumerate((g1_in, b1_in, g2_in, b2_in, db_in))]
    l_raw.append(local(ub_in, rawu))
    l_tok = local(tok_in, tok.at[h])
    greet = plan.greeted()
    bar = pltpu.get_barrier_semaphore()
    for peer in greet:
        pl.semaphore_signal(bar, inc=1, device_id=peer(me), device_id_type=MESH)
    for copy in l_raw:
        copy.wait()
    own = [raw[i].astype(F32) for i in range(4)] + [rawu[...].astype(F32), raw[4].astype(F32)]
    used = 5 + span // 128
    small[fs] = jnp.concatenate(own + [jnp.zeros((16 - used, 128), F32)], axis=0)
    pl.semaphore_wait(bar, len(greet))

    sent = []

    def send(src, dst, dev):
        n = next(counter)
        copy = pltpu.make_async_remote_copy(
            src_ref=src, dst_ref=dst, send_sem=ssem.at[n], recv_sem=rsem.at[n],
            device_id=dev, device_id_type=MESH)
        copy.start()
        sent.append(copy)
        return copy

    posted = []

    def new_group():
        first = next(counter)
        for _ in range(HEADS - 1):
            next(counter)
        return first

    def post(group, to, src, dst):
        copy = pltpu.make_async_remote_copy(
            src_ref=src, dst_ref=dst, send_sem=ssem.at[group + to], recv_sem=rsem.at[group + h],
            device_id=plan.at(seq, to * G + g), device_id_type=MESH)

        @pl.when(h != to)
        def _():
            copy.start()

        posted.append((to, copy))

    def arrived(group, ref):
        for source in range(HEADS):
            copy = pltpu.make_async_remote_copy(
                src_ref=ref.at[source], dst_ref=ref.at[source], send_sem=ssem.at[group + source],
                recv_sem=rsem.at[group + source], device_id=plan.at(seq, source * G + g), device_id_type=MESH)

            @pl.when(h != source)
            def _():
                copy.wait_recv()

    low, high = plan.fsdp_low(me), plan.fsdp_high(me)
    fhigh = (fs + 2) % F
    head_dev = {k: plan.head_peer(me, k) for k in range(1, HEADS)}
    head_idx = {k: (h + k) % HEADS for k in range(1, HEADS)}
    sib_dev = {k: plan.sibling(me, k) for k in range(1, G)}
    sib_idx = {k: (g + k) % G for k in range(1, G)}

    far = plan.seq_peer(me)
    sm_low = send(small.at[fs], small.at[fs], low)
    sm_high = send(small.at[fs], small.at[fs], high)
    shards = ((wq_in, wq, 128), (wo_in, wo, 128), (wu_in, wu, 128), (wd_in, wd, span))

    def rows_of(w, first, count):
        return w.at[pl.ds(pl.multiple_of(first, count), count), :]

    def group_of(ref, which, c):
        return ref.at[pl.ds(pl.multiple_of(which * 128, 128), 128), c * D : (c + 1) * D]

    order = (1, 2, 0)
    q_high = {c: send(wq_in.at[:, c * D : (c + 1) * D], group_of(wq, fs, c), high) for c in order}
    q_low = {c: send(wq_in.at[:, c * D : (c + 1) * D], group_of(wq, fs, c), low) for c in order}
    half_rows = ROWS // 2

    def tokens_out(part):
        rows = slice(part * half_rows, (part + 1) * half_rows)
        return [send(tok_in.at[rows, :], tok.at[h, rows, :], head_dev[k]) for k in (2, 4, 6)]

    tok_copies = tokens_out(0)
    w_high, w_low = {}, {}
    for q in range(1, 4):
        src, dst, step = shards[q]
        w_low[q] = send(src, rows_of(dst, fs * step, step), low)
    l_w = [local(src, rows_of(dst, fs * step, step)) for src, dst, step in shards]
    l_cot = local(cot_in, c2.at[0])

    crossed, passed = {}, {}
    cuts = {1: 1, 2: 2, 3: 2}

    def slice_of(q, owner, p):
        count = shards[q][2] // (2 * cuts[q])
        first = (seq * cuts[q] + p) * count
        return count, first, owner * shards[q][2] + first

    def fetch(q):
        src, dst, step = shards[q]
        for p in range(cuts[q]):
            count, first, at = slice_of(q, fs, p)
            w_high[q, p] = send(rows_of(src, first, count), rows_of(dst, at, count), high)

    def cross(q, p):
        w_high[q, p].wait_recv()
        count, _, at = slice_of(q, fhigh, p)
        piece = rows_of(shards[q][1], at, count)
        crossed[q, p] = send(piece, piece, far)

    def hand_on(q):
        for p in range(cuts[q]):
            crossed[q, p].wait_recv()
        _, dst, step = shards[q]
        piece = rows_of(dst, fhigh * step, step)
        passed[q] = send(piece, piece, low)

    sm_low.wait_recv()
    sm_high.wait_recv()
    sm_fwd = send(small.at[fhigh], small.at[fhigh], low)
    l_tok.wait()
    inputs = tok[h].astype(F32)
    n_one, r_one = row_norm(inputs)
    sm_fwd.wait_recv()

    def vec(first, many=1):
        return jnp.concatenate(
            [small[q, first + r : first + r + 1, :] for q in range(F) for r in range(many)], axis=1)

    gain1, bias1, gain2, bias2 = vec(0), vec(1), vec(2), vec(3)
    down_bias = vec(4 + span // 128)
    normed = (n_one * gain1 + bias1).astype(BF16)
    nall[h] = normed
    l_w[0].wait()
    qkv_in = {}
    for c in order:
        q_low[c].wait_recv()
        q_high[c].wait_recv()
        piece = group_of(wq, fhigh, c)
        handed = send(piece, piece, low)
        handed.wait_recv()
        proj = mm(normed, wq[:, c * D : (c + 1) * D])
        if c == 0:
            proj = proj * (HEAD_DIM ** -0.5)
        msg[c] = proj.T.astype(BF16).reshape(HEADS, HEAD_DIM, ROWS)
        for k in range(1, HEADS):
            dst = qb.at[h] if c == 0 else kvb.at[h, g, (c - 1) * 64 : c * 64]
            qkv_in[c, k] = send(msg.at[c, head_idx[k]], dst, head_dev[k])
        if c == 0:
            qb[h] = msg[c, h]
        else:
            kvb[h, g, (c - 1) * 64 : c * 64] = msg[c, h]
    fetch(1)
    fetch(2)
    fetch(3)
    tok_copies += tokens_out(1)
    for c in (1, 2):
        for k in range(1, HEADS):
            qkv_in[c, k].wait_recv()
    kv_sib = {k: send(kvb.at[:, g], kvb.at[:, g], sib_dev[k]) for k in range(1, G)}

    def spread_block(hp, gg):
        at = pl.multiple_of((hp * G + gg) * ROWS, ROWS)
        block = kvb[hp, gg]
        kvw[:, pl.ds(at, ROWS)] = block
        kvn[pl.ds(at, ROWS), :] = block.astype(F32).T.astype(BF16)

    @pl.loop(0, HEADS)
    def _(hp):
        spread_block(hp, g)

    for k in range(1, G):
        kv_sib[k].wait_recv()
    for k in range(1, G):
        @pl.loop(0, HEADS)
        def _(hp, k=k):
            spread_block(hp, sib_idx[k])
    cross(1, 0)
    for k in range(1, HEADS):
        qkv_in[0, k].wait_recv()

    tiles = HEADS // 2

    def span_of(i, most):
        keys = (i + 1) * 2 * G * ROWS
        count = 1
        while keys % count or keys // count > most:
            count += 1
        return keys // count, count

    def over(count, step, start):
        return step(0, start) if count == 1 else lax.fori_loop(0, count, step, start)

    def keys_at(kc, size):
        return pl.ds(pl.multiple_of(kc * size, size), size) if not isinstance(kc, int) else slice(0, size)

    def key_iota(size):
        return lax.broadcasted_iota(jnp.int32, (size, 2 * ROWS), 0)

    def limits(i):
        col = lax.broadcasted_iota(jnp.int32, (1, 2 * ROWS), 1)
        pos = ((2 * i + col // ROWS) * G + g) * ROWS + col % ROWS
        return jnp.minimum(pos + 1, valid)

    nothing = jnp.zeros((HEAD_DIM, 2 * ROWS), BF16)

    def attend(i):
        qt = jnp.concatenate([qb[2 * i], qb[2 * i + 1]], axis=1)
        stacked = jnp.concatenate([qt, nothing], axis=0)
        limit = limits(i)

        size, count = span_of(i, KEYS)

        def step(kc, carry):
            at = keys_at(kc, size)
            st = mm(kvn[at, :], stacked)
            st = jnp.where(key_iota(size) < limit - kc * size, st, NEG)
            mn = jnp.max(st, axis=0, keepdims=True)
            if carry is not None:
                m, l, acc = carry
                mn = jnp.maximum(m, mn)
            e = jnp.exp(st - mn)
            total_e = jnp.sum(e, axis=0, keepdims=True)
            out = mm(kvw[64:128, at], e.astype(BF16))
            if carry is not None:
                al = jnp.exp(m - mn)
                total_e, out = l * al + total_e, acc * al + out
            return mn, total_e, out

        first = None if count == 1 else (
            jnp.full((1, 2 * ROWS), NEG, F32), jnp.zeros((1, 2 * ROWS), F32),
            jnp.zeros((HEAD_DIM, 2 * ROWS), F32))
        m, l, acc = over(count, step, first)
        o = acc / l
        ot[i] = o
        lse[i] = m + jnp.log(l)
        for p in range(2):
            o_send[2 * i + p] = o[:, p * ROWS : (p + 1) * ROWS].astype(BF16)
            post(o_group, 2 * i + p, o_send.at[2 * i + p], at2.at[0, h])

    o_group = new_group()
    for i in range(tiles):
        attend(i)
        if i == 1:
            cross(2, 0)
        if i == 2:
            cross(2, 1)
            hand_on(1)
    at2[0, h] = o_send[h]
    cross(3, 0)
    parity = h % 2
    flip = plan.flip_peer(me)
    for copy in tok_copies:
        copy.wait_recv()
    l_cot.wait()
    sib_c = send(c2.at[0], c2.at[1], low)
    tok4 = tok.reshape(HEADS // 2, 2, ROWS, D)
    tok_flip = send(tok4.at[:, parity], tok4.at[:, parity], flip)
    hand_on(2)
    cross(3, 1)
    arrived(o_group, at2.at[0])
    sib_at = send(at2.at[0], at2.at[1], low)

    def add_rows(dst, refs, rows):
        block = max(b for b in (16, 32, 64) if rows % b == 0)

        @pl.loop(0, rows // block)
        def _(t):
            at = pl.ds(pl.multiple_of(t * block, block), block)
            if len(refs) == 2:
                dst[at, :] = refs[0][at, :] + refs[1][at, :]
            else:
                x = refs[0][at, :].astype(F32)
                for ref in refs[1:]:
                    x = x + ref[at, :].astype(F32)
                dst[at, :] = x.astype(BF16)

    pool = {"into": 0, "sums": 0}

    def take(name, rows):
        first = pool[name]
        pool[name] += rows
        ref = {"into": into, "sums": sums}[name]
        return ref.at[pl.ds(first, rows), :]

    class Part:
        def __init__(self, first, rows, y_first, quads):
            self.off, self.n = first, rows
            self.pair = sa.at[:, pl.ds(first, rows), :]
            self.piece = None
            x = ("cut", [far], 2, seq)
            y = ("pick", [high], 2, fh)
            self.steps = [y, x] if y_first else [x, y]
            n, bits = rows // 2, list(plan.bits)
            while bits:
                b = bits[0]
                if quads and len(bits) > 1 and n % 64 == 0:
                    peers = [plan.quad_peer(me, b, k) for k in (1, 2, 3)]
                    self.steps.append(("cut", peers, 4, (ctx // b) % 4))
                    bits, n = bits[2:], n // 4
                else:
                    kind = "cut" if n % 32 == 0 else "whole"
                    self.steps.append((kind, [plan.ctx_peer(me, b)], 2, (ctx // b) % 2))
                    bits, n = bits[1:], n // 2 if kind == "cut" else n
            self.trail = []
            self.t = -1
            self.done = False

        def pump(self):
            if self.done:
                return
            if self.t >= 0:
                for copy in self.copies:
                    copy.wait_recv()
                if self.t < len(self.steps):
                    self.finish()
                else:
                    self.off, self.n = self.region
            self.t += 1
            if self.t < len(self.steps):
                self.begin()
            elif self.trail:
                peers, off, n = self.trail.pop()
                region = out_r.at[pl.ds(pl.multiple_of(self.off, 16), self.n), :]
                self.copies = [send(region, region, dev) for dev in peers]
                self.region = off, n
            else:
                self.done = True

        def slot(self, ref, which, size):
            return ref.at[pl.ds(pl.multiple_of(which * size, 16), size), :]

        def begin(self):
            kind, peers, ways, mine = self.steps[self.t]
            self.size = self.n // ways if kind == "cut" else self.n
            self.got, self.copies = [], []
            for k, dev in enumerate(peers):
                there = (mine + k + 1) % ways
                if self.piece is None and kind == "cut":
                    got = take("into", 2 * self.size).reshape(2, self.size, D)
                    src = self.pair.at[:, pl.ds(pl.multiple_of(there * self.size, 16), self.size), :]
                else:
                    got = take("into", self.size)
                    if kind == "pick":
                        src = self.pair.at[there]
                    elif kind == "cut":
                        src = self.slot(self.piece, there, self.size)
                    else:
                        src = self.piece
                self.got.append(got)
                self.copies.append(send(src, got, dev))

        def finish(self):
            kind, peers, ways, mine = self.steps[self.t]
            size = self.size
            if kind == "cut":
                self.trail.append((peers, self.off, self.n))
                self.off = self.off + mine * size
            if self.piece is None and kind == "cut":
                dst = take("sums", 2 * size).reshape(2, size, D)
                for y in range(2):
                    add_rows(dst.at[y], [self.slot(self.pair.at[y], mine, size)] + [got.at[y] for got in self.got], size)
                self.pair = dst
            else:
                if self.t + 1 == len(self.steps):
                    dst = out_r.at[pl.ds(pl.multiple_of(self.off, 16), size), :]
                else:
                    dst = take("sums", size)
                if kind == "pick":
                    own = self.pair.at[mine]
                elif kind == "cut":
                    own = self.slot(self.piece, mine, size)
                else:
                    own = self.piece
                add_rows(dst, [own] + self.got, size)
                self.piece = dst
            self.n = size

    class Vectors:
        def __init__(self):
            self.steps = [([p], 2, None) for p in (low, high)]
            bits = list(plan.bits)
            while bits:
                b = bits[0]
                if len(bits) > 1:
                    self.steps.append(([plan.quad_peer(me, b, k) for k in (1, 2, 3)], 4, (ctx // b) % 4))
                    bits = bits[2:]
                else:
                    self.steps.append(([plan.ctx_peer(me, b)], 2, None))
                    bits = bits[1:]
            self.steps.append(([far], 2, None))
            self.t = -1
            self.done = False

        def begin(self, src):
            peers, ways, mine = self.steps[self.t]
            if ways == 2:
                self.copies = [send(src, vrecv.at[self.t, 0], peers[0])]
            else:
                vrecv[self.t, mine] = src[...]
                self.copies = [send(src, vrecv.at[self.t, mine], dev) for dev in peers]

        def pump(self):
            if self.done:
                return
            t = self.t
            if t < 0:
                self.t = 0
                self.begin(v0)
                return
            for copy in self.copies:
                copy.wait_recv()
            if self.steps[t][1] == 2:
                vacc[t] = (v0[...] if t == 0 else vacc[t - 1]) + vrecv[t, 0]
            else:
                vacc[t] = (vrecv[t, 0] + vrecv[t, 1]) + (vrecv[t, 2] + vrecv[t, 3])
            self.t += 1
            if self.t < len(self.steps):
                self.begin(vacc.at[t])
            else:
                self.done = True

    events, parts = [], []

    turns = iter(TICKS)

    def step_parts(count):
        for _ in range(min(count, len(events))):
            parts[events.pop(0)].pump()

    def tick():
        step_parts(next(turns))

    for q in range(1, 4):
        l_w[q].wait()
        w_low[q].wait_recv()
    passed[1].wait_recv()
    at_t = at2[0].reshape(D, ROWS)
    attention_out = mm(at_t, wo[...], 0, 0)
    middle = tok[h].astype(F32) + attention_out
    n_two, r_two = row_norm(middle)
    normed_two = (n_two * gain2 + bias2).astype(BF16)
    n2[0] = normed_two
    sib_n = send(n2.at[0], n2.at[1], low)
    passed[2].wait_recv()
    for q in range(F):
        cols = slice(q * span, (q + 1) * span)
        bias = jnp.concatenate([small[q, 4 + r : 5 + r, :] for r in range(span // 128)], axis=1)
        raised = mm(normed_two, wu[:, cols]) + bias
        cdf = 0.5 * (1.0 + erf(raised * (0.5 ** 0.5)))
        pdf = jnp.exp(-0.5 * raised * raised) * 0.3989422804014327
        actb[q // 2, q % 2] = (raised * cdf).astype(BF16)
        slope[q] = cdf + raised * pdf
    sib_a = send(actb.at[:, 1 - fl], xa, low)
    cots = c2[0]
    gnt = jnp.zeros((ROWS, D), F32)

    def back_block(step, gnt):
        q = (2 * fh + step) % F
        cols = pl.ds(pl.multiple_of(q * span, span), span)
        grad = (mm(cots, wd[cols, :], 1, 1) * slope[q]).astype(BF16)
        g2[0, :, cols] = grad
        return gnt + mm(grad, wu[:, cols], 1, 1)

    def share_blocks(y):
        cols = pl.ds(pl.multiple_of(y * 2 * span, 2 * span), 2 * span)
        return send(g2.at[0, :, cols], g2.at[1, :, cols], low)

    for step in range(F // 2):
        gnt = back_block(step, gnt)
    sib_g = [share_blocks(fh)]
    hand_on(3)
    sib_c.wait_recv()
    sib_a.wait_recv()
    both_c = c2[...].reshape(2 * ROWS, D)
    for y in range(2):
        a = jnp.concatenate([actb[y, fl], xa[y]], axis=0)
        sa[y, 0:span, :] = mm(a, both_c, 0, 0).astype(BF16)
    parts += [Part(*p) for p in PARTS]
    events += EVENTS
    tick()
    passed[3].wait_recv()
    for step in range(F // 2, F):
        gnt = back_block(step, gnt)
    sib_g.append(share_blocks(1 - fh))

    def scatter_row(ref, row, x):
        for q in range(F):
            ref[q, row : row + 1, :] = x[:, 128 * q : 128 * (q + 1)]

    grad_final = cots.astype(F32)
    e2 = gnt * gain2
    grad_middle = grad_final + r_two * (
        e2 - jnp.mean(e2, axis=1, keepdims=True) - n_two * jnp.mean(e2 * n_two, axis=1, keepdims=True))
    mid[...] = grad_middle
    gb = grad_middle.astype(BF16)
    gb2[0] = gb
    sib_b = send(gb2.at[0], gb2.at[1], low)
    ga = mm(wo[...], gb, 1, 1).astype(BF16)
    do_send[...] = ga.reshape(HEADS, HEAD_DIM, ROWS)
    do_in = {k: send(do_send.at[head_idx[k]], do_recv.at[h], head_dev[k]) for k in range(1, HEADS)}
    do_recv[h] = do_send[h]

    sib_n.wait_recv()
    for copy in sib_g:
        copy.wait_recv()
    for y in range(2):
        spot = pl.ds(pl.multiple_of((2 * y + fl) * 128, 128), 128)
        a = n2[:, :, spot].reshape(2 * ROWS, 128)
        for q in range(F):
            cols = slice(q * span, (q + 1) * span)
            sa[y, span + 128 * q : span + 128 * (q + 1), :] = mm(
                a, g2[:, :, cols].reshape(2 * ROWS, span), 0, 0).astype(BF16)
    tick()
    sib_at.wait_recv()
    sib_b.wait_recv()
    for y in range(2):
        x = jnp.zeros((128, D), F32)
        for p in range(2):
            rows = at2[p, pl.ds(pl.multiple_of((2 * y + fl) * 2, 2), 2)].reshape(128, ROWS)
            x = x + mm(rows, gb2[p])
        sa[y, span + 512 : span + 640, :] = x.astype(BF16)

    tick()

    feed_out = down_bias
    for q in range(F):
        cols = slice(q * span, (q + 1) * span)
        feed_out = feed_out + mm(actb[q // 2, q % 2], wd[cols, :])
        grad = g2[0, :, cols].astype(F32)
        v0[q, 2 : 2 + span // 128, :] = jnp.concatenate(
            [jnp.sum(grad[:, 128 * r : 128 * (r + 1)], axis=0, keepdims=True)
             for r in range(span // 128)], axis=0)
    final = middle + feed_out
    out_y[...] = final.astype(BF16)
    scatter_row(v0, 0, jnp.sum(gnt * n_two, axis=0, keepdims=True))
    scatter_row(v0, 1, jnp.sum(gnt, axis=0, keepdims=True))
    scatter_row(v0, 2 + span // 128, jnp.sum(grad_final, axis=0, keepdims=True))
    place = (ctx * F + fs) * ROWS
    row = lax.broadcasted_iota(jnp.int32, (ROWS, 1), 0) + place
    live = (row < valid).astype(F32)

    def total(x):
        return jnp.sum(jnp.sum(x, axis=1, keepdims=True) * live, axis=0, keepdims=True)

    lane1 = lax.broadcasted_iota(jnp.int32, (1, 128), 1)
    stats = jnp.where(lane1 == 0, total(final * final), 0.0)
    stats = jnp.where(lane1 == 1, total(attention_out * attention_out), stats)
    stats = jnp.where(lane1 == 2, total(feed_out * feed_out), stats)
    stats = jnp.where(lane1 == 3, jnp.sum(live, axis=0, keepdims=True), stats)
    for q in range(F):
        v0[q, 3 + span // 128 : 4 + span // 128, :] = stats

    parts.append(Vectors())
    tick()
    for k in range(1, HEADS):
        do_in[k].wait_recv()
    tick()

    dq_group, dkv_group = new_group(), new_group()
    dkv_sib = {}

    def attend_back(i):
        qt = jnp.concatenate([qb[2 * i], qb[2 * i + 1]], axis=1)
        dt = jnp.concatenate([do_recv[2 * i], do_recv[2 * i + 1]], axis=1)
        stacked = jnp.concatenate(
            [jnp.concatenate([qt, nothing], axis=1), jnp.concatenate([nothing, dt], axis=1)], axis=0)
        delta = jnp.sum(dt.astype(F32) * ot[i], axis=0, keepdims=True)
        level = lse[i]
        limit = limits(i)

        size, count = span_of(i, KEYS_BACK)

        def step(kc, acc):
            at = keys_at(kc, size)
            both = mm(kvn[at, :], stacked)
            st = jnp.where(key_iota(size) < limit - kc * size, both[:, : 2 * ROWS], NEG)
            p = jnp.exp(st - level)
            ds = (p * (both[:, 2 * ROWS :] - delta)).astype(BF16)
            pair = jnp.concatenate([ds, p.astype(BF16)], axis=1)
            more = mm(pair, stacked, 1, 1)
            if i == tiles - 1:
                dkv[at, :] = more
            else:
                dkv[at, :] += more
            out = mm(kvw[0:64, at], ds)
            return out if acc is None else acc + out

        acc = over(count, step, None if count == 1 else jnp.zeros((HEAD_DIM, 2 * ROWS), F32))
        low_dq = (acc.astype(BF16).astype(F32) * (HEAD_DIM ** -0.5)).astype(BF16)
        for p in range(2):
            j = 2 * i + p
            dq_send[j] = low_dq[:, p * ROWS : (p + 1) * ROWS]
            post(dq_group, j, dq_send.at[j], dq_recv.at[h])
            for k in range(1, G):
                spot = pl.multiple_of((j * G + sib_idx[k]) * ROWS, ROWS)
                dkvs[k - 1, j] = dkv[pl.ds(spot, ROWS), :].astype(BF16)
        for k in range(1, G):
            pairs = slice(2 * i, 2 * i + 2)
            dkv_sib[i, k] = send(dkvs.at[k - 1, pairs], dkvr.at[k - 1, pairs], sib_dev[k])

    def give_back(i):
        for k in range(1, G):
            dkv_sib[i, k].wait_recv()
        for j in (2 * i, 2 * i + 1):
            x = dkv[pl.ds(pl.multiple_of((j * G + g) * ROWS, ROWS), ROWS), :]
            for k in range(1, G):
                x = x + dkvr[k - 1, j].astype(F32)
            dkv_red[j] = x.astype(BF16)
            post(dkv_group, j, dkv_red.at[j], dkv_recv.at[h])

    for i in reversed(range(tiles)):
        attend_back(i)
        if i < tiles - 1:
            give_back(i + 1)
        tick()
    give_back(0)
    dq_recv[h] = dq_send[h]
    dkv_recv[h] = dkv_red[h]
    tick()

    tok_flip.wait_recv()

    @pl.loop(0, HEADS)
    def _(j):
        n, _ = row_norm(tok[j].astype(F32))
        nall[j] = (n * gain1 + bias1).astype(BF16)

    dq_cat = jnp.concatenate([dq_send[j] for j in range(HEADS)], axis=1)
    dkv_cat = jnp.concatenate([dkv_red[j].astype(F32).T.astype(BF16) for j in range(HEADS)], axis=1)
    heads_t = jnp.concatenate([dq_cat, dkv_cat], axis=0)
    gw = mm(heads_t, nall[...].reshape(HEADS * ROWS, D)).astype(BF16)
    for q in range(F):
        gp[q // Gm, q % Gm] = gw[:, 128 * q : 128 * (q + 1)]
    g_sib = {k: send(gp.at[:, sib_idx[k] % Gm], gr1.at[k - 1], sib_dev[k]) for k in range(1, G)}
    tick()
    for k in range(1, G):
        g_sib[k].wait_recv()
    own = gp[:, g % Gm].astype(F32)
    for k in range(1, G):
        own = own + gr1[k - 1].astype(F32)
    gs[...] = own.astype(BF16)
    if plan.S > 1:
        g_seq = send(gs, gr2, far)
    tick()

    arrived(dq_group, dq_recv)
    arrived(dkv_group, dkv_recv)
    tick()
    lane = lax.broadcasted_iota(jnp.int32, (ROWS, 128), 1)
    left = lane < 64
    cols = [[], []]
    for i in range(HEADS // 2):
        a = dkv_recv[2 * i].astype(F32)
        b = dkv_recv[2 * i + 1].astype(F32)
        cols[0].append(jnp.where(left, a, pltpu.roll(b, 64, 1)))
        cols[1].append(jnp.where(left, pltpu.roll(a, 64, 1), b))
    kv_cols = jnp.concatenate(cols[0] + cols[1], axis=1).astype(BF16)
    grad_normed = mm(kv_cols, wq[:, D:], 1, 1) + mm(dq_recv[...].reshape(D, ROWS), wq[:, :D], 0, 1)
    n_one, r_one = row_norm(tok[h].astype(F32))
    scatter_row(v1, 0, jnp.sum(grad_normed * n_one, axis=0, keepdims=True))
    scatter_row(v1, 1, jnp.sum(grad_normed, axis=0, keepdims=True))
    v1_sib = {k: send(v1, v1r.at[k - 1], sib_dev[k]) for k in range(1, G)}
    e1 = grad_normed * gain1
    out_dx[...] = mid[...] + r_one * (
        e1 - jnp.mean(e1, axis=1, keepdims=True) - n_one * jnp.mean(e1 * n_one, axis=1, keepdims=True))
    tick()
    for k in range(1, G):
        v1_sib[k].wait_recv()
    acc1 = v1[...]
    for k in range(1, G):
        acc1 = acc1 + v1r[k - 1]
    v1s[...] = acc1
    if plan.S > 1:
        v1_seq = send(v1s, v1r2, far)
    tick()
    if plan.S > 1:
        g_seq.wait_recv()
        gt[...] = (gs[...].astype(F32) + gr2[...].astype(F32)).astype(BF16)
    else:
        gt[...] = gs[...]
    gr[h] = gt[fs // Gm]
    g_in = {}
    for k in range(1, HEADS):
        there = (head_idx[k] * G + g) % F
        g_in[k] = send(gt.at[there // Gm], gr.at[h], head_dev[k])
        if k % 2 == 0:
            tick()
    if plan.S > 1:
        v1_seq.wait_recv()
        v1t[...] = v1s[...] + v1r2[...]
    else:
        v1t[...] = v1s[...]
    v1_in = {}
    for k in range(1, HEADS):
        there = (head_idx[k] * G + g) % F
        v1_in[k] = send(v1t.at[there], v1r3.at[h], head_dev[k])
    v1r3[h] = v1t[fs]
    step_parts(len(events))
    while not all(p.done for p in parts):
        for p in parts:
            p.pump()
    out_v[...] = vacc[len(parts[-1].steps) - 1, fs]

    for k in range(1, HEADS):
        g_in[k].wait_recv()
    for i in range(HEADS // 2):
        for part_no in range(3):
            lo, hi = 64 * part_no, 64 * (part_no + 1)
            x = jnp.concatenate([gr[2 * i, lo:hi, :], gr[2 * i + 1, lo:hi, :]], axis=0)
            out_dq[:, D * part_no + 128 * i : D * part_no + 128 * (i + 1)] = x.astype(F32).T
    for k in range(1, HEADS):
        v1_in[k].wait_recv()
    out_v1[...] = jnp.sum(v1r3[...], axis=0)
    for copy in sent:
        copy.wait_send()
    for to, copy in posted:
        @pl.when(h != to)
        def _(copy=copy):
            copy.wait_send()


def layer(plan, lengths, vectors, tokens, cotangent, qkv_weight, out_weight, up_weight, down_weight):
    G, F, N = plan.G, plan.F, plan.N
    Gm = min(G, F)
    D = tokens.shape[1]
    FF = up_weight.shape[1]
    span = FF // F
    nv = 3 + len(plan.bits)
    shard = span + 4 * 128 + 128
    hbm = pl.BlockSpec(memory_space=pltpu.HBM)
    vm = pl.BlockSpec(memory_space=pltpu.VMEM)
    V = pltpu.VMEM
    sib = max(G - 1, 1)
    nsem = 192 + 8 * G
    heads = lambda: V((HEADS, HEAD_DIM, ROWS), BF16)
    scratch = [
        V((5, 1, 128), BF16), V((span // 128, 128), BF16), V((F, 16, 128), F32),
        V((HEADS, ROWS, D), BF16),
        V((D, 3 * D), BF16), V((D, D), BF16), V((D, FF), BF16), V((FF, D), BF16),
        V((3, HEADS, HEAD_DIM, ROWS), BF16),
        V((HEADS, G, 128, ROWS), BF16),
        V((N * ROWS, 128), BF16), V((128, N * ROWS), BF16),
        heads(), heads(), V((2, HEADS, HEAD_DIM, ROWS), BF16),
        V((HEADS // 2, HEAD_DIM, 2 * ROWS), F32), V((HEADS // 2, 1, 2 * ROWS), F32),
        heads(), heads(),
        V((N * ROWS, 128), F32),
        V((sib, HEADS, ROWS, 128), BF16), V((sib, HEADS, ROWS, 128), BF16),
        V((HEADS, ROWS, 128), BF16), V((HEADS, ROWS, 128), BF16),
        heads(), heads(),
        V((HEADS, ROWS, D), BF16),
        V((F // Gm, Gm, 192, 128), BF16), V((sib, F // Gm, 192, 128), BF16),
        V((F // Gm, 192, 128), BF16), V((F // Gm, 192, 128), BF16), V((F // Gm, 192, 128), BF16),
        V((HEADS, 192, 128), BF16),
        V((F, 8, 128), F32), V((sib, F, 8, 128), F32), V((F, 8, 128), F32), V((F, 8, 128), F32),
        V((F, 8, 128), F32), V((HEADS, 8, 128), F32),
        V((F, 8, 128), F32), V((nv, 4, F, 8, 128), F32), V((nv, F, 8, 128), F32),
        V((ROWS, D), F32),
        V((F, ROWS, span), F32),
        V((2, 2, ROWS, span), BF16), V((2, ROWS, span), BF16),
        V((2, ROWS, D), BF16), V((2, ROWS, D), BF16), V((2, ROWS, FF), BF16), V((2, ROWS, D), BF16),
        V((2, shard, D), BF16),
        V((3 * shard, D), BF16), V((3 * shard, D), BF16),
        pltpu.SemaphoreType.DMA((16,)), pltpu.SemaphoreType.DMA((nsem,)), pltpu.SemaphoreType.DMA((nsem,)),
    ]
    S = jax.ShapeDtypeStruct
    return pl.pallas_call(
        partial(body, plan),
        out_shape=(S((ROWS, D), BF16), S((ROWS, D), F32), S((ROWS, 3 * D), F32),
                   S((shard, D), BF16), S((8, 128), F32), S((8, 128), F32)),
        in_specs=[pl.BlockSpec(memory_space=pltpu.SMEM)] + [hbm] * 12,
        out_specs=(vm,) * 6,
        scratch_shapes=scratch,
        compiler_params=pltpu.CompilerParams(
            collective_id=0, has_side_effects=True, vmem_limit_bytes=(34 << 20) + 12 * N * ROWS * 128),
    )(lengths, *(pltpu.with_memory_space_constraint(x, pltpu.HBM) for x in (
        *vectors, tokens, cotangent, qkv_weight, out_weight, up_weight, down_weight)))


def finish(y, dx, dq, r, v, v1, o_y, o_dx, o_g1, o_b1, o_dq, o_out, o_g2, o_b2, o_up, o_ub, o_down, o_db, o_rms,
           down, up, out, sem):
    D = dx.shape[1]
    span = o_down.shape[0]
    n = span // 128

    def go(i, src, dst):
        copy = pltpu.make_async_copy(src, dst, sem.at[i])
        copy.start()
        return copy

    outs = [go(0, dq, o_dq), go(1, dx, o_dx), go(2, y, o_y)]
    for q in range(o_up.shape[1] // span):
        up[:, q * span : (q + 1) * span] = r[span + 128 * q : span + 128 * (q + 1), :].astype(F32)
    outs.append(go(3, up, o_up))
    down[...] = r[0:span, :].astype(F32)
    outs.append(go(4, down, o_down))
    out[...] = r[span + 512 : span + 640, :].astype(F32)
    outs.append(go(5, out, o_out))
    o_g1[...] = v1[0:1, :]
    o_b1[...] = v1[1:2, :]
    o_g2[...] = v[0:1, :]
    o_b2[...] = v[1:2, :]
    o_ub[...] = v[2 : 2 + n, :]
    o_db[...] = v[2 + n : 3 + n, :]
    stats = v[3 + n : 4 + n, :]
    o_rms[...] = jnp.sqrt(stats[:, 0:3] / (stats[:, 3:4] * D))
    for copy in outs:
        copy.wait()


def on_device(plan, tokens, lengths, ln1_gain, ln1_bias, qkv_weight, out_weight, ln2_gain, ln2_bias,
              up_weight, up_bias, down_weight, down_bias, cotangent):
    D = tokens.shape[1]
    F = plan.F
    span = up_weight.shape[1] // F
    vectors = [x.reshape(-1, 128) for x in (ln1_gain, ln1_bias, ln2_gain, ln2_bias, up_bias, down_bias)]
    results = layer(
        plan, lengths, vectors, tokens, cotangent, qkv_weight, out_weight, up_weight, down_weight)
    S = jax.ShapeDtypeStruct
    vec = S((1, 128), F32)
    vm = pl.BlockSpec(memory_space=pltpu.VMEM)
    hbm = pl.BlockSpec(memory_space=pltpu.HBM)
    outs = pl.pallas_call(
        finish,
        out_shape=(S((ROWS, D), BF16), S((ROWS, D), F32), vec, vec, S((ROWS, 3 * D), F32), S((128, D), F32),
                   vec, vec, S((128, F * span), F32), S((span // 128, 128), F32), S((span, D), F32), vec,
                   S((1, 3), F32)),
        in_specs=[vm] * 6,
        out_specs=(hbm, hbm, vm, vm, hbm, hbm, vm, vm, hbm, vm, hbm, vm, vm),
        scratch_shapes=[
            pltpu.VMEM((span, D), F32), pltpu.VMEM((128, F * span), F32), pltpu.VMEM((128, D), F32),
            pltpu.SemaphoreType.DMA((6,))],
        compiler_params=pltpu.CompilerParams(vmem_limit_bytes=16 << 20),
    )(*results)
    outs = list(outs)
    for i in (2, 3, 6, 7, 9, 11, 12):
        outs[i] = outs[i].reshape(-1)
    return tuple(outs)


def solution(mesh):
    plan = Plan(mesh.shape["seq"], mesh.shape["ctx"], mesh.shape["fsdp"])
    rows = P(("seq", "ctx", "fsdp"), None)
    f1, f2 = P("fsdp"), P("fsdp", None)
    return jax.shard_map(
        partial(on_device, plan),
        mesh=mesh,
        in_specs=(rows, P("seq"), f1, f1, f2, f2, f1, f1, f2, f1, f2, f1, rows),
        out_specs=(rows, rows, f1, f1, f2, f2, f1, f1, f2, f1, f2, f1, P()),
        check_vma=False,
    )
```

```python
from functools import partial
import itertools

import jax
import jax.numpy as jnp
from jax import lax
from jax.experimental import pallas as pl
from jax.experimental.pallas import tpu as pltpu
from jax.sharding import PartitionSpec as P

HEADS = 8
HEAD_DIM = 64
EPS = 1e-05
NEG = -1e30
F32 = jnp.float32
BF16 = jnp.bfloat16
MESH = pl.DeviceIdType.MESH
ROWS = 128
KEYS = 512
KEYS_BACK = 512
LAST = 2
PARTS = [(0, 256, False, False), (256, 256, False, False), (512, 256, False, False), (768, 128, False, False), (896, 128, True, True), (1024, 128, False, False)]
EVENTS = [0, 1, 2, 3, 4, 5, 0, 6, 6, 4, 1, 0, 6, 1, 2, 0, 6, 3, 1, 5, 2, 0, 4, 6, 3, 2, 5, 1, 0, 3, 5, 4, 2, 1, 0, 3, 5, 4, 1, 2, 3, 0, 5, 4, 2, 3, 1, 5, 2, 3, 5]
TICKS = [1, 1, 3, 1, 1, 1, 3, 2, 0, 4, 1, 6, 4, 0, 5, 4, 0, 7, 0, 0, 0, 0]

ERF_TOP = (
    0.00022905065861350646,
    0.0034082910107109506,
    0.050955695062380861,
    0.18520832239976145,
    1.128379143519084,
)
ERF_LOW = (
    -1.1791602954361697e-7,
    0.000023547966471313185,
    0.0010179625278914885,
    0.014070470171167667,
    0.11098505178285362,
    0.49746925110067538,
    1.0,
)


def mm(a, b, ca=1, cb=0):
    return lax.dot_general(a, b, (((ca,), (cb,)), ((), ())), preferred_element_type=F32)


def erf(x):
    x = jnp.clip(x, -3.832506856900711, 3.832506856900711)
    s = x * x
    top = jnp.full_like(s, ERF_TOP[0])
    for c in ERF_TOP[1:]:
        top = top * s + c
    low = jnp.full_like(s, ERF_LOW[0])
    for c in ERF_LOW[1:]:
        low = low * s + c
    return x * top / low


def row_norm(x):
    center = jnp.mean(x, axis=1, keepdims=True)
    shifted = x - center
    spread = jnp.mean(shifted * shifted, axis=1, keepdims=True)
    r = lax.rsqrt(spread + EPS)
    return shifted * r, r


class Plan:
    def __init__(self, seqs, ctx, fsdp):
        self.S, self.C, self.F = seqs, ctx, fsdp
        self.N = ctx * fsdp
        self.G = self.N // HEADS
        self.bits = []
        b = 1
        while b < ctx:
            self.bits.append(b)
            b *= 2

    def split(self, dev):
        s, c, f = dev
        p = c * self.F + f
        return p // self.G, p % self.G

    def at(self, s, p):
        return (s, p // self.F, p % self.F)

    def head_peer(self, dev, k):
        h, g = self.split(dev)
        return self.at(dev[0], ((h + k) % HEADS) * self.G + g)

    def flip_peer(self, dev):
        h, g = self.split(dev)
        return self.at(dev[0], (h + 1 - 2 * (h % 2)) * self.G + g)

    def sibling(self, dev, k):
        h, g = self.split(dev)
        return self.at(dev[0], h * self.G + (g + k) % self.G)

    def fsdp_low(self, dev):
        s, c, f = dev
        return (s, c, f + 1 - 2 * (f % 2))

    def fsdp_high(self, dev):
        s, c, f = dev
        return (s, c, (f + 2) % self.F)

    def seq_peer(self, dev):
        s, c, f = dev
        return ((s + 1) % self.S, c, f)

    def ctx_peer(self, dev, b):
        s, c, f = dev
        return (s, c + b - 2 * b * ((c // b) % 2), f)

    def quad_peer(self, dev, b, k):
        s, c, f = dev
        return (s, (c // (4 * b)) * (4 * b) + ((c // b + k) % 4) * b + c % b, f)

    def greeted(self):
        base = [partial(self._head, k) for k in range(1, HEADS)]
        base += [partial(self._sib, k) for k in range(1, self.G)]
        base += [self.seq_peer]
        more = [self.fsdp_low, self.fsdp_high] + [partial(self._ctx, b) for b in self.bits]
        more += [partial(self._quad, b, k) for b in self.bits[:-1:2] for k in (1, 2, 3)]
        devs = list(itertools.product(range(self.S), range(self.C), range(self.F)))
        for extra in more:
            if not all(extra(d) in [p(d) for p in base] for d in devs):
                base.append(extra)
        return base

    def _head(self, k, dev):
        return self.head_peer(dev, k)

    def _sib(self, k, dev):
        return self.sibling(dev, k)

    def _quad(self, b, k, dev):
        return self.quad_peer(dev, b, k)

    def _ctx(self, b, dev):
        return self.ctx_peer(dev, b)


def body(plan, lens, g1_in, b1_in, g2_in, b2_in, ub_in, db_in, tok_in, cot_in, wq_in, wo_in, wu_in, wd_in,
         out_y, out_dx, out_dq, out_down, out_up, out_out, out_v, out_v1,
         raw, rawu, small, tok, wq, wo, wu, wd,
         msg, kvb, kvn, kvw, qb, o_send, at2, ot, lse, do_send, do_recv,
         dkv, dkvs, dkvr, dkv_red, dkv_recv, dq_send, dq_recv, nall,
         gp, gr1, gs, gr2, gt, gr,
         v1, v1r, v1s, v1r2, v1t, v1r3, v0, vrecv, vacc,
         mid, slope, out_r, actb, xa, c2, n2, g2, gb2, sa, into, sums, lsem, ssem, rsem):
    G, F, N = plan.G, plan.F, plan.N
    Gm = min(G, F)
    seq, ctx, fs = (lax.axis_index(a) for a in ("seq", "ctx", "fsdp"))
    me = (seq, ctx, fs)
    h, g = plan.split(me)
    fl, fh = fs % 2, fs // 2
    D = tok.shape[2]
    FF = wu.shape[1]
    span = FF // F
    valid = lens[0]
    counter = itertools.count()
    locals_ = itertools.count()

    def local(src, dst):
        copy = pltpu.make_async_copy(src, dst, lsem.at[next(locals_)])
        copy.start()
        return copy

    l_raw = [local(x, raw.at[i]) for i, x in enumerate((g1_in, b1_in, g2_in, b2_in, db_in))]
    l_raw.append(local(ub_in, rawu))
    l_tok = local(tok_in, tok.at[h])
    greet = plan.greeted()
    bar = pltpu.get_barrier_semaphore()
    for peer in greet:
        pl.semaphore_signal(bar, inc=1, device_id=peer(me), device_id_type=MESH)
    for copy in l_raw:
        copy.wait()
    own = [raw[i].astype(F32) for i in range(4)] + [rawu[...].astype(F32), raw[4].astype(F32)]
    used = 5 + span // 128
    small[fs] = jnp.concatenate(own + [jnp.zeros((16 - used, 128), F32)], axis=0)
    pl.semaphore_wait(bar, len(greet))

    sent = []

    def send(src, dst, dev):
        n = next(counter)
        copy = pltpu.make_async_remote_copy(
            src_ref=src, dst_ref=dst, send_sem=ssem.at[n], recv_sem=rsem.at[n],
            device_id=dev, device_id_type=MESH)
        copy.start()
        sent.append(copy)
        return copy

    posted = []

    def new_group():
        first = next(counter)
        for _ in range(HEADS - 1):
            next(counter)
        return first

    def post(group, to, src, dst):
        copy = pltpu.make_async_remote_copy(
            src_ref=src, dst_ref=dst, send_sem=ssem.at[group + to], recv_sem=rsem.at[group + h],
            device_id=plan.at(seq, to * G + g), device_id_type=MESH)

        @pl.when(h != to)
        def _():
            copy.start()

        posted.append((to, copy))

    def arrived(group, ref):
        for source in range(HEADS):
            copy = pltpu.make_async_remote_copy(
                src_ref=ref.at[source], dst_ref=ref.at[source], send_sem=ssem.at[group + source],
                recv_sem=rsem.at[group + source], device_id=plan.at(seq, source * G + g), device_id_type=MESH)

            @pl.when(h != source)
            def _():
                copy.wait_recv()

    low, high = plan.fsdp_low(me), plan.fsdp_high(me)
    fhigh = (fs + 2) % F
    head_dev = {k: plan.head_peer(me, k) for k in range(1, HEADS)}
    head_idx = {k: (h + k) % HEADS for k in range(1, HEADS)}
    sib_dev = {k: plan.sibling(me, k) for k in range(1, G)}
    sib_idx = {k: (g + k) % G for k in range(1, G)}

    far = plan.seq_peer(me)
    sm_low = send(small.at[fs], small.at[fs], low)
    sm_high = send(small.at[fs], small.at[fs], high)
    shards = ((wq_in, wq, 128), (wo_in, wo, 128), (wu_in, wu, 128), (wd_in, wd, span))

    def rows_of(w, first, count):
        return w.at[pl.ds(pl.multiple_of(first, count), count), :]

    def group_of(ref, which, c):
        return ref.at[pl.ds(pl.multiple_of(which * 128, 128), 128), c * D : (c + 1) * D]

    order = (1, 2, 0)
    q_high = {c: send(wq_in.at[:, c * D : (c + 1) * D], group_of(wq, fs, c), high) for c in order}
    q_low = {c: send(wq_in.at[:, c * D : (c + 1) * D], group_of(wq, fs, c), low) for c in order}
    half_rows = ROWS // 2

    def tokens_out(part):
        rows = slice(part * half_rows, (part + 1) * half_rows)
        return [send(tok_in.at[rows, :], tok.at[h, rows, :], head_dev[k]) for k in (2, 4, 6)]

    tok_copies = tokens_out(0)
    w_high, w_low = {}, {}
    for q in range(1, 4):
        src, dst, step = shards[q]
        w_low[q] = send(src, rows_of(dst, fs * step, step), low)
    l_w = [local(src, rows_of(dst, fs * step, step)) for src, dst, step in shards]
    l_cot = local(cot_in, c2.at[0])

    crossed, passed = {}, {}
    cuts = {1: 1, 2: 2, 3: 2}

    def slice_of(q, owner, p):
        count = shards[q][2] // (2 * cuts[q])
        first = (seq * cuts[q] + p) * count
        return count, first, owner * shards[q][2] + first

    def fetch(q):
        src, dst, step = shards[q]
        for p in range(cuts[q]):
            count, first, at = slice_of(q, fs, p)
            w_high[q, p] = send(rows_of(src, first, count), rows_of(dst, at, count), high)

    def cross(q, p):
        w_high[q, p].wait_recv()
        count, _, at = slice_of(q, fhigh, p)
        piece = rows_of(shards[q][1], at, count)
        crossed[q, p] = send(piece, piece, far)

    def hand_on(q):
        for p in range(cuts[q]):
            crossed[q, p].wait_recv()
        _, dst, step = shards[q]
        piece = rows_of(dst, fhigh * step, step)
        passed[q] = send(piece, piece, low)

    sm_low.wait_recv()
    sm_high.wait_recv()
    sm_fwd = send(small.at[fhigh], small.at[fhigh], low)
    l_tok.wait()
    inputs = tok[h].astype(F32)
    n_one, r_one = row_norm(inputs)
    sm_fwd.wait_recv()

    def vec(first, many=1):
        return jnp.concatenate(
            [small[q, first + r : first + r + 1, :] for q in range(F) for r in range(many)], axis=1)

    gain1, bias1, gain2, bias2 = vec(0), vec(1), vec(2), vec(3)
    down_bias = vec(4 + span // 128)
    normed = (n_one * gain1 + bias1).astype(BF16)
    nall[h] = normed
    l_w[0].wait()
    qkv_in = {}
    for c in order:
        q_low[c].wait_recv()
        q_high[c].wait_recv()
        piece = group_of(wq, fhigh, c)
        handed = send(piece, piece, low)
        handed.wait_recv()
        proj = mm(normed, wq[:, c * D : (c + 1) * D])
        if c == 0:
            proj = proj * (HEAD_DIM ** -0.5)
        msg[c] = proj.T.astype(BF16).reshape(HEADS, HEAD_DIM, ROWS)
        for k in range(1, HEADS):
            dst = qb.at[h] if c == 0 else kvb.at[h, g, (c - 1) * 64 : c * 64]
            qkv_in[c, k] = send(msg.at[c, head_idx[k]], dst, head_dev[k])
        if c == 0:
            qb[h] = msg[c, h]
        else:
            kvb[h, g, (c - 1) * 64 : c * 64] = msg[c, h]
    fetch(1)
    fetch(2)
    fetch(3)
    tok_copies += tokens_out(1)
    for c in (1, 2):
        for k in range(1, HEADS):
            qkv_in[c, k].wait_recv()
    kv_sib = {k: send(kvb.at[:, g], kvb.at[:, g], sib_dev[k]) for k in range(1, G)}

    def spread_block(hp, gg):
        at = pl.multiple_of((hp * G + gg) * ROWS, ROWS)
        block = kvb[hp, gg]
        kvw[:, pl.ds(at, ROWS)] = block
        kvn[pl.ds(at, ROWS), :] = block.astype(F32).T.astype(BF16)

    @pl.loop(0, HEADS)
    def _(hp):
        spread_block(hp, g)

    for k in range(1, G):
        kv_sib[k].wait_recv()
    for k in range(1, G):
        @pl.loop(0, HEADS)
        def _(hp, k=k):
            spread_block(hp, sib_idx[k])
    cross(1, 0)
    for k in range(1, HEADS):
        qkv_in[0, k].wait_recv()

    tiles = HEADS // 2

    def span_of(i, most):
        keys = (i + 1) * 2 * G * ROWS
        count = 1
        while keys % count or keys // count > most:
            count += 1
        return keys // count, count

    def over(count, step, start):
        return step(0, start) if count == 1 else lax.fori_loop(0, count, step, start)

    def keys_at(kc, size):
        return pl.ds(pl.multiple_of(kc * size, size), size) if not isinstance(kc, int) else slice(0, size)

    def key_iota(size):
        return lax.broadcasted_iota(jnp.int32, (size, 2 * ROWS), 0)

    def limits(i):
        col = lax.broadcasted_iota(jnp.int32, (1, 2 * ROWS), 1)
        pos = ((2 * i + col // ROWS) * G + g) * ROWS + col % ROWS
        return jnp.minimum(pos + 1, valid)

    nothing = jnp.zeros((HEAD_DIM, 2 * ROWS), BF16)

    def attend(i):
        qt = jnp.concatenate([qb[2 * i], qb[2 * i + 1]], axis=1)
        stacked = jnp.concatenate([qt, nothing], axis=0)
        limit = limits(i)

        size, count = span_of(i, KEYS)

        def step(kc, carry):
            at = keys_at(kc, size)
            st = mm(kvn[at, :], stacked)
            st = jnp.where(key_iota(size) < limit - kc * size, st, NEG)
            mn = jnp.max(st, axis=0, keepdims=True)
            if carry is not None:
                m, l, acc = carry
                mn = jnp.maximum(m, mn)
            e = jnp.exp(st - mn)
            total_e = jnp.sum(e, axis=0, keepdims=True)
            out = mm(kvw[64:128, at], e.astype(BF16))
            if carry is not None:
                al = jnp.exp(m - mn)
                total_e, out = l * al + total_e, acc * al + out
            return mn, total_e, out

        first = None if count == 1 else (
            jnp.full((1, 2 * ROWS), NEG, F32), jnp.zeros((1, 2 * ROWS), F32),
            jnp.zeros((HEAD_DIM, 2 * ROWS), F32))
        m, l, acc = over(count, step, first)
        o = acc / l
        ot[i] = o
        lse[i] = m + jnp.log(l)
        for p in range(2):
            o_send[2 * i + p] = o[:, p * ROWS : (p + 1) * ROWS].astype(BF16)
            post(o_group, 2 * i + p, o_send.at[2 * i + p], at2.at[0, h])

    o_group = new_group()
    for i in range(tiles):
        attend(i)
        if i == 1:
            cross(2, 0)
        if i == 2:
            cross(2, 1)
            hand_on(1)
    at2[0, h] = o_send[h]
    cross(3, 0)
    parity = h % 2
    flip = plan.flip_peer(me)
    for copy in tok_copies:
        copy.wait_recv()
    l_cot.wait()
    sib_c = send(c2.at[0], c2.at[1], low)
    tok4 = tok.reshape(HEADS // 2, 2, ROWS, D)
    tok_flip = send(tok4.at[:, parity], tok4.at[:, parity], flip)
    hand_on(2)
    cross(3, 1)
    arrived(o_group, at2.at[0])
    sib_at = send(at2.at[0], at2.at[1], low)

    def add_rows(dst, refs, rows):
        block = max(b for b in (16, 32, 64) if rows % b == 0)

        @pl.loop(0, rows // block)
        def _(t):
            at = pl.ds(pl.multiple_of(t * block, block), block)
            if len(refs) == 2:
                dst[at, :] = refs[0][at, :] + refs[1][at, :]
            else:
                x = refs[0][at, :].astype(F32)
                for ref in refs[1:]:
                    x = x + ref[at, :].astype(F32)
                dst[at, :] = x.astype(BF16)

    pool = {"into": 0, "sums": 0}

    def take(name, rows):
        first = pool[name]
        pool[name] += rows
        ref = {"into": into, "sums": sums}[name]
        return ref.at[pl.ds(first, rows), :]

    class Part:
        def __init__(self, first, rows, y_first, quads):
            self.first, self.rows = first, rows
            self.off, self.n = first, rows
            self.pair = sa.at[:, pl.ds(first, rows), :]
            self.piece = None
            x = ("cut", [far], 2, seq)
            y = ("pick", [high], 2, fh)
            self.steps = [y, x] if y_first else [x, y]
            n, bits = rows // 2, list(plan.bits)
            while bits:
                b = bits[0]
                if quads and len(bits) > 1 and n % 64 == 0:
                    peers = [plan.quad_peer(me, b, k) for k in (1, 2, 3)]
                    self.steps.append(("cut", peers, 4, (ctx // b) % 4))
                    bits, n = bits[2:], n // 4
                else:
                    kind = "cut" if n % 32 == 0 else "whole"
                    self.steps.append((kind, [plan.ctx_peer(me, b)], 2, (ctx // b) % 2))
                    bits, n = bits[1:], n // 2 if kind == "cut" else n
            self.trail = []
            self.t = -1
            self.done = False

        def pump(self):
            if self.done:
                return
            if self.t >= 0:
                for copy in self.copies:
                    copy.wait_recv()
                if self.t < len(self.steps):
                    self.finish()
                else:
                    self.off, self.n = self.region
            self.t += 1
            if self.t < len(self.steps):
                self.begin()
            elif self.trail:
                peers, off, n = self.trail.pop()
                region = out_r.at[pl.ds(pl.multiple_of(self.off, 16), self.n), :]
                self.copies = [send(region, region, dev) for dev in peers]
                self.region = off, n
            else:
                self.done = True
                self.store()

        def store(self):
            for row in range(self.first, self.first + self.rows, 128):
                x = out_r[row : row + 128, :].astype(F32)
                if row < span:
                    out_down[row : row + 128, :] = x
                elif row < span + 512:
                    q = (row - span) // 128
                    out_up[:, q * span : (q + 1) * span] = x
                else:
                    out_out[...] = x

        def slot(self, ref, which, size):
            return ref.at[pl.ds(pl.multiple_of(which * size, 16), size), :]

        def begin(self):
            kind, peers, ways, mine = self.steps[self.t]
            self.size = self.n // ways if kind == "cut" else self.n
            self.got, self.copies = [], []
            for k, dev in enumerate(peers):
                there = (mine + k + 1) % ways
                if self.piece is None and kind == "cut":
                    got = take("into", 2 * self.size).reshape(2, self.size, D)
                    src = self.pair.at[:, pl.ds(pl.multiple_of(there * self.size, 16), self.size), :]
                else:
                    got = take("into", self.size)
                    if kind == "pick":
                        src = self.pair.at[there]
                    elif kind == "cut":
                        src = self.slot(self.piece, there, self.size)
                    else:
                        src = self.piece
                self.got.append(got)
                self.copies.append(send(src, got, dev))

        def finish(self):
            kind, peers, ways, mine = self.steps[self.t]
            size = self.size
            if kind == "cut":
                self.trail.append((peers, self.off, self.n))
                self.off = self.off + mine * size
            if self.piece is None and kind == "cut":
                dst = take("sums", 2 * size).reshape(2, size, D)
                for y in range(2):
                    add_rows(dst.at[y], [self.slot(self.pair.at[y], mine, size)] + [got.at[y] for got in self.got], size)
                self.pair = dst
            else:
                if self.t + 1 == len(self.steps):
                    dst = out_r.at[pl.ds(pl.multiple_of(self.off, 16), size), :]
                else:
                    dst = take("sums", size)
                if kind == "pick":
                    own = self.pair.at[mine]
                elif kind == "cut":
                    own = self.slot(self.piece, mine, size)
                else:
                    own = self.piece
                add_rows(dst, [own] + self.got, size)
                self.piece = dst
            self.n = size

    class Vectors:
        def __init__(self):
            self.steps = [([p], 2, None) for p in (low, high)]
            bits = list(plan.bits)
            while bits:
                b = bits[0]
                if len(bits) > 1:
                    self.steps.append(([plan.quad_peer(me, b, k) for k in (1, 2, 3)], 4, (ctx // b) % 4))
                    bits = bits[2:]
                else:
                    self.steps.append(([plan.ctx_peer(me, b)], 2, None))
                    bits = bits[1:]
            self.steps.append(([far], 2, None))
            self.t = -1
            self.done = False

        def begin(self, src):
            peers, ways, mine = self.steps[self.t]
            if ways == 2:
                self.copies = [send(src, vrecv.at[self.t, 0], peers[0])]
            else:
                vrecv[self.t, mine] = src[...]
                self.copies = [send(src, vrecv.at[self.t, mine], dev) for dev in peers]

        def pump(self):
            if self.done:
                return
            t = self.t
            if t < 0:
                self.t = 0
                self.begin(v0)
                return
            for copy in self.copies:
                copy.wait_recv()
            if self.steps[t][1] == 2:
                vacc[t] = (v0[...] if t == 0 else vacc[t - 1]) + vrecv[t, 0]
            else:
                vacc[t] = (vrecv[t, 0] + vrecv[t, 1]) + (vrecv[t, 2] + vrecv[t, 3])
            self.t += 1
            if self.t < len(self.steps):
                self.begin(vacc.at[t])
            else:
                self.done = True

    events, parts = [], []

    turns = iter(TICKS)

    def step_parts(count):
        for _ in range(min(count, len(events))):
            parts[events.pop(0)].pump()

    def tick():
        step_parts(next(turns))

    for q in range(1, 4):
        l_w[q].wait()
        w_low[q].wait_recv()
    passed[1].wait_recv()
    at_t = at2[0].reshape(D, ROWS)
    attention_out = mm(at_t, wo[...], 0, 0)
    middle = tok[h].astype(F32) + attention_out
    n_two, r_two = row_norm(middle)
    normed_two = (n_two * gain2 + bias2).astype(BF16)
    n2[0] = normed_two
    sib_n = send(n2.at[0], n2.at[1], low)
    passed[2].wait_recv()
    sib_a = []
    half = span // 2
    for p in range(2):
        mine = slice(p * half, (p + 1) * half)
        for q in range(F):
            rows = range(4 + p * half // 128, 4 + (p + 1) * half // 128)
            bias = jnp.concatenate([small[q, r : r + 1, :] for r in rows], axis=1)
            raised = mm(normed_two, wu[:, q * span + p * half : q * span + (p + 1) * half]) + bias
            cdf = 0.5 * (1.0 + erf(raised * (0.5 ** 0.5)))
            pdf = jnp.exp(-0.5 * raised * raised) * 0.3989422804014327
            actb[q // 2, q % 2, :, mine] = (raised * cdf).astype(BF16)
            slope[q, :, mine] = cdf + raised * pdf
        sib_a.append(send(actb.at[:, 1 - fl, :, mine], xa.at[:, :, mine], low))
    sib_c.wait_recv()
    both_c = c2[...].reshape(2 * ROWS, D)
    cots = c2[0]
    gnt = jnp.zeros((ROWS, D), F32)

    def back_block(step, gnt):
        q = (2 * fh + step) % F
        cols = pl.ds(pl.multiple_of(q * span, span), span)
        grad = (mm(cots, wd[cols, :], 1, 1) * slope[q]).astype(BF16)
        g2[0, :, cols] = grad
        return gnt + mm(grad, wu[:, cols], 1, 1)

    def share_blocks(y):
        cols = pl.ds(pl.multiple_of(y * 2 * span, 2 * span), 2 * span)
        return send(g2.at[0, :, cols], g2.at[1, :, cols], low)

    parts += [Part(*p) for p in PARTS]
    events += EVENTS
    for p in range(2):
        mine = slice(p * half, (p + 1) * half)
        sib_a[p].wait_recv()
        for y in range(2):
            a = jnp.concatenate([actb[y, fl, :, mine], xa[y, :, mine]], axis=0)
            sa[y, mine, :] = mm(a, both_c, 0, 0).astype(BF16)
        tick()
        gnt = back_block(p, gnt)
    sib_g = [share_blocks(fh)]
    hand_on(3)
    passed[3].wait_recv()
    for step in range(F // 2, F):
        gnt = back_block(step, gnt)
    sib_g.append(share_blocks(1 - fh))

    def scatter_row(ref, row, x):
        for q in range(F):
            ref[q, row : row + 1, :] = x[:, 128 * q : 128 * (q + 1)]

    grad_final = cots.astype(F32)
    e2 = gnt * gain2
    grad_middle = grad_final + r_two * (
        e2 - jnp.mean(e2, axis=1, keepdims=True) - n_two * jnp.mean(e2 * n_two, axis=1, keepdims=True))
    mid[...] = grad_middle
    gb = grad_middle.astype(BF16)
    gb2[0] = gb
    sib_b = send(gb2.at[0], gb2.at[1], low)
    ga = mm(wo[...], gb, 1, 1).astype(BF16)
    do_send[...] = ga.reshape(HEADS, HEAD_DIM, ROWS)
    do_in = {k: send(do_send.at[head_idx[k]], do_recv.at[h], head_dev[k]) for k in range(1, HEADS)}
    do_recv[h] = do_send[h]

    sib_n.wait_recv()
    for copy in sib_g:
        copy.wait_recv()
    for y in range(2):
        spot = pl.ds(pl.multiple_of((2 * y + fl) * 128, 128), 128)
        a = n2[:, :, spot].reshape(2 * ROWS, 128)
        for q in range(F):
            cols = slice(q * span, (q + 1) * span)
            sa[y, span + 128 * q : span + 128 * (q + 1), :] = mm(
                a, g2[:, :, cols].reshape(2 * ROWS, span), 0, 0).astype(BF16)
    tick()
    sib_at.wait_recv()
    sib_b.wait_recv()
    for y in range(2):
        x = jnp.zeros((128, D), F32)
        for p in range(2):
            rows = at2[p, pl.ds(pl.multiple_of((2 * y + fl) * 2, 2), 2)].reshape(128, ROWS)
            x = x + mm(rows, gb2[p])
        sa[y, span + 512 : span + 640, :] = x.astype(BF16)

    tick()

    feed_out = down_bias
    for q in range(F):
        cols = slice(q * span, (q + 1) * span)
        feed_out = feed_out + mm(actb[q // 2, q % 2], wd[cols, :])
        grad = g2[0, :, cols].astype(F32)
        v0[q, 2 : 2 + span // 128, :] = jnp.concatenate(
            [jnp.sum(grad[:, 128 * r : 128 * (r + 1)], axis=0, keepdims=True)
             for r in range(span // 128)], axis=0)
    final = middle + feed_out
    out_y[...] = final.astype(BF16)
    scatter_row(v0, 0, jnp.sum(gnt * n_two, axis=0, keepdims=True))
    scatter_row(v0, 1, jnp.sum(gnt, axis=0, keepdims=True))
    scatter_row(v0, 2 + span // 128, jnp.sum(grad_final, axis=0, keepdims=True))
    place = (ctx * F + fs) * ROWS
    row = lax.broadcasted_iota(jnp.int32, (ROWS, 1), 0) + place
    live = (row < valid).astype(F32)

    def total(x):
        return jnp.sum(jnp.sum(x, axis=1, keepdims=True) * live, axis=0, keepdims=True)

    lane1 = lax.broadcasted_iota(jnp.int32, (1, 128), 1)
    stats = jnp.where(lane1 == 0, total(final * final), 0.0)
    stats = jnp.where(lane1 == 1, total(attention_out * attention_out), stats)
    stats = jnp.where(lane1 == 2, total(feed_out * feed_out), stats)
    stats = jnp.where(lane1 == 3, jnp.sum(live, axis=0, keepdims=True), stats)
    for q in range(F):
        v0[q, 3 + span // 128 : 4 + span // 128, :] = stats

    parts.append(Vectors())
    tick()
    for k in range(1, HEADS):
        do_in[k].wait_recv()
    tick()

    dq_group, dkv_group = new_group(), new_group()
    dkv_sib = {}

    def attend_back(i):
        qt = jnp.concatenate([qb[2 * i], qb[2 * i + 1]], axis=1)
        dt = jnp.concatenate([do_recv[2 * i], do_recv[2 * i + 1]], axis=1)
        stacked = jnp.concatenate(
            [jnp.concatenate([qt, nothing], axis=1), jnp.concatenate([nothing, dt], axis=1)], axis=0)
        delta = jnp.sum(dt.astype(F32) * ot[i], axis=0, keepdims=True)
        level = lse[i]
        limit = limits(i)

        size, count = span_of(i, KEYS_BACK)

        def step(kc, acc):
            at = keys_at(kc, size)
            both = mm(kvn[at, :], stacked)
            st = jnp.where(key_iota(size) < limit - kc * size, both[:, : 2 * ROWS], NEG)
            p = jnp.exp(st - level)
            ds = (p * (both[:, 2 * ROWS :] - delta)).astype(BF16)
            pair = jnp.concatenate([ds, p.astype(BF16)], axis=1)
            more = mm(pair, stacked, 1, 1)
            if i == tiles - 1:
                dkv[at, :] = more
            else:
                dkv[at, :] += more
            out = mm(kvw[0:64, at], ds)
            return out if acc is None else acc + out

        acc = over(count, step, None if count == 1 else jnp.zeros((HEAD_DIM, 2 * ROWS), F32))
        low_dq = (acc.astype(BF16).astype(F32) * (HEAD_DIM ** -0.5)).astype(BF16)
        for p in range(2):
            j = 2 * i + p
            dq_send[j] = low_dq[:, p * ROWS : (p + 1) * ROWS]
            post(dq_group, j, dq_send.at[j], dq_recv.at[h])
            for k in range(1, G):
                spot = pl.multiple_of((j * G + sib_idx[k]) * ROWS, ROWS)
                dkvs[k - 1, j] = dkv[pl.ds(spot, ROWS), :].astype(BF16)
        for k in range(1, G):
            pairs = slice(2 * i, 2 * i + 2)
            dkv_sib[i, k] = send(dkvs.at[k - 1, pairs], dkvr.at[k - 1, pairs], sib_dev[k])

    def give_back(i):
        for k in range(1, G):
            dkv_sib[i, k].wait_recv()
        for j in (2 * i, 2 * i + 1):
            x = dkv[pl.ds(pl.multiple_of((j * G + g) * ROWS, ROWS), ROWS), :]
            for k in range(1, G):
                x = x + dkvr[k - 1, j].astype(F32)
            dkv_red[j] = x.astype(BF16)
            post(dkv_group, j, dkv_red.at[j], dkv_recv.at[h])

    for i in reversed(range(tiles)):
        attend_back(i)
        if i < tiles - 1:
            give_back(i + 1)
        tick()
    give_back(0)
    dq_recv[h] = dq_send[h]
    dkv_recv[h] = dkv_red[h]
    tick()

    tok_flip.wait_recv()

    @pl.loop(0, HEADS)
    def _(j):
        n, _ = row_norm(tok[j].astype(F32))
        nall[j] = (n * gain1 + bias1).astype(BF16)

    dq_cat = jnp.concatenate([dq_send[j] for j in range(HEADS)], axis=1)
    dkv_cat = jnp.concatenate([dkv_red[j].astype(F32).T.astype(BF16) for j in range(HEADS)], axis=1)
    heads_t = jnp.concatenate([dq_cat, dkv_cat], axis=0)
    gw = mm(heads_t, nall[...].reshape(HEADS * ROWS, D)).astype(BF16)
    for q in range(F):
        gp[q // Gm, q % Gm] = gw[:, 128 * q : 128 * (q + 1)]
    g_sib = {k: send(gp.at[:, sib_idx[k] % Gm], gr1.at[k - 1], sib_dev[k]) for k in range(1, G)}
    tick()
    for k in range(1, G):
        g_sib[k].wait_recv()
    own = gp[:, g % Gm].astype(F32)
    for k in range(1, G):
        own = own + gr1[k - 1].astype(F32)
    gs[...] = own.astype(BF16)
    if plan.S > 1:
        g_seq = send(gs, gr2, far)
    tick()

    arrived(dq_group, dq_recv)
    arrived(dkv_group, dkv_recv)
    tick()
    lane = lax.broadcasted_iota(jnp.int32, (ROWS, 128), 1)
    left = lane < 64
    cols = [[], []]
    for i in range(HEADS // 2):
        a = dkv_recv[2 * i].astype(F32)
        b = dkv_recv[2 * i + 1].astype(F32)
        cols[0].append(jnp.where(left, a, pltpu.roll(b, 64, 1)))
        cols[1].append(jnp.where(left, pltpu.roll(a, 64, 1), b))
    kv_cols = jnp.concatenate(cols[0] + cols[1], axis=1).astype(BF16)
    grad_normed = mm(kv_cols, wq[:, D:], 1, 1) + mm(dq_recv[...].reshape(D, ROWS), wq[:, :D], 0, 1)
    n_one, r_one = row_norm(tok[h].astype(F32))
    scatter_row(v1, 0, jnp.sum(grad_normed * n_one, axis=0, keepdims=True))
    scatter_row(v1, 1, jnp.sum(grad_normed, axis=0, keepdims=True))
    v1_sib = {k: send(v1, v1r.at[k - 1], sib_dev[k]) for k in range(1, G)}
    e1 = grad_normed * gain1
    out_dx[...] = mid[...] + r_one * (
        e1 - jnp.mean(e1, axis=1, keepdims=True) - n_one * jnp.mean(e1 * n_one, axis=1, keepdims=True))
    tick()
    for k in range(1, G):
        v1_sib[k].wait_recv()
    acc1 = v1[...]
    for k in range(1, G):
        acc1 = acc1 + v1r[k - 1]
    v1s[...] = acc1
    if plan.S > 1:
        v1_seq = send(v1s, v1r2, far)
    tick()
    if plan.S > 1:
        g_seq.wait_recv()
        gt[...] = (gs[...].astype(F32) + gr2[...].astype(F32)).astype(BF16)
    else:
        gt[...] = gs[...]
    gr[h] = gt[fs // Gm]
    g_in = {}
    for k in range(1, HEADS):
        there = (head_idx[k] * G + g) % F
        g_in[k] = send(gt.at[there // Gm], gr.at[h], head_dev[k])
        if k % 2 == 0:
            tick()
    if plan.S > 1:
        v1_seq.wait_recv()
        v1t[...] = v1s[...] + v1r2[...]
    else:
        v1t[...] = v1s[...]
    v1_in = {}
    for k in range(1, HEADS):
        there = (head_idx[k] * G + g) % F
        v1_in[k] = send(v1t.at[there], v1r3.at[h], head_dev[k])
    v1r3[h] = v1t[fs]
    step_parts(len(events) - LAST)

    for k in range(1, HEADS):
        g_in[k].wait_recv()
    for i in range(HEADS // 2):
        for part_no in range(3):
            lo, hi = 64 * part_no, 64 * (part_no + 1)
            x = jnp.concatenate([gr[2 * i, lo:hi, :], gr[2 * i + 1, lo:hi, :]], axis=0)
            out_dq[:, D * part_no + 128 * i : D * part_no + 128 * (i + 1)] = x.astype(F32).T
    step_parts(len(events))
    while not all(p.done for p in parts):
        for p in parts:
            p.pump()
    out_v[...] = vacc[len(parts[-1].steps) - 1, fs]
    for k in range(1, HEADS):
        v1_in[k].wait_recv()
    out_v1[...] = jnp.sum(v1r3[...], axis=0)
    for copy in sent:
        copy.wait_send()
    for to, copy in posted:
        @pl.when(h != to)
        def _(copy=copy):
            copy.wait_send()


def layer(plan, lengths, vectors, tokens, cotangent, qkv_weight, out_weight, up_weight, down_weight):
    G, F, N = plan.G, plan.F, plan.N
    Gm = min(G, F)
    D = tokens.shape[1]
    FF = up_weight.shape[1]
    span = FF // F
    nv = 3 + len(plan.bits)
    shard = span + 4 * 128 + 128
    hbm = pl.BlockSpec(memory_space=pltpu.HBM)
    vm = pl.BlockSpec(memory_space=pltpu.VMEM)
    V = pltpu.VMEM
    sib = max(G - 1, 1)
    nsem = 192 + 8 * G
    heads = lambda: V((HEADS, HEAD_DIM, ROWS), BF16)
    scratch = [
        V((5, 1, 128), BF16), V((span // 128, 128), BF16), V((F, 16, 128), F32),
        V((HEADS, ROWS, D), BF16),
        V((D, 3 * D), BF16), V((D, D), BF16), V((D, FF), BF16), V((FF, D), BF16),
        V((3, HEADS, HEAD_DIM, ROWS), BF16),
        V((HEADS, G, 128, ROWS), BF16),
        V((N * ROWS, 128), BF16), V((128, N * ROWS), BF16),
        heads(), heads(), V((2, HEADS, HEAD_DIM, ROWS), BF16),
        V((HEADS // 2, HEAD_DIM, 2 * ROWS), F32), V((HEADS // 2, 1, 2 * ROWS), F32),
        heads(), heads(),
        V((N * ROWS, 128), F32),
        V((sib, HEADS, ROWS, 128), BF16), V((sib, HEADS, ROWS, 128), BF16),
        V((HEADS, ROWS, 128), BF16), V((HEADS, ROWS, 128), BF16),
        heads(), heads(),
        V((HEADS, ROWS, D), BF16),
        V((F // Gm, Gm, 192, 128), BF16), V((sib, F // Gm, 192, 128), BF16),
        V((F // Gm, 192, 128), BF16), V((F // Gm, 192, 128), BF16), V((F // Gm, 192, 128), BF16),
        V((HEADS, 192, 128), BF16),
        V((F, 8, 128), F32), V((sib, F, 8, 128), F32), V((F, 8, 128), F32), V((F, 8, 128), F32),
        V((F, 8, 128), F32), V((HEADS, 8, 128), F32),
        V((F, 8, 128), F32), V((nv, 4, F, 8, 128), F32), V((nv, F, 8, 128), F32),
        V((ROWS, D), F32),
        V((F, ROWS, span), F32), V((shard, D), BF16),
        V((2, 2, ROWS, span), BF16), V((2, ROWS, span), BF16),
        V((2, ROWS, D), BF16), V((2, ROWS, D), BF16), V((2, ROWS, FF), BF16), V((2, ROWS, D), BF16),
        V((2, shard, D), BF16),
        V((5 * shard // 2, D), BF16), V((5 * shard // 2, D), BF16),
        pltpu.SemaphoreType.DMA((16,)), pltpu.SemaphoreType.DMA((nsem,)), pltpu.SemaphoreType.DMA((nsem,)),
    ]
    S = jax.ShapeDtypeStruct
    return pl.pallas_call(
        partial(body, plan),
        out_shape=(S((ROWS, D), BF16), S((ROWS, D), F32), S((ROWS, 3 * D), F32),
                   S((span, D), F32), S((128, FF), F32), S((128, D), F32), S((8, 128), F32), S((8, 128), F32)),
        in_specs=[pl.BlockSpec(memory_space=pltpu.SMEM)] + [hbm] * 12,
        out_specs=(vm,) * 8,
        scratch_shapes=scratch,
        compiler_params=pltpu.CompilerParams(
            collective_id=0, has_side_effects=True, vmem_limit_bytes=(36 << 20) + 12 * N * ROWS * 128),
    )(lengths, *(pltpu.with_memory_space_constraint(x, pltpu.HBM) for x in (
        *vectors, tokens, cotangent, qkv_weight, out_weight, up_weight, down_weight)))


def finish(y, dx, dq, down, up, out, v, v1, o_y, o_dx, o_g1, o_b1, o_dq, o_out, o_g2, o_b2, o_up, o_ub, o_down, o_db,
           o_rms, sem):
    D = dx.shape[1]
    n = down.shape[0] // 128
    pairs = ((up, o_up), (down, o_down), (dq, o_dq), (dx, o_dx), (out, o_out), (y, o_y))
    copies = [pltpu.make_async_copy(src, dst, sem.at[i]) for i, (src, dst) in enumerate(pairs)]
    for copy in copies:
        copy.start()
    o_g1[...] = v1[0:1, :]
    o_b1[...] = v1[1:2, :]
    o_g2[...] = v[0:1, :]
    o_b2[...] = v[1:2, :]
    o_ub[...] = v[2 : 2 + n, :]
    o_db[...] = v[2 + n : 3 + n, :]
    stats = v[3 + n : 4 + n, :]
    o_rms[...] = jnp.sqrt(stats[:, 0:3] / (stats[:, 3:4] * D))
    for copy in copies:
        copy.wait()


def on_device(plan, tokens, lengths, ln1_gain, ln1_bias, qkv_weight, out_weight, ln2_gain, ln2_bias,
              up_weight, up_bias, down_weight, down_bias, cotangent):
    D = tokens.shape[1]
    F = plan.F
    span = up_weight.shape[1] // F
    vectors = [x.reshape(-1, 128) for x in (ln1_gain, ln1_bias, ln2_gain, ln2_bias, up_bias, down_bias)]
    results = layer(
        plan, lengths, vectors, tokens, cotangent, qkv_weight, out_weight, up_weight, down_weight)
    S = jax.ShapeDtypeStruct
    vec = S((1, 128), F32)
    vm = pl.BlockSpec(memory_space=pltpu.VMEM)
    hbm = pl.BlockSpec(memory_space=pltpu.HBM)
    outs = pl.pallas_call(
        finish,
        out_shape=(S((ROWS, D), BF16), S((ROWS, D), F32), vec, vec, S((ROWS, 3 * D), F32), S((128, D), F32),
                   vec, vec, S((128, F * span), F32), S((span // 128, 128), F32), S((span, D), F32), vec,
                   S((1, 3), F32)),
        in_specs=[vm] * 8,
        out_specs=(hbm, hbm, vm, vm, hbm, hbm, vm, vm, hbm, vm, hbm, vm, vm),
        scratch_shapes=[pltpu.SemaphoreType.DMA((6,))],
        compiler_params=pltpu.CompilerParams(vmem_limit_bytes=16 << 20),
    )(*results)
    outs = list(outs)
    for i in (2, 3, 6, 7, 9, 11, 12):
        outs[i] = outs[i].reshape(-1)
    return tuple(outs)


def solution(mesh):
    plan = Plan(mesh.shape["seq"], mesh.shape["ctx"], mesh.shape["fsdp"])
    rows = P(("seq", "ctx", "fsdp"), None)
    f1, f2 = P("fsdp"), P("fsdp", None)
    return jax.shard_map(
        partial(on_device, plan),
        mesh=mesh,
        in_specs=(rows, P("seq"), f1, f1, f2, f2, f1, f1, f2, f1, f2, f1, rows),
        out_specs=(rows, rows, f1, f1, f2, f2, f1, f1, f2, f1, f2, f1, P()),
        check_vma=False,
    )
```

```python
from functools import partial
import itertools

import jax
import jax.numpy as jnp
from jax import lax
from jax.experimental import pallas as pl
from jax.experimental.pallas import tpu as pltpu
from jax.sharding import PartitionSpec as P

HEADS = 8
HEAD_DIM = 64
EPS = 1e-05
NEG = -1e30
F32 = jnp.float32
BF16 = jnp.bfloat16
MESH = pl.DeviceIdType.MESH
ROWS = 128
KEYS = 512
KEYS_BACK = 512
LAST = 2
PARTS = [(0, 256, False, False), (256, 256, False, False), (512, 128, False, False), (640, 128, False, False), (768, 128, True, False), (896, 128, False, True), (1024, 128, False, False)]
EVENTS = [0, 1, 2, 3, 4, 5, 6, 0, 7, 7, 4, 1, 0, 2, 7, 1, 3, 0, 7, 2, 5, 1, 6, 2, 3, 4, 0, 5, 7, 3, 6, 4, 1, 2, 0, 6, 5, 3, 4, 1, 2, 0, 6, 5, 3, 4, 1, 2, 0, 6, 5, 3, 4, 6, 1, 2, 3, 4, 6]
TICKS = [1, 1, 4, 1, 1, 1, 3, 3, 0, 6, 8, 0, 5, 0, 5, 4, 0, 7, 3, 0, 0, 0]

ERF_TOP = (
    0.00022905065861350646,
    0.0034082910107109506,
    0.050955695062380861,
    0.18520832239976145,
    1.128379143519084,
)
ERF_LOW = (
    -1.1791602954361697e-7,
    0.000023547966471313185,
    0.0010179625278914885,
    0.014070470171167667,
    0.11098505178285362,
    0.49746925110067538,
    1.0,
)


def mm(a, b, ca=1, cb=0):
    return lax.dot_general(a, b, (((ca,), (cb,)), ((), ())), preferred_element_type=F32)


def erf(x):
    x = jnp.clip(x, -3.832506856900711, 3.832506856900711)
    s = x * x
    top = jnp.full_like(s, ERF_TOP[0])
    for c in ERF_TOP[1:]:
        top = top * s + c
    low = jnp.full_like(s, ERF_LOW[0])
    for c in ERF_LOW[1:]:
        low = low * s + c
    return x * top / low


def row_norm(x):
    center = jnp.mean(x, axis=1, keepdims=True)
    shifted = x - center
    spread = jnp.mean(shifted * shifted, axis=1, keepdims=True)
    r = lax.rsqrt(spread + EPS)
    return shifted * r, r


class Plan:
    def __init__(self, seqs, ctx, fsdp):
        self.S, self.C, self.F = seqs, ctx, fsdp
        self.N = ctx * fsdp
        self.G = self.N // HEADS
        self.bits = []
        b = 1
        while b < ctx:
            self.bits.append(b)
            b *= 2

    def split(self, dev):
        s, c, f = dev
        p = c * self.F + f
        return p // self.G, p % self.G

    def at(self, s, p):
        return (s, p // self.F, p % self.F)

    def head_peer(self, dev, k):
        h, g = self.split(dev)
        return self.at(dev[0], ((h + k) % HEADS) * self.G + g)

    def flip_peer(self, dev):
        h, g = self.split(dev)
        return self.at(dev[0], (h + 1 - 2 * (h % 2)) * self.G + g)

    def sibling(self, dev, k):
        h, g = self.split(dev)
        return self.at(dev[0], h * self.G + (g + k) % self.G)

    def fsdp_low(self, dev):
        s, c, f = dev
        return (s, c, f + 1 - 2 * (f % 2))

    def fsdp_high(self, dev):
        s, c, f = dev
        return (s, c, (f + 2) % self.F)

    def seq_peer(self, dev):
        s, c, f = dev
        return ((s + 1) % self.S, c, f)

    def ctx_peer(self, dev, b):
        s, c, f = dev
        return (s, c + b - 2 * b * ((c // b) % 2), f)

    def quad_peer(self, dev, b, k):
        s, c, f = dev
        return (s, (c // (4 * b)) * (4 * b) + ((c // b + k) % 4) * b + c % b, f)

    def greeted(self):
        base = [partial(self._head, k) for k in range(1, HEADS)]
        base += [partial(self._sib, k) for k in range(1, self.G)]
        base += [self.seq_peer]
        more = [self.fsdp_low, self.fsdp_high] + [partial(self._ctx, b) for b in self.bits]
        more += [partial(self._quad, b, k) for b in self.bits[:-1:2] for k in (1, 2, 3)]
        devs = list(itertools.product(range(self.S), range(self.C), range(self.F)))
        for extra in more:
            if not all(extra(d) in [p(d) for p in base] for d in devs):
                base.append(extra)
        return base

    def _head(self, k, dev):
        return self.head_peer(dev, k)

    def _sib(self, k, dev):
        return self.sibling(dev, k)

    def _quad(self, b, k, dev):
        return self.quad_peer(dev, b, k)

    def _ctx(self, b, dev):
        return self.ctx_peer(dev, b)


def body(plan, lens, g1_in, b1_in, g2_in, b2_in, ub_in, db_in, tok_in, cot_in, wq_in, wo_in, wu_in, wd_in,
         out_y, out_dx, out_dq, out_down, out_up, out_out, out_v, out_v1,
         raw, rawu, small, tok, wq, wo, wu, wd,
         msg, kvb, kvn, kvw, qb, o_send, at2, ot, lse, do_send, do_recv,
         dkv, dkvs, dkvr, dkv_red, dkv_recv, dq_send, dq_recv, nall,
         gp, gr1, gs, gr2, gt, gr,
         v1, v1r, v1s, v1r2, v1t, v1r3, v0, vrecv, vacc,
         mid, slope, out_r, actb, xa, c2, n2, g2, gb2, sa, into, sums, lsem, ssem, rsem):
    G, F, N = plan.G, plan.F, plan.N
    Gm = min(G, F)
    seq, ctx, fs = (lax.axis_index(a) for a in ("seq", "ctx", "fsdp"))
    me = (seq, ctx, fs)
    h, g = plan.split(me)
    fl, fh = fs % 2, fs // 2
    D = tok.shape[2]
    FF = wu.shape[1]
    span = FF // F
    valid = lens[0]
    counter = itertools.count()
    locals_ = itertools.count()

    def local(src, dst):
        copy = pltpu.make_async_copy(src, dst, lsem.at[next(locals_)])
        copy.start()
        return copy

    l_raw = [local(x, raw.at[i]) for i, x in enumerate((g1_in, b1_in, g2_in, b2_in, db_in))]
    l_raw.append(local(ub_in, rawu))
    l_tok = local(tok_in, tok.at[h])
    greet = plan.greeted()
    bar = pltpu.get_barrier_semaphore()
    for peer in greet:
        pl.semaphore_signal(bar, inc=1, device_id=peer(me), device_id_type=MESH)
    for copy in l_raw:
        copy.wait()
    own = [raw[i].astype(F32) for i in range(4)] + [rawu[...].astype(F32), raw[4].astype(F32)]
    used = 5 + span // 128
    small[fs] = jnp.concatenate(own + [jnp.zeros((16 - used, 128), F32)], axis=0)
    pl.semaphore_wait(bar, len(greet))

    sent = []

    def send(src, dst, dev):
        n = next(counter)
        copy = pltpu.make_async_remote_copy(
            src_ref=src, dst_ref=dst, send_sem=ssem.at[n], recv_sem=rsem.at[n],
            device_id=dev, device_id_type=MESH)
        copy.start()
        sent.append(copy)
        return copy

    posted = []

    def new_group():
        first = next(counter)
        for _ in range(HEADS - 1):
            next(counter)
        return first

    def post(group, to, src, dst):
        copy = pltpu.make_async_remote_copy(
            src_ref=src, dst_ref=dst, send_sem=ssem.at[group + to], recv_sem=rsem.at[group + h],
            device_id=plan.at(seq, to * G + g), device_id_type=MESH)

        @pl.when(h != to)
        def _():
            copy.start()

        posted.append((to, copy))

    def arrived(group, ref):
        for source in range(HEADS):
            copy = pltpu.make_async_remote_copy(
                src_ref=ref.at[source], dst_ref=ref.at[source], send_sem=ssem.at[group + source],
                recv_sem=rsem.at[group + source], device_id=plan.at(seq, source * G + g), device_id_type=MESH)

            @pl.when(h != source)
            def _():
                copy.wait_recv()

    low, high = plan.fsdp_low(me), plan.fsdp_high(me)
    fhigh = (fs + 2) % F
    head_dev = {k: plan.head_peer(me, k) for k in range(1, HEADS)}
    head_idx = {k: (h + k) % HEADS for k in range(1, HEADS)}
    sib_dev = {k: plan.sibling(me, k) for k in range(1, G)}
    sib_idx = {k: (g + k) % G for k in range(1, G)}

    far = plan.seq_peer(me)
    sm_low = send(small.at[fs], small.at[fs], low)
    sm_high = send(small.at[fs], small.at[fs], high)
    shards = ((wq_in, wq, 128), (wo_in, wo, 128), (wu_in, wu, 128), (wd_in, wd, span))

    def rows_of(w, first, count):
        return w.at[pl.ds(pl.multiple_of(first, count), count), :]

    def group_of(ref, which, c):
        return ref.at[pl.ds(pl.multiple_of(which * 128, 128), 128), c * D : (c + 1) * D]

    order = (1, 2, 0)
    q_high = {c: send(wq_in.at[:, c * D : (c + 1) * D], group_of(wq, fs, c), high) for c in order}
    q_low = {c: send(wq_in.at[:, c * D : (c + 1) * D], group_of(wq, fs, c), low) for c in order}
    half_rows = ROWS // 2

    def tokens_out(part):
        rows = slice(part * half_rows, (part + 1) * half_rows)
        return [send(tok_in.at[rows, :], tok.at[h, rows, :], head_dev[k]) for k in (2, 4, 6)]

    tok_copies = tokens_out(0)
    w_high, w_low = {}, {}
    for q in range(1, 4):
        src, dst, step = shards[q]
        w_low[q] = send(src, rows_of(dst, fs * step, step), low)
    l_w = [local(src, rows_of(dst, fs * step, step)) for src, dst, step in shards]
    l_cot = local(cot_in, c2.at[0])

    crossed, passed = {}, {}
    cuts = {1: 1, 2: 2, 3: 2}

    def slice_of(q, owner, p):
        count = shards[q][2] // (2 * cuts[q])
        first = (seq * cuts[q] + p) * count
        return count, first, owner * shards[q][2] + first

    def fetch(q):
        src, dst, step = shards[q]
        for p in range(cuts[q]):
            count, first, at = slice_of(q, fs, p)
            w_high[q, p] = send(rows_of(src, first, count), rows_of(dst, at, count), high)

    def cross(q, p):
        w_high[q, p].wait_recv()
        count, _, at = slice_of(q, fhigh, p)
        piece = rows_of(shards[q][1], at, count)
        crossed[q, p] = send(piece, piece, far)

    def hand_on(q):
        for p in range(cuts[q]):
            crossed[q, p].wait_recv()
        _, dst, step = shards[q]
        piece = rows_of(dst, fhigh * step, step)
        passed[q] = send(piece, piece, low)

    sm_low.wait_recv()
    sm_high.wait_recv()
    sm_fwd = send(small.at[fhigh], small.at[fhigh], low)
    l_tok.wait()
    inputs = tok[h].astype(F32)
    n_one, r_one = row_norm(inputs)
    sm_fwd.wait_recv()

    def vec(first, many=1):
        return jnp.concatenate(
            [small[q, first + r : first + r + 1, :] for q in range(F) for r in range(many)], axis=1)

    gain1, bias1, gain2, bias2 = vec(0), vec(1), vec(2), vec(3)
    down_bias = vec(4 + span // 128)
    normed = (n_one * gain1 + bias1).astype(BF16)
    nall[h] = normed
    l_w[0].wait()
    qkv_in = {}
    for c in order:
        q_low[c].wait_recv()
        q_high[c].wait_recv()
        piece = group_of(wq, fhigh, c)
        handed = send(piece, piece, low)
        handed.wait_recv()
        proj = mm(normed, wq[:, c * D : (c + 1) * D])
        if c == 0:
            proj = proj * (HEAD_DIM ** -0.5)
        msg[c] = proj.T.astype(BF16).reshape(HEADS, HEAD_DIM, ROWS)
        for k in range(1, HEADS):
            dst = qb.at[h] if c == 0 else kvb.at[h, g, (c - 1) * 64 : c * 64]
            qkv_in[c, k] = send(msg.at[c, head_idx[k]], dst, head_dev[k])
        if c == 0:
            qb[h] = msg[c, h]
        else:
            kvb[h, g, (c - 1) * 64 : c * 64] = msg[c, h]
    fetch(1)
    fetch(2)
    fetch(3)
    for c in (1, 2):
        for k in range(1, HEADS):
            qkv_in[c, k].wait_recv()
    tok_copies += tokens_out(1)
    kv_sib = {k: send(kvb.at[:, g], kvb.at[:, g], sib_dev[k]) for k in range(1, G)}

    def spread_block(hp, gg):
        at = pl.multiple_of((hp * G + gg) * ROWS, ROWS)
        block = kvb[hp, gg]
        kvw[:, pl.ds(at, ROWS)] = block
        kvn[pl.ds(at, ROWS), :] = block.astype(F32).T.astype(BF16)

    @pl.loop(0, HEADS)
    def _(hp):
        spread_block(hp, g)

    for k in range(1, G):
        kv_sib[k].wait_recv()
    for k in range(1, G):
        @pl.loop(0, HEADS)
        def _(hp, k=k):
            spread_block(hp, sib_idx[k])
    cross(1, 0)
    for k in range(1, HEADS):
        qkv_in[0, k].wait_recv()

    tiles = HEADS // 2

    def span_of(i, most):
        keys = (i + 1) * 2 * G * ROWS
        count = 1
        while keys % count or keys // count > most:
            count += 1
        return keys // count, count

    def over(count, step, start):
        return step(0, start) if count == 1 else lax.fori_loop(0, count, step, start)

    def keys_at(kc, size):
        return pl.ds(pl.multiple_of(kc * size, size), size) if not isinstance(kc, int) else slice(0, size)

    def key_iota(size):
        return lax.broadcasted_iota(jnp.int32, (size, 2 * ROWS), 0)

    def limits(i):
        col = lax.broadcasted_iota(jnp.int32, (1, 2 * ROWS), 1)
        pos = ((2 * i + col // ROWS) * G + g) * ROWS + col % ROWS
        return jnp.minimum(pos + 1, valid)

    nothing = jnp.zeros((HEAD_DIM, 2 * ROWS), BF16)

    def attend(i):
        qt = jnp.concatenate([qb[2 * i], qb[2 * i + 1]], axis=1)
        stacked = jnp.concatenate([qt, nothing], axis=0)
        limit = limits(i)

        size, count = span_of(i, KEYS)

        def step(kc, carry):
            at = keys_at(kc, size)
            st = mm(kvn[at, :], stacked)
            st = jnp.where(key_iota(size) < limit - kc * size, st, NEG)
            mn = jnp.max(st, axis=0, keepdims=True)
            if carry is not None:
                m, l, acc = carry
                mn = jnp.maximum(m, mn)
            e = jnp.exp(st - mn)
            total_e = jnp.sum(e, axis=0, keepdims=True)
            out = mm(kvw[64:128, at], e.astype(BF16))
            if carry is not None:
                al = jnp.exp(m - mn)
                total_e, out = l * al + total_e, acc * al + out
            return mn, total_e, out

        first = None if count == 1 else (
            jnp.full((1, 2 * ROWS), NEG, F32), jnp.zeros((1, 2 * ROWS), F32),
            jnp.zeros((HEAD_DIM, 2 * ROWS), F32))
        m, l, acc = over(count, step, first)
        o = acc / l
        ot[i] = o
        lse[i] = m + jnp.log(l)
        for p in range(2):
            o_send[2 * i + p] = o[:, p * ROWS : (p + 1) * ROWS].astype(BF16)
            post(o_group, 2 * i + p, o_send.at[2 * i + p], at2.at[0, h])

    o_group = new_group()
    for i in range(tiles):
        attend(i)
        if i == 1:
            cross(2, 0)
        if i == 2:
            cross(2, 1)
            hand_on(1)
    at2[0, h] = o_send[h]
    cross(3, 0)
    parity = h % 2
    flip = plan.flip_peer(me)
    for copy in tok_copies:
        copy.wait_recv()
    l_cot.wait()
    sib_c = send(c2.at[0], c2.at[1], low)
    tok4 = tok.reshape(HEADS // 2, 2, ROWS, D)
    tok_flip = send(tok4.at[:, parity], tok4.at[:, parity], flip)
    hand_on(2)
    cross(3, 1)
    arrived(o_group, at2.at[0])
    sib_at = send(at2.at[0], at2.at[1], low)

    def add_rows(dst, refs, rows):
        block = max(b for b in (16, 32, 64) if rows % b == 0)

        @pl.loop(0, rows // block)
        def _(t):
            at = pl.ds(pl.multiple_of(t * block, block), block)
            if len(refs) == 2:
                dst[at, :] = refs[0][at, :] + refs[1][at, :]
            else:
                x = refs[0][at, :].astype(F32)
                for ref in refs[1:]:
                    x = x + ref[at, :].astype(F32)
                dst[at, :] = x.astype(BF16)

    pool = {"into": 0, "sums": 0}

    def take(name, rows):
        first = pool[name]
        pool[name] += rows
        ref = {"into": into, "sums": sums}[name]
        return ref.at[pl.ds(first, rows), :]

    class Part:
        def __init__(self, first, rows, y_first, quads):
            self.first, self.rows = first, rows
            self.off, self.n = first, rows
            self.pair = sa.at[:, pl.ds(first, rows), :]
            self.piece = None
            x = ("cut", [far], 2, seq)
            y = ("pick", [high], 2, fh)
            self.steps = [y, x] if y_first else [x, y]
            n, bits = rows // 2, list(plan.bits)
            while bits:
                b = bits[0]
                if quads and len(bits) > 1 and n % 64 == 0:
                    peers = [plan.quad_peer(me, b, k) for k in (1, 2, 3)]
                    self.steps.append(("cut", peers, 4, (ctx // b) % 4))
                    bits, n = bits[2:], n // 4
                else:
                    kind = "cut" if n % 32 == 0 else "whole"
                    self.steps.append((kind, [plan.ctx_peer(me, b)], 2, (ctx // b) % 2))
                    bits, n = bits[1:], n // 2 if kind == "cut" else n
            self.trail = []
            self.t = -1
            self.done = False

        def pump(self):
            if self.done:
                return
            if self.t >= 0:
                for copy in self.copies:
                    copy.wait_recv()
                if self.t < len(self.steps):
                    self.finish()
                else:
                    self.off, self.n = self.region
            self.t += 1
            if self.t < len(self.steps):
                self.begin()
            elif self.trail:
                peers, off, n = self.trail.pop()
                region = out_r.at[pl.ds(pl.multiple_of(self.off, 16), self.n), :]
                self.copies = [send(region, region, dev) for dev in peers]
                self.region = off, n
            else:
                self.done = True
                self.store()

        def store(self):
            for row in range(self.first, self.first + self.rows, 128):
                x = out_r[row : row + 128, :].astype(F32)
                if row < span:
                    out_down[row : row + 128, :] = x
                elif row < span + 512:
                    q = (row - span) // 128
                    out_up[:, q * span : (q + 1) * span] = x
                else:
                    out_out[...] = x

        def slot(self, ref, which, size):
            return ref.at[pl.ds(pl.multiple_of(which * size, 16), size), :]

        def begin(self):
            kind, peers, ways, mine = self.steps[self.t]
            self.size = self.n // ways if kind == "cut" else self.n
            self.got, self.copies = [], []
            for k, dev in enumerate(peers):
                there = (mine + k + 1) % ways
                if self.piece is None and kind == "cut":
                    got = take("into", 2 * self.size).reshape(2, self.size, D)
                    src = self.pair.at[:, pl.ds(pl.multiple_of(there * self.size, 16), self.size), :]
                else:
                    got = take("into", self.size)
                    if kind == "pick":
                        src = self.pair.at[there]
                    elif kind == "cut":
                        src = self.slot(self.piece, there, self.size)
                    else:
                        src = self.piece
                self.got.append(got)
                self.copies.append(send(src, got, dev))

        def finish(self):
            kind, peers, ways, mine = self.steps[self.t]
            size = self.size
            if kind == "cut":
                self.trail.append((peers, self.off, self.n))
                self.off = self.off + mine * size
            if self.piece is None and kind == "cut":
                dst = take("sums", 2 * size).reshape(2, size, D)
                for y in range(2):
                    add_rows(dst.at[y], [self.slot(self.pair.at[y], mine, size)] + [got.at[y] for got in self.got], size)
                self.pair = dst
            else:
                if self.t + 1 == len(self.steps):
                    dst = out_r.at[pl.ds(pl.multiple_of(self.off, 16), size), :]
                else:
                    dst = take("sums", size)
                if kind == "pick":
                    own = self.pair.at[mine]
                elif kind == "cut":
                    own = self.slot(self.piece, mine, size)
                else:
                    own = self.piece
                add_rows(dst, [own] + self.got, size)
                self.piece = dst
            self.n = size

    class Vectors:
        def __init__(self):
            self.steps = [([p], 2, None) for p in (low, high)]
            bits = list(plan.bits)
            while bits:
                b = bits[0]
                if len(bits) > 1:
                    self.steps.append(([plan.quad_peer(me, b, k) for k in (1, 2, 3)], 4, (ctx // b) % 4))
                    bits = bits[2:]
                else:
                    self.steps.append(([plan.ctx_peer(me, b)], 2, None))
                    bits = bits[1:]
            self.steps.append(([far], 2, None))
            self.t = -1
            self.done = False

        def begin(self, src):
            peers, ways, mine = self.steps[self.t]
            if ways == 2:
                self.copies = [send(src, vrecv.at[self.t, 0], peers[0])]
            else:
                vrecv[self.t, mine] = src[...]
                self.copies = [send(src, vrecv.at[self.t, mine], dev) for dev in peers]

        def pump(self):
            if self.done:
                return
            t = self.t
            if t < 0:
                self.t = 0
                self.begin(v0)
                return
            for copy in self.copies:
                copy.wait_recv()
            if self.steps[t][1] == 2:
                vacc[t] = (v0[...] if t == 0 else vacc[t - 1]) + vrecv[t, 0]
            else:
                vacc[t] = (vrecv[t, 0] + vrecv[t, 1]) + (vrecv[t, 2] + vrecv[t, 3])
            self.t += 1
            if self.t < len(self.steps):
                self.begin(vacc.at[t])
            else:
                self.done = True

    events, parts = [], []

    turns = iter(TICKS)

    def step_parts(count):
        for _ in range(min(count, len(events))):
            parts[events.pop(0)].pump()

    def tick():
        step_parts(next(turns))

    for q in range(1, 4):
        l_w[q].wait()
        w_low[q].wait_recv()
    passed[1].wait_recv()
    at_t = at2[0].reshape(D, ROWS)
    attention_out = mm(at_t, wo[...], 0, 0)
    middle = tok[h].astype(F32) + attention_out
    n_two, r_two = row_norm(middle)
    normed_two = (n_two * gain2 + bias2).astype(BF16)
    n2[0] = normed_two
    sib_n = send(n2.at[0], n2.at[1], low)
    passed[2].wait_recv()
    sib_a = []
    half = span // 2
    for p in range(2):
        mine = slice(p * half, (p + 1) * half)
        for q in range(F):
            rows = range(4 + p * half // 128, 4 + (p + 1) * half // 128)
            bias = jnp.concatenate([small[q, r : r + 1, :] for r in rows], axis=1)
            raised = mm(normed_two, wu[:, q * span + p * half : q * span + (p + 1) * half]) + bias
            cdf = 0.5 * (1.0 + erf(raised * (0.5 ** 0.5)))
            pdf = jnp.exp(-0.5 * raised * raised) * 0.3989422804014327
            actb[q // 2, q % 2, :, mine] = (raised * cdf).astype(BF16)
            slope[q, :, mine] = cdf + raised * pdf
        sib_a.append(send(actb.at[:, 1 - fl, :, mine], xa.at[:, :, mine], low))
    sib_c.wait_recv()
    both_c = c2[...].reshape(2 * ROWS, D)
    cots = c2[0]
    gnt = jnp.zeros((ROWS, D), F32)

    def back_block(step, gnt):
        q = (2 * fh + step) % F
        cols = pl.ds(pl.multiple_of(q * span, span), span)
        grad = (mm(cots, wd[cols, :], 1, 1) * slope[q]).astype(BF16)
        g2[0, :, cols] = grad
        return gnt + mm(grad, wu[:, cols], 1, 1)

    def share_blocks(y):
        cols = pl.ds(pl.multiple_of(y * 2 * span, 2 * span), 2 * span)
        return send(g2.at[0, :, cols], g2.at[1, :, cols], low)

    parts += [Part(*p) for p in PARTS]
    events += EVENTS
    for p in range(2):
        mine = slice(p * half, (p + 1) * half)
        sib_a[p].wait_recv()
        for y in range(2):
            a = jnp.concatenate([actb[y, fl, :, mine], xa[y, :, mine]], axis=0)
            sa[y, mine, :] = mm(a, both_c, 0, 0).astype(BF16)
        tick()
        gnt = back_block(p, gnt)
    sib_g = [share_blocks(fh)]
    hand_on(3)
    passed[3].wait_recv()
    for step in range(F // 2, F):
        gnt = back_block(step, gnt)
    sib_g.append(share_blocks(1 - fh))

    def scatter_row(ref, row, x):
        for q in range(F):
            ref[q, row : row + 1, :] = x[:, 128 * q : 128 * (q + 1)]

    grad_final = cots.astype(F32)
    e2 = gnt * gain2
    grad_middle = grad_final + r_two * (
        e2 - jnp.mean(e2, axis=1, keepdims=True) - n_two * jnp.mean(e2 * n_two, axis=1, keepdims=True))
    mid[...] = grad_middle
    gb = grad_middle.astype(BF16)
    gb2[0] = gb
    sib_b = send(gb2.at[0], gb2.at[1], low)
    ga = mm(wo[...], gb, 1, 1).astype(BF16)
    do_send[...] = ga.reshape(HEADS, HEAD_DIM, ROWS)
    do_in = {k: send(do_send.at[head_idx[k]], do_recv.at[h], head_dev[k]) for k in range(1, HEADS)}
    do_recv[h] = do_send[h]

    sib_n.wait_recv()
    for copy in sib_g:
        copy.wait_recv()
    for y in range(2):
        spot = pl.ds(pl.multiple_of((2 * y + fl) * 128, 128), 128)
        a = n2[:, :, spot].reshape(2 * ROWS, 128)
        for q in range(F):
            cols = slice(q * span, (q + 1) * span)
            sa[y, span + 128 * q : span + 128 * (q + 1), :] = mm(
                a, g2[:, :, cols].reshape(2 * ROWS, span), 0, 0).astype(BF16)
    tick()
    sib_at.wait_recv()
    sib_b.wait_recv()
    for y in range(2):
        x = jnp.zeros((128, D), F32)
        for p in range(2):
            rows = at2[p, pl.ds(pl.multiple_of((2 * y + fl) * 2, 2), 2)].reshape(128, ROWS)
            x = x + mm(rows, gb2[p])
        sa[y, span + 512 : span + 640, :] = x.astype(BF16)

    tick()

    feed_out = down_bias
    for q in range(F):
        cols = slice(q * span, (q + 1) * span)
        feed_out = feed_out + mm(actb[q // 2, q % 2], wd[cols, :])
        grad = g2[0, :, cols].astype(F32)
        v0[q, 2 : 2 + span // 128, :] = jnp.concatenate(
            [jnp.sum(grad[:, 128 * r : 128 * (r + 1)], axis=0, keepdims=True)
             for r in range(span // 128)], axis=0)
    final = middle + feed_out
    out_y[...] = final.astype(BF16)
    scatter_row(v0, 0, jnp.sum(gnt * n_two, axis=0, keepdims=True))
    scatter_row(v0, 1, jnp.sum(gnt, axis=0, keepdims=True))
    scatter_row(v0, 2 + span // 128, jnp.sum(grad_final, axis=0, keepdims=True))
    place = (ctx * F + fs) * ROWS
    row = lax.broadcasted_iota(jnp.int32, (ROWS, 1), 0) + place
    live = (row < valid).astype(F32)

    def total(x):
        return jnp.sum(jnp.sum(x, axis=1, keepdims=True) * live, axis=0, keepdims=True)

    lane1 = lax.broadcasted_iota(jnp.int32, (1, 128), 1)
    stats = jnp.where(lane1 == 0, total(final * final), 0.0)
    stats = jnp.where(lane1 == 1, total(attention_out * attention_out), stats)
    stats = jnp.where(lane1 == 2, total(feed_out * feed_out), stats)
    stats = jnp.where(lane1 == 3, jnp.sum(live, axis=0, keepdims=True), stats)
    for q in range(F):
        v0[q, 3 + span // 128 : 4 + span // 128, :] = stats

    parts.append(Vectors())
    tick()
    tok_flip.wait_recv()

    @pl.loop(0, HEADS)
    def _(j):
        n, _ = row_norm(tok[j].astype(F32))
        nall[j] = (n * gain1 + bias1).astype(BF16)

    for k in range(1, HEADS):
        do_in[k].wait_recv()
    tick()

    dq_group, dkv_group = new_group(), new_group()
    dkv_sib = {}

    def attend_back(i):
        qt = jnp.concatenate([qb[2 * i], qb[2 * i + 1]], axis=1)
        dt = jnp.concatenate([do_recv[2 * i], do_recv[2 * i + 1]], axis=1)
        stacked = jnp.concatenate(
            [jnp.concatenate([qt, nothing], axis=1), jnp.concatenate([nothing, dt], axis=1)], axis=0)
        delta = jnp.sum(dt.astype(F32) * ot[i], axis=0, keepdims=True)
        level = lse[i]
        limit = limits(i)

        size, count = span_of(i, KEYS_BACK)

        def step(kc, acc):
            at = keys_at(kc, size)
            both = mm(kvn[at, :], stacked)
            st = jnp.where(key_iota(size) < limit - kc * size, both[:, : 2 * ROWS], NEG)
            p = jnp.exp(st - level)
            ds = (p * (both[:, 2 * ROWS :] - delta)).astype(BF16)
            pair = jnp.concatenate([ds, p.astype(BF16)], axis=1)
            more = mm(pair, stacked, 1, 1)
            if i == tiles - 1:
                dkv[at, :] = more
            else:
                dkv[at, :] += more
            out = mm(kvw[0:64, at], ds)
            return out if acc is None else acc + out

        acc = over(count, step, None if count == 1 else jnp.zeros((HEAD_DIM, 2 * ROWS), F32))
        low_dq = (acc.astype(BF16).astype(F32) * (HEAD_DIM ** -0.5)).astype(BF16)
        for p in range(2):
            j = 2 * i + p
            dq_send[j] = low_dq[:, p * ROWS : (p + 1) * ROWS]
            post(dq_group, j, dq_send.at[j], dq_recv.at[h])
            for k in range(1, G):
                spot = pl.multiple_of((j * G + sib_idx[k]) * ROWS, ROWS)
                dkvs[k - 1, j] = dkv[pl.ds(spot, ROWS), :].astype(BF16)
        for k in range(1, G):
            pairs = slice(2 * i, 2 * i + 2)
            dkv_sib[i, k] = send(dkvs.at[k - 1, pairs], dkvr.at[k - 1, pairs], sib_dev[k])

    def give_back(i):
        for k in range(1, G):
            dkv_sib[i, k].wait_recv()
        for j in (2 * i, 2 * i + 1):
            x = dkv[pl.ds(pl.multiple_of((j * G + g) * ROWS, ROWS), ROWS), :]
            for k in range(1, G):
                x = x + dkvr[k - 1, j].astype(F32)
            dkv_red[j] = x.astype(BF16)
            post(dkv_group, j, dkv_red.at[j], dkv_recv.at[h])

    for i in reversed(range(tiles)):
        attend_back(i)
        if i < tiles - 1:
            give_back(i + 1)
        tick()
    give_back(0)
    dq_recv[h] = dq_send[h]
    dkv_recv[h] = dkv_red[h]
    tick()

    dq_cat = jnp.concatenate([dq_send[j] for j in range(HEADS)], axis=1)
    dkv_cat = jnp.concatenate([dkv_red[j].astype(F32).T.astype(BF16) for j in range(HEADS)], axis=1)
    heads_t = jnp.concatenate([dq_cat, dkv_cat], axis=0)
    gw = mm(heads_t, nall[...].reshape(HEADS * ROWS, D)).astype(BF16)
    for q in range(F):
        gp[q // Gm, q % Gm] = gw[:, 128 * q : 128 * (q + 1)]
    g_sib = {k: send(gp.at[:, sib_idx[k] % Gm], gr1.at[k - 1], sib_dev[k]) for k in range(1, G)}
    tick()
    for k in range(1, G):
        g_sib[k].wait_recv()
    own = gp[:, g % Gm].astype(F32)
    for k in range(1, G):
        own = own + gr1[k - 1].astype(F32)
    gs[...] = own.astype(BF16)
    if plan.S > 1:
        g_seq = send(gs, gr2, far)
    tick()

    arrived(dq_group, dq_recv)
    arrived(dkv_group, dkv_recv)
    tick()
    lane = lax.broadcasted_iota(jnp.int32, (ROWS, 128), 1)
    left = lane < 64
    cols = [[], []]
    for i in range(HEADS // 2):
        a = dkv_recv[2 * i].astype(F32)
        b = dkv_recv[2 * i + 1].astype(F32)
        cols[0].append(jnp.where(left, a, pltpu.roll(b, 64, 1)))
        cols[1].append(jnp.where(left, pltpu.roll(a, 64, 1), b))
    kv_cols = jnp.concatenate(cols[0] + cols[1], axis=1).astype(BF16)
    grad_normed = mm(kv_cols, wq[:, D:], 1, 1) + mm(dq_recv[...].reshape(D, ROWS), wq[:, :D], 0, 1)
    n_one, r_one = row_norm(tok[h].astype(F32))
    scatter_row(v1, 0, jnp.sum(grad_normed * n_one, axis=0, keepdims=True))
    scatter_row(v1, 1, jnp.sum(grad_normed, axis=0, keepdims=True))
    v1_sib = {k: send(v1, v1r.at[k - 1], sib_dev[k]) for k in range(1, G)}
    e1 = grad_normed * gain1
    out_dx[...] = mid[...] + r_one * (
        e1 - jnp.mean(e1, axis=1, keepdims=True) - n_one * jnp.mean(e1 * n_one, axis=1, keepdims=True))
    tick()
    for k in range(1, G):
        v1_sib[k].wait_recv()
    acc1 = v1[...]
    for k in range(1, G):
        acc1 = acc1 + v1r[k - 1]
    v1s[...] = acc1
    if plan.S > 1:
        v1_seq = send(v1s, v1r2, far)
    tick()
    if plan.S > 1:
        g_seq.wait_recv()
        gt[...] = (gs[...].astype(F32) + gr2[...].astype(F32)).astype(BF16)
    else:
        gt[...] = gs[...]
    gr[h] = gt[fs // Gm]
    g_in = {}
    for k in range(1, HEADS):
        there = (head_idx[k] * G + g) % F
        g_in[k] = send(gt.at[there // Gm], gr.at[h], head_dev[k])
        if k % 2 == 0:
            tick()
    if plan.S > 1:
        v1_seq.wait_recv()
        v1t[...] = v1s[...] + v1r2[...]
    else:
        v1t[...] = v1s[...]
    v1_in = {}
    for k in range(1, HEADS):
        there = (head_idx[k] * G + g) % F
        v1_in[k] = send(v1t.at[there], v1r3.at[h], head_dev[k])
    v1r3[h] = v1t[fs]
    step_parts(len(events) - LAST)

    for k in range(1, HEADS):
        g_in[k].wait_recv()
    for i in range(HEADS // 2):
        for part_no in range(3):
            lo, hi = 64 * part_no, 64 * (part_no + 1)
            x = jnp.concatenate([gr[2 * i, lo:hi, :], gr[2 * i + 1, lo:hi, :]], axis=0)
            out_dq[:, D * part_no + 128 * i : D * part_no + 128 * (i + 1)] = x.astype(F32).T
    step_parts(len(events))
    while not all(p.done for p in parts):
        for p in parts:
            p.pump()
    out_v[...] = vacc[len(parts[-1].steps) - 1, fs]
    for k in range(1, HEADS):
        v1_in[k].wait_recv()
    out_v1[...] = jnp.sum(v1r3[...], axis=0)
    for copy in sent:
        copy.wait_send()
    for to, copy in posted:
        @pl.when(h != to)
        def _(copy=copy):
            copy.wait_send()


def layer(plan, lengths, vectors, tokens, cotangent, qkv_weight, out_weight, up_weight, down_weight):
    G, F, N = plan.G, plan.F, plan.N
    Gm = min(G, F)
    D = tokens.shape[1]
    FF = up_weight.shape[1]
    span = FF // F
    nv = 3 + len(plan.bits)
    shard = span + 4 * 128 + 128
    hbm = pl.BlockSpec(memory_space=pltpu.HBM)
    vm = pl.BlockSpec(memory_space=pltpu.VMEM)
    V = pltpu.VMEM
    sib = max(G - 1, 1)
    nsem = 192 + 8 * G
    heads = lambda: V((HEADS, HEAD_DIM, ROWS), BF16)
    scratch = [
        V((5, 1, 128), BF16), V((span // 128, 128), BF16), V((F, 16, 128), F32),
        V((HEADS, ROWS, D), BF16),
        V((D, 3 * D), BF16), V((D, D), BF16), V((D, FF), BF16), V((FF, D), BF16),
        V((3, HEADS, HEAD_DIM, ROWS), BF16),
        V((HEADS, G, 128, ROWS), BF16),
        V((N * ROWS, 128), BF16), V((128, N * ROWS), BF16),
        heads(), heads(), V((2, HEADS, HEAD_DIM, ROWS), BF16),
        V((HEADS // 2, HEAD_DIM, 2 * ROWS), F32), V((HEADS // 2, 1, 2 * ROWS), F32),
        heads(), heads(),
        V((N * ROWS, 128), F32),
        V((sib, HEADS, ROWS, 128), BF16), V((sib, HEADS, ROWS, 128), BF16),
        V((HEADS, ROWS, 128), BF16), V((HEADS, ROWS, 128), BF16),
        heads(), heads(),
        V((HEADS, ROWS, D), BF16),
        V((F // Gm, Gm, 192, 128), BF16), V((sib, F // Gm, 192, 128), BF16),
        V((F // Gm, 192, 128), BF16), V((F // Gm, 192, 128), BF16), V((F // Gm, 192, 128), BF16),
        V((HEADS, 192, 128), BF16),
        V((F, 8, 128), F32), V((sib, F, 8, 128), F32), V((F, 8, 128), F32), V((F, 8, 128), F32),
        V((F, 8, 128), F32), V((HEADS, 8, 128), F32),
        V((F, 8, 128), F32), V((nv, 4, F, 8, 128), F32), V((nv, F, 8, 128), F32),
        V((ROWS, D), F32),
        V((F, ROWS, span), F32), V((shard, D), BF16),
        V((2, 2, ROWS, span), BF16), V((2, ROWS, span), BF16),
        V((2, ROWS, D), BF16), V((2, ROWS, D), BF16), V((2, ROWS, FF), BF16), V((2, ROWS, D), BF16),
        V((2, shard, D), BF16),
        V((5 * shard // 2, D), BF16), V((5 * shard // 2, D), BF16),
        pltpu.SemaphoreType.DMA((16,)), pltpu.SemaphoreType.DMA((nsem,)), pltpu.SemaphoreType.DMA((nsem,)),
    ]
    S = jax.ShapeDtypeStruct
    return pl.pallas_call(
        partial(body, plan),
        out_shape=(S((ROWS, D), BF16), S((ROWS, D), F32), S((ROWS, 3 * D), F32),
                   S((span, D), F32), S((128, FF), F32), S((128, D), F32), S((8, 128), F32), S((8, 128), F32)),
        in_specs=[pl.BlockSpec(memory_space=pltpu.SMEM)] + [hbm] * 12,
        out_specs=(vm,) * 8,
        scratch_shapes=scratch,
        compiler_params=pltpu.CompilerParams(
            collective_id=0, has_side_effects=True, vmem_limit_bytes=(36 << 20) + 12 * N * ROWS * 128),
    )(lengths, *(pltpu.with_memory_space_constraint(x, pltpu.HBM) for x in (
        *vectors, tokens, cotangent, qkv_weight, out_weight, up_weight, down_weight)))


def finish(y, dx, dq, down, up, out, v, v1, o_y, o_dx, o_g1, o_b1, o_dq, o_out, o_g2, o_b2, o_up, o_ub, o_down, o_db,
           o_rms, sem):
    D = dx.shape[1]
    n = down.shape[0] // 128
    pairs = ((up, o_up), (down, o_down), (dq, o_dq), (dx, o_dx), (out, o_out), (y, o_y))
    copies = [pltpu.make_async_copy(src, dst, sem.at[i]) for i, (src, dst) in enumerate(pairs)]
    for copy in copies:
        copy.start()
    o_g1[...] = v1[0:1, :]
    o_b1[...] = v1[1:2, :]
    o_g2[...] = v[0:1, :]
    o_b2[...] = v[1:2, :]
    o_ub[...] = v[2 : 2 + n, :]
    o_db[...] = v[2 + n : 3 + n, :]
    stats = v[3 + n : 4 + n, :]
    o_rms[...] = jnp.sqrt(stats[:, 0:3] / (stats[:, 3:4] * D))
    for copy in copies:
        copy.wait()


def on_device(plan, tokens, lengths, ln1_gain, ln1_bias, qkv_weight, out_weight, ln2_gain, ln2_bias,
              up_weight, up_bias, down_weight, down_bias, cotangent):
    D = tokens.shape[1]
    F = plan.F
    span = up_weight.shape[1] // F
    vectors = [x.reshape(-1, 128) for x in (ln1_gain, ln1_bias, ln2_gain, ln2_bias, up_bias, down_bias)]
    results = layer(
        plan, lengths, vectors, tokens, cotangent, qkv_weight, out_weight, up_weight, down_weight)
    S = jax.ShapeDtypeStruct
    vec = S((1, 128), F32)
    vm = pl.BlockSpec(memory_space=pltpu.VMEM)
    hbm = pl.BlockSpec(memory_space=pltpu.HBM)
    outs = pl.pallas_call(
        finish,
        out_shape=(S((ROWS, D), BF16), S((ROWS, D), F32), vec, vec, S((ROWS, 3 * D), F32), S((128, D), F32),
                   vec, vec, S((128, F * span), F32), S((span // 128, 128), F32), S((span, D), F32), vec,
                   S((1, 3), F32)),
        in_specs=[vm] * 8,
        out_specs=(hbm, hbm, vm, vm, hbm, hbm, vm, vm, hbm, vm, hbm, vm, vm),
        scratch_shapes=[pltpu.SemaphoreType.DMA((6,))],
        compiler_params=pltpu.CompilerParams(vmem_limit_bytes=16 << 20),
    )(*results)
    outs = list(outs)
    for i in (2, 3, 6, 7, 9, 11, 12):
        outs[i] = outs[i].reshape(-1)
    return tuple(outs)


def solution(mesh):
    plan = Plan(mesh.shape["seq"], mesh.shape["ctx"], mesh.shape["fsdp"])
    rows = P(("seq", "ctx", "fsdp"), None)
    f1, f2 = P("fsdp"), P("fsdp", None)
    return jax.shard_map(
        partial(on_device, plan),
        mesh=mesh,
        in_specs=(rows, P("seq"), f1, f1, f2, f2, f1, f1, f2, f1, f2, f1, rows),
        out_specs=(rows, rows, f1, f1, f2, f2, f1, f1, f2, f1, f2, f1, P()),
        check_vma=False,
    )
```

```python
from functools import partial
import itertools

import jax
import jax.numpy as jnp
from jax import lax
from jax.experimental import pallas as pl
from jax.experimental.pallas import tpu as pltpu
from jax.sharding import PartitionSpec as P

HEADS = 8
HEAD_DIM = 64
EPS = 1e-05
NEG = -1e30
F32 = jnp.float32
BF16 = jnp.bfloat16
MESH = pl.DeviceIdType.MESH
ROWS = 128
KEYS = 512
KEYS_BACK = 512
LAST = 3
PARTS = [(0, 256, False, False), (256, 256, False, False), (512, 128, False, False), (640, 128, False, False), (768, 128, True, False), (896, 128, False, True), (1024, 128, False, False)]
EVENTS = [0, 1, 2, 3, 4, 5, 6, 0, 7, 7, 4, 1, 0, 2, 7, 1, 3, 0, 7, 2, 5, 1, 6, 2, 3, 4, 0, 5, 7, 3, 6, 4, 1, 2, 0, 6, 5, 3, 4, 1, 2, 0, 6, 5, 3, 4, 1, 2, 0, 6, 5, 3, 4, 6, 1, 2, 3, 4, 6]
TICKS = [1, 1, 4, 1, 1, 1, 3, 3, 0, 6, 8, 0, 5, 0, 5, 4, 0, 7, 3, 0, 0, 0]

ERF_TOP = (
    0.00022905065861350646,
    0.0034082910107109506,
    0.050955695062380861,
    0.18520832239976145,
    1.128379143519084,
)
ERF_LOW = (
    -1.1791602954361697e-7,
    0.000023547966471313185,
    0.0010179625278914885,
    0.014070470171167667,
    0.11098505178285362,
    0.49746925110067538,
    1.0,
)


def mm(a, b, ca=1, cb=0):
    return lax.dot_general(a, b, (((ca,), (cb,)), ((), ())), preferred_element_type=F32)


def erf(x):
    x = jnp.clip(x, -3.832506856900711, 3.832506856900711)
    s = x * x
    top = jnp.full_like(s, ERF_TOP[0])
    for c in ERF_TOP[1:]:
        top = top * s + c
    low = jnp.full_like(s, ERF_LOW[0])
    for c in ERF_LOW[1:]:
        low = low * s + c
    return x * top / low


def row_norm(x):
    center = jnp.mean(x, axis=1, keepdims=True)
    shifted = x - center
    spread = jnp.mean(shifted * shifted, axis=1, keepdims=True)
    r = lax.rsqrt(spread + EPS)
    return shifted * r, r


class Plan:
    def __init__(self, seqs, ctx, fsdp):
        self.S, self.C, self.F = seqs, ctx, fsdp
        self.N = ctx * fsdp
        self.G = self.N // HEADS
        self.bits = []
        b = 1
        while b < ctx:
            self.bits.append(b)
            b *= 2

    def split(self, dev):
        s, c, f = dev
        p = c * self.F + f
        return p // self.G, p % self.G

    def at(self, s, p):
        return (s, p // self.F, p % self.F)

    def head_peer(self, dev, k):
        h, g = self.split(dev)
        return self.at(dev[0], ((h + k) % HEADS) * self.G + g)

    def flip_peer(self, dev):
        h, g = self.split(dev)
        return self.at(dev[0], (h + 1 - 2 * (h % 2)) * self.G + g)

    def sibling(self, dev, k):
        h, g = self.split(dev)
        return self.at(dev[0], h * self.G + (g + k) % self.G)

    def fsdp_low(self, dev):
        s, c, f = dev
        return (s, c, f + 1 - 2 * (f % 2))

    def fsdp_high(self, dev):
        s, c, f = dev
        return (s, c, (f + 2) % self.F)

    def seq_peer(self, dev):
        s, c, f = dev
        return ((s + 1) % self.S, c, f)

    def ctx_peer(self, dev, b):
        s, c, f = dev
        return (s, c + b - 2 * b * ((c // b) % 2), f)

    def quad_peer(self, dev, b, k):
        s, c, f = dev
        return (s, (c // (4 * b)) * (4 * b) + ((c // b + k) % 4) * b + c % b, f)

    def greeted(self):
        base = [partial(self._head, k) for k in range(1, HEADS)]
        base += [partial(self._sib, k) for k in range(1, self.G)]
        base += [self.seq_peer]
        more = [self.fsdp_low, self.fsdp_high] + [partial(self._ctx, b) for b in self.bits]
        more += [partial(self._quad, b, k) for b in self.bits[:-1:2] for k in (1, 2, 3)]
        devs = list(itertools.product(range(self.S), range(self.C), range(self.F)))
        for extra in more:
            if not all(extra(d) in [p(d) for p in base] for d in devs):
                base.append(extra)
        return base

    def _head(self, k, dev):
        return self.head_peer(dev, k)

    def _sib(self, k, dev):
        return self.sibling(dev, k)

    def _quad(self, b, k, dev):
        return self.quad_peer(dev, b, k)

    def _ctx(self, b, dev):
        return self.ctx_peer(dev, b)


def body(plan, lens, g1_in, b1_in, g2_in, b2_in, ub_in, db_in, tok_in, cot_in, wq_in, wo_in, wu_in, wd_in,
         out_y, out_dx, out_dq, out_down, out_up, out_out, out_v, out_v1,
         raw, rawu, small, tok, wq, wo, wu, wd,
         msg, kvb, kvn, kvw, qb, o_send, at2, ot, lse, do_send, do_recv,
         dkv, dkvs, dkvr, dkv_red, dkv_recv, dq_send, dq_recv, nall,
         gp, gr1, gs, gr2, gt, gr,
         v1, v1r, v1s, v1r2, v1t, v1r3, v0, vrecv, vacc,
         mid, slope, out_r, actb, xa, c2, n2, g2, gb2, sa, into, sums, lsem, ssem, rsem):
    G, F, N = plan.G, plan.F, plan.N
    Gm = min(G, F)
    seq, ctx, fs = (lax.axis_index(a) for a in ("seq", "ctx", "fsdp"))
    me = (seq, ctx, fs)
    h, g = plan.split(me)
    fl, fh = fs % 2, fs // 2
    D = tok.shape[2]
    FF = wu.shape[1]
    span = FF // F
    valid = lens[0]
    counter = itertools.count()
    locals_ = itertools.count()

    def local(src, dst):
        copy = pltpu.make_async_copy(src, dst, lsem.at[next(locals_)])
        copy.start()
        return copy

    l_raw = [local(x, raw.at[i]) for i, x in enumerate((g1_in, b1_in, g2_in, b2_in, db_in))]
    l_raw.append(local(ub_in, rawu))
    l_tok = local(tok_in, tok.at[h])
    greet = plan.greeted()
    bar = pltpu.get_barrier_semaphore()
    for peer in greet:
        pl.semaphore_signal(bar, inc=1, device_id=peer(me), device_id_type=MESH)
    for copy in l_raw:
        copy.wait()
    own = [raw[i].astype(F32) for i in range(4)] + [rawu[...].astype(F32), raw[4].astype(F32)]
    used = 5 + span // 128
    small[fs] = jnp.concatenate(own + [jnp.zeros((16 - used, 128), F32)], axis=0)
    pl.semaphore_wait(bar, len(greet))

    sent = []

    def send(src, dst, dev):
        n = next(counter)
        copy = pltpu.make_async_remote_copy(
            src_ref=src, dst_ref=dst, send_sem=ssem.at[n], recv_sem=rsem.at[n],
            device_id=dev, device_id_type=MESH)
        copy.start()
        sent.append(copy)
        return copy

    posted = []

    def new_group():
        first = next(counter)
        for _ in range(HEADS - 1):
            next(counter)
        return first

    def post(group, to, src, dst):
        copy = pltpu.make_async_remote_copy(
            src_ref=src, dst_ref=dst, send_sem=ssem.at[group + to], recv_sem=rsem.at[group + h],
            device_id=plan.at(seq, to * G + g), device_id_type=MESH)

        @pl.when(h != to)
        def _():
            copy.start()

        posted.append((to, copy))

    def arrived(group, ref):
        for source in range(HEADS):
            copy = pltpu.make_async_remote_copy(
                src_ref=ref.at[source], dst_ref=ref.at[source], send_sem=ssem.at[group + source],
                recv_sem=rsem.at[group + source], device_id=plan.at(seq, source * G + g), device_id_type=MESH)

            @pl.when(h != source)
            def _():
                copy.wait_recv()

    low, high = plan.fsdp_low(me), plan.fsdp_high(me)
    fhigh = (fs + 2) % F
    head_dev = {k: plan.head_peer(me, k) for k in range(1, HEADS)}
    head_idx = {k: (h + k) % HEADS for k in range(1, HEADS)}
    sib_dev = {k: plan.sibling(me, k) for k in range(1, G)}
    sib_idx = {k: (g + k) % G for k in range(1, G)}

    far = plan.seq_peer(me)
    sm_low = send(small.at[fs], small.at[fs], low)
    sm_high = send(small.at[fs], small.at[fs], high)
    shards = ((wq_in, wq, 128), (wo_in, wo, 128), (wu_in, wu, 128), (wd_in, wd, span))

    def rows_of(w, first, count):
        return w.at[pl.ds(pl.multiple_of(first, count), count), :]

    def group_of(ref, which, c):
        return ref.at[pl.ds(pl.multiple_of(which * 128, 128), 128), c * D : (c + 1) * D]

    order = (1, 2, 0)
    q_high = {c: send(wq_in.at[:, c * D : (c + 1) * D], group_of(wq, fs, c), high) for c in order}
    q_low = {c: send(wq_in.at[:, c * D : (c + 1) * D], group_of(wq, fs, c), low) for c in order}
    half_rows = ROWS // 2

    def tokens_out(part):
        rows = slice(part * half_rows, (part + 1) * half_rows)
        return [send(tok_in.at[rows, :], tok.at[h, rows, :], head_dev[k]) for k in (2, 4, 6)]

    tok_copies = tokens_out(0)
    w_high, w_low = {}, {}
    for q in range(1, 4):
        src, dst, step = shards[q]
        w_low[q] = send(src, rows_of(dst, fs * step, step), low)
    l_w = [local(src, rows_of(dst, fs * step, step)) for src, dst, step in shards]
    l_cot = local(cot_in, c2.at[0])

    crossed, passed = {}, {}
    cuts = {1: 1, 2: 2, 3: 2}

    def slice_of(q, owner, p):
        count = shards[q][2] // (2 * cuts[q])
        first = (seq * cuts[q] + p) * count
        return count, first, owner * shards[q][2] + first

    def fetch(q):
        src, dst, step = shards[q]
        for p in range(cuts[q]):
            count, first, at = slice_of(q, fs, p)
            w_high[q, p] = send(rows_of(src, first, count), rows_of(dst, at, count), high)

    def cross(q, p):
        w_high[q, p].wait_recv()
        count, _, at = slice_of(q, fhigh, p)
        piece = rows_of(shards[q][1], at, count)
        crossed[q, p] = send(piece, piece, far)

    def hand_on(q):
        for p in range(cuts[q]):
            crossed[q, p].wait_recv()
        _, dst, step = shards[q]
        piece = rows_of(dst, fhigh * step, step)
        passed[q] = send(piece, piece, low)

    sm_low.wait_recv()
    sm_high.wait_recv()
    sm_fwd = send(small.at[fhigh], small.at[fhigh], low)
    l_tok.wait()
    inputs = tok[h].astype(F32)
    n_one, r_one = row_norm(inputs)
    sm_fwd.wait_recv()

    def vec(first, many=1):
        return jnp.concatenate(
            [small[q, first + r : first + r + 1, :] for q in range(F) for r in range(many)], axis=1)

    gain1, bias1, gain2, bias2 = vec(0), vec(1), vec(2), vec(3)
    down_bias = vec(4 + span // 128)
    normed = (n_one * gain1 + bias1).astype(BF16)
    nall[h] = normed
    l_w[0].wait()
    qkv_in = {}
    for c in order:
        q_low[c].wait_recv()
        q_high[c].wait_recv()
        piece = group_of(wq, fhigh, c)
        handed = send(piece, piece, low)
        handed.wait_recv()
        proj = mm(normed, wq[:, c * D : (c + 1) * D])
        if c == 0:
            proj = proj * (HEAD_DIM ** -0.5)
        msg[c] = proj.T.astype(BF16).reshape(HEADS, HEAD_DIM, ROWS)
        for k in range(1, HEADS):
            dst = qb.at[h] if c == 0 else kvb.at[h, g, (c - 1) * 64 : c * 64]
            qkv_in[c, k] = send(msg.at[c, head_idx[k]], dst, head_dev[k])
        if c == 0:
            qb[h] = msg[c, h]
        else:
            kvb[h, g, (c - 1) * 64 : c * 64] = msg[c, h]
    fetch(1)
    fetch(2)
    fetch(3)
    for c in (1, 2):
        for k in range(1, HEADS):
            qkv_in[c, k].wait_recv()
    tok_copies += tokens_out(1)
    kv_sib = {k: send(kvb.at[:, g], kvb.at[:, g], sib_dev[k]) for k in range(1, G)}

    def spread_block(hp, gg):
        at = pl.multiple_of((hp * G + gg) * ROWS, ROWS)
        block = kvb[hp, gg]
        kvw[:, pl.ds(at, ROWS)] = block
        kvn[pl.ds(at, ROWS), :] = block.astype(F32).T.astype(BF16)

    @pl.loop(0, HEADS)
    def _(hp):
        spread_block(hp, g)

    for k in range(1, G):
        kv_sib[k].wait_recv()
    for k in range(1, G):
        @pl.loop(0, HEADS)
        def _(hp, k=k):
            spread_block(hp, sib_idx[k])
    cross(1, 0)
    for k in range(1, HEADS):
        qkv_in[0, k].wait_recv()

    tiles = HEADS // 2

    def span_of(i, most):
        keys = (i + 1) * 2 * G * ROWS
        count = 1
        while keys % count or keys // count > most:
            count += 1
        return keys // count, count

    def over(count, step, start):
        return step(0, start) if count == 1 else lax.fori_loop(0, count, step, start)

    def keys_at(kc, size):
        return pl.ds(pl.multiple_of(kc * size, size), size) if not isinstance(kc, int) else slice(0, size)

    def key_iota(size):
        return lax.broadcasted_iota(jnp.int32, (size, 2 * ROWS), 0)

    def limits(i):
        col = lax.broadcasted_iota(jnp.int32, (1, 2 * ROWS), 1)
        pos = ((2 * i + col // ROWS) * G + g) * ROWS + col % ROWS
        return jnp.minimum(pos + 1, valid)

    nothing = jnp.zeros((HEAD_DIM, 2 * ROWS), BF16)

    def attend(i):
        qt = jnp.concatenate([qb[2 * i], qb[2 * i + 1]], axis=1)
        stacked = jnp.concatenate([qt, nothing], axis=0)
        limit = limits(i)

        size, count = span_of(i, KEYS)

        def step(kc, carry):
            at = keys_at(kc, size)
            st = mm(kvn[at, :], stacked)
            st = jnp.where(key_iota(size) < limit - kc * size, st, NEG)
            mn = jnp.max(st, axis=0, keepdims=True)
            if carry is not None:
                m, l, acc = carry
                mn = jnp.maximum(m, mn)
            e = jnp.exp(st - mn)
            total_e = jnp.sum(e, axis=0, keepdims=True)
            out = mm(kvw[64:128, at], e.astype(BF16))
            if carry is not None:
                al = jnp.exp(m - mn)
                total_e, out = l * al + total_e, acc * al + out
            return mn, total_e, out

        first = None if count == 1 else (
            jnp.full((1, 2 * ROWS), NEG, F32), jnp.zeros((1, 2 * ROWS), F32),
            jnp.zeros((HEAD_DIM, 2 * ROWS), F32))
        m, l, acc = over(count, step, first)
        o = acc / l
        ot[i] = o
        lse[i] = m + jnp.log(l)
        for p in range(2):
            o_send[2 * i + p] = o[:, p * ROWS : (p + 1) * ROWS].astype(BF16)
            post(o_group, 2 * i + p, o_send.at[2 * i + p], at2.at[0, h])

    o_group = new_group()
    for i in range(tiles):
        attend(i)
        if i == 1:
            cross(2, 0)
        if i == 2:
            cross(2, 1)
            hand_on(1)
    at2[0, h] = o_send[h]
    cross(3, 0)
    parity = h % 2
    flip = plan.flip_peer(me)
    for copy in tok_copies:
        copy.wait_recv()
    l_cot.wait()
    sib_c = send(c2.at[0], c2.at[1], low)
    tok4 = tok.reshape(HEADS // 2, 2, ROWS, D)
    tok_flip = send(tok4.at[:, parity], tok4.at[:, parity], flip)
    hand_on(2)
    cross(3, 1)
    arrived(o_group, at2.at[0])
    sib_at = send(at2.at[0], at2.at[1], low)

    def add_rows(dst, refs, rows):
        block = max(b for b in (16, 32, 64) if rows % b == 0)

        @pl.loop(0, rows // block)
        def _(t):
            at = pl.ds(pl.multiple_of(t * block, block), block)
            if len(refs) == 2:
                dst[at, :] = refs[0][at, :] + refs[1][at, :]
            else:
                x = refs[0][at, :].astype(F32)
                for ref in refs[1:]:
                    x = x + ref[at, :].astype(F32)
                dst[at, :] = x.astype(BF16)

    pool = {"into": 0, "sums": 0}

    def take(name, rows):
        first = pool[name]
        pool[name] += rows
        ref = {"into": into, "sums": sums}[name]
        return ref.at[pl.ds(first, rows), :]

    class Part:
        def __init__(self, first, rows, y_first, quads):
            self.first, self.rows = first, rows
            self.off, self.n = first, rows
            self.pair = sa.at[:, pl.ds(first, rows), :]
            self.piece = None
            x = ("cut", [far], 2, seq)
            y = ("pick", [high], 2, fh)
            self.steps = [y, x] if y_first else [x, y]
            n, bits = rows // 2, list(plan.bits)
            while bits:
                b = bits[0]
                if quads and len(bits) > 1 and n % 64 == 0:
                    peers = [plan.quad_peer(me, b, k) for k in (1, 2, 3)]
                    self.steps.append(("cut", peers, 4, (ctx // b) % 4))
                    bits, n = bits[2:], n // 4
                else:
                    kind = "cut" if n % 32 == 0 else "whole"
                    self.steps.append((kind, [plan.ctx_peer(me, b)], 2, (ctx // b) % 2))
                    bits, n = bits[1:], n // 2 if kind == "cut" else n
            self.trail = []
            self.t = -1
            self.done = False

        def pump(self):
            if self.done:
                return
            if self.t >= 0:
                for copy in self.copies:
                    copy.wait_recv()
                if self.t < len(self.steps):
                    self.finish()
                else:
                    self.off, self.n = self.region
            self.t += 1
            if self.t < len(self.steps):
                self.begin()
            elif self.trail:
                peers, off, n = self.trail.pop()
                region = out_r.at[pl.ds(pl.multiple_of(self.off, 16), self.n), :]
                self.copies = [send(region, region, dev) for dev in peers]
                self.region = off, n
            else:
                self.done = True
                self.store()

        def store(self):
            for row in range(self.first, self.first + self.rows, 128):
                x = out_r[row : row + 128, :].astype(F32)
                if row < span:
                    out_down[row : row + 128, :] = x
                elif row < span + 512:
                    q = (row - span) // 128
                    out_up[:, q * span : (q + 1) * span] = x
                else:
                    out_out[...] = x

        def slot(self, ref, which, size):
            return ref.at[pl.ds(pl.multiple_of(which * size, 16), size), :]

        def begin(self):
            kind, peers, ways, mine = self.steps[self.t]
            self.size = self.n // ways if kind == "cut" else self.n
            self.got, self.copies = [], []
            for k, dev in enumerate(peers):
                there = (mine + k + 1) % ways
                if self.piece is None and kind == "cut":
                    got = take("into", 2 * self.size).reshape(2, self.size, D)
                    src = self.pair.at[:, pl.ds(pl.multiple_of(there * self.size, 16), self.size), :]
                else:
                    got = take("into", self.size)
                    if kind == "pick":
                        src = self.pair.at[there]
                    elif kind == "cut":
                        src = self.slot(self.piece, there, self.size)
                    else:
                        src = self.piece
                self.got.append(got)
                self.copies.append(send(src, got, dev))

        def finish(self):
            kind, peers, ways, mine = self.steps[self.t]
            size = self.size
            if kind == "cut":
                self.trail.append((peers, self.off, self.n))
                self.off = self.off + mine * size
            if self.piece is None and kind == "cut":
                dst = take("sums", 2 * size).reshape(2, size, D)
                for y in range(2):
                    add_rows(dst.at[y], [self.slot(self.pair.at[y], mine, size)] + [got.at[y] for got in self.got], size)
                self.pair = dst
            else:
                if self.t + 1 == len(self.steps):
                    dst = out_r.at[pl.ds(pl.multiple_of(self.off, 16), size), :]
                else:
                    dst = take("sums", size)
                if kind == "pick":
                    own = self.pair.at[mine]
                elif kind == "cut":
                    own = self.slot(self.piece, mine, size)
                else:
                    own = self.piece
                add_rows(dst, [own] + self.got, size)
                self.piece = dst
            self.n = size

    class Vectors:
        def __init__(self):
            self.steps = [([p], 2, None) for p in (low, high)]
            bits = list(plan.bits)
            while bits:
                b = bits[0]
                if len(bits) > 1:
                    self.steps.append(([plan.quad_peer(me, b, k) for k in (1, 2, 3)], 4, (ctx // b) % 4))
                    bits = bits[2:]
                else:
                    self.steps.append(([plan.ctx_peer(me, b)], 2, None))
                    bits = bits[1:]
            self.steps.append(([far], 2, None))
            self.t = -1
            self.done = False

        def begin(self, src):
            peers, ways, mine = self.steps[self.t]
            if ways == 2:
                self.copies = [send(src, vrecv.at[self.t, 0], peers[0])]
            else:
                vrecv[self.t, mine] = src[...]
                self.copies = [send(src, vrecv.at[self.t, mine], dev) for dev in peers]

        def pump(self):
            if self.done:
                return
            t = self.t
            if t < 0:
                self.t = 0
                self.begin(v0)
                return
            for copy in self.copies:
                copy.wait_recv()
            if self.steps[t][1] == 2:
                vacc[t] = (v0[...] if t == 0 else vacc[t - 1]) + vrecv[t, 0]
            else:
                vacc[t] = (vrecv[t, 0] + vrecv[t, 1]) + (vrecv[t, 2] + vrecv[t, 3])
            self.t += 1
            if self.t < len(self.steps):
                self.begin(vacc.at[t])
            else:
                self.done = True

    events, parts = [], []

    turns = iter(TICKS)

    def step_parts(count):
        for _ in range(min(count, len(events))):
            parts[events.pop(0)].pump()

    def tick():
        step_parts(next(turns))

    for q in range(1, 4):
        l_w[q].wait()
        w_low[q].wait_recv()
    passed[1].wait_recv()
    at_t = at2[0].reshape(D, ROWS)
    attention_out = mm(at_t, wo[...], 0, 0)
    middle = tok[h].astype(F32) + attention_out
    n_two, r_two = row_norm(middle)
    normed_two = (n_two * gain2 + bias2).astype(BF16)
    n2[0] = normed_two
    sib_n = send(n2.at[0], n2.at[1], low)
    passed[2].wait_recv()
    sib_a = []
    half = span // 2
    for p in range(2):
        mine = slice(p * half, (p + 1) * half)
        for q in range(F):
            rows = range(4 + p * half // 128, 4 + (p + 1) * half // 128)
            bias = jnp.concatenate([small[q, r : r + 1, :] for r in rows], axis=1)
            raised = mm(normed_two, wu[:, q * span + p * half : q * span + (p + 1) * half]) + bias
            cdf = 0.5 * (1.0 + erf(raised * (0.5 ** 0.5)))
            pdf = jnp.exp(-0.5 * raised * raised) * 0.3989422804014327
            actb[q // 2, q % 2, :, mine] = (raised * cdf).astype(BF16)
            slope[q, :, mine] = cdf + raised * pdf
        sib_a.append(send(actb.at[:, 1 - fl, :, mine], xa.at[:, :, mine], low))
    sib_c.wait_recv()
    both_c = c2[...].reshape(2 * ROWS, D)
    cots = c2[0]
    gnt = jnp.zeros((ROWS, D), F32)

    def back_block(step, gnt):
        q = (2 * fh + step) % F
        cols = pl.ds(pl.multiple_of(q * span, span), span)
        grad = (mm(cots, wd[cols, :], 1, 1) * slope[q]).astype(BF16)
        g2[0, :, cols] = grad
        return gnt + mm(grad, wu[:, cols], 1, 1)

    def share_blocks(y):
        cols = pl.ds(pl.multiple_of(y * 2 * span, 2 * span), 2 * span)
        return send(g2.at[0, :, cols], g2.at[1, :, cols], low)

    parts += [Part(*p) for p in PARTS]
    events += EVENTS
    for p in range(2):
        mine = slice(p * half, (p + 1) * half)
        sib_a[p].wait_recv()
        for y in range(2):
            a = jnp.concatenate([actb[y, fl, :, mine], xa[y, :, mine]], axis=0)
            sa[y, mine, :] = mm(a, both_c, 0, 0).astype(BF16)
        tick()
        gnt = back_block(p, gnt)
    sib_g = [share_blocks(fh)]
    hand_on(3)
    passed[3].wait_recv()
    for step in range(F // 2, F):
        gnt = back_block(step, gnt)
    sib_g.append(share_blocks(1 - fh))

    def scatter_row(ref, row, x):
        for q in range(F):
            ref[q, row : row + 1, :] = x[:, 128 * q : 128 * (q + 1)]

    grad_final = cots.astype(F32)
    e2 = gnt * gain2
    grad_middle = grad_final + r_two * (
        e2 - jnp.mean(e2, axis=1, keepdims=True) - n_two * jnp.mean(e2 * n_two, axis=1, keepdims=True))
    mid[...] = grad_middle
    gb = grad_middle.astype(BF16)
    gb2[0] = gb
    sib_b = send(gb2.at[0], gb2.at[1], low)
    ga = mm(wo[...], gb, 1, 1).astype(BF16)
    do_send[...] = ga.reshape(HEADS, HEAD_DIM, ROWS)
    do_in = {k: send(do_send.at[head_idx[k]], do_recv.at[h], head_dev[k]) for k in (4, 3, 5, 2, 6, 1, 7)}
    do_recv[h] = do_send[h]

    sib_n.wait_recv()
    for copy in sib_g:
        copy.wait_recv()
    for y in range(2):
        spot = pl.ds(pl.multiple_of((2 * y + fl) * 128, 128), 128)
        a = n2[:, :, spot].reshape(2 * ROWS, 128)
        for q in range(F):
            cols = slice(q * span, (q + 1) * span)
            sa[y, span + 128 * q : span + 128 * (q + 1), :] = mm(
                a, g2[:, :, cols].reshape(2 * ROWS, span), 0, 0).astype(BF16)
    tick()
    sib_at.wait_recv()
    sib_b.wait_recv()
    for y in range(2):
        x = jnp.zeros((128, D), F32)
        for p in range(2):
            rows = at2[p, pl.ds(pl.multiple_of((2 * y + fl) * 2, 2), 2)].reshape(128, ROWS)
            x = x + mm(rows, gb2[p])
        sa[y, span + 512 : span + 640, :] = x.astype(BF16)

    tick()

    feed_out = down_bias
    for q in range(F):
        cols = slice(q * span, (q + 1) * span)
        feed_out = feed_out + mm(actb[q // 2, q % 2], wd[cols, :])
        grad = g2[0, :, cols].astype(F32)
        v0[q, 2 : 2 + span // 128, :] = jnp.concatenate(
            [jnp.sum(grad[:, 128 * r : 128 * (r + 1)], axis=0, keepdims=True)
             for r in range(span // 128)], axis=0)
    final = middle + feed_out
    out_y[...] = final.astype(BF16)
    scatter_row(v0, 0, jnp.sum(gnt * n_two, axis=0, keepdims=True))
    scatter_row(v0, 1, jnp.sum(gnt, axis=0, keepdims=True))
    scatter_row(v0, 2 + span // 128, jnp.sum(grad_final, axis=0, keepdims=True))
    place = (ctx * F + fs) * ROWS
    row = lax.broadcasted_iota(jnp.int32, (ROWS, 1), 0) + place
    live = (row < valid).astype(F32)

    def total(x):
        return jnp.sum(jnp.sum(x, axis=1, keepdims=True) * live, axis=0, keepdims=True)

    lane1 = lax.broadcasted_iota(jnp.int32, (1, 128), 1)
    stats = jnp.where(lane1 == 0, total(final * final), 0.0)
    stats = jnp.where(lane1 == 1, total(attention_out * attention_out), stats)
    stats = jnp.where(lane1 == 2, total(feed_out * feed_out), stats)
    stats = jnp.where(lane1 == 3, jnp.sum(live, axis=0, keepdims=True), stats)
    for q in range(F):
        v0[q, 3 + span // 128 : 4 + span // 128, :] = stats

    parts.append(Vectors())
    tick()
    tok_flip.wait_recv()

    @pl.loop(0, HEADS)
    def _(j):
        n, _ = row_norm(tok[j].astype(F32))
        nall[j] = (n * gain1 + bias1).astype(BF16)

    for k in range(1, HEADS):
        do_in[k].wait_recv()
    tick()

    dq_group, dkv_group = new_group(), new_group()
    dkv_sib = {}

    def attend_back(i):
        qt = jnp.concatenate([qb[2 * i], qb[2 * i + 1]], axis=1)
        dt = jnp.concatenate([do_recv[2 * i], do_recv[2 * i + 1]], axis=1)
        stacked = jnp.concatenate(
            [jnp.concatenate([qt, nothing], axis=1), jnp.concatenate([nothing, dt], axis=1)], axis=0)
        delta = jnp.sum(dt.astype(F32) * ot[i], axis=0, keepdims=True)
        level = lse[i]
        limit = limits(i)

        size, count = span_of(i, KEYS_BACK)

        def step(kc, acc):
            at = keys_at(kc, size)
            both = mm(kvn[at, :], stacked)
            st = jnp.where(key_iota(size) < limit - kc * size, both[:, : 2 * ROWS], NEG)
            p = jnp.exp(st - level)
            ds = (p * (both[:, 2 * ROWS :] - delta)).astype(BF16)
            pair = jnp.concatenate([ds, p.astype(BF16)], axis=1)
            more = mm(pair, stacked, 1, 1)
            if i == tiles - 1:
                dkv[at, :] = more
            else:
                dkv[at, :] += more
            out = mm(kvw[0:64, at], ds)
            return out if acc is None else acc + out

        acc = over(count, step, None if count == 1 else jnp.zeros((HEAD_DIM, 2 * ROWS), F32))
        low_dq = (acc.astype(BF16).astype(F32) * (HEAD_DIM ** -0.5)).astype(BF16)
        for p in range(2):
            j = 2 * i + p
            dq_send[j] = low_dq[:, p * ROWS : (p + 1) * ROWS]
            post(dq_group, j, dq_send.at[j], dq_recv.at[h])
            for k in range(1, G):
                spot = pl.multiple_of((j * G + sib_idx[k]) * ROWS, ROWS)
                dkvs[k - 1, j] = dkv[pl.ds(spot, ROWS), :].astype(BF16)
        for k in range(1, G):
            pairs = slice(2 * i, 2 * i + 2)
            dkv_sib[i, k] = send(dkvs.at[k - 1, pairs], dkvr.at[k - 1, pairs], sib_dev[k])

    def give_back(i):
        for k in range(1, G):
            dkv_sib[i, k].wait_recv()
        for j in (2 * i, 2 * i + 1):
            x = dkv[pl.ds(pl.multiple_of((j * G + g) * ROWS, ROWS), ROWS), :]
            for k in range(1, G):
                x = x + dkvr[k - 1, j].astype(F32)
            dkv_red[j] = x.astype(BF16)
            post(dkv_group, j, dkv_red.at[j], dkv_recv.at[h])

    for i in reversed(range(tiles)):
        attend_back(i)
        if i < tiles - 1:
            give_back(i + 1)
        tick()
    give_back(0)
    dq_recv[h] = dq_send[h]
    dkv_recv[h] = dkv_red[h]
    tick()

    dq_cat = jnp.concatenate([dq_send[j] for j in range(HEADS)], axis=1)
    dkv_cat = jnp.concatenate([dkv_red[j].astype(F32).T.astype(BF16) for j in range(HEADS)], axis=1)
    heads_t = jnp.concatenate([dq_cat, dkv_cat], axis=0)
    gw = mm(heads_t, nall[...].reshape(HEADS * ROWS, D)).astype(BF16)
    for q in range(F):
        gp[q // Gm, q % Gm] = gw[:, 128 * q : 128 * (q + 1)]
    g_sib = {k: send(gp.at[:, sib_idx[k] % Gm], gr1.at[k - 1], sib_dev[k]) for k in range(1, G)}
    tick()
    for k in range(1, G):
        g_sib[k].wait_recv()
    own = gp[:, g % Gm].astype(F32)
    for k in range(1, G):
        own = own + gr1[k - 1].astype(F32)
    gs[...] = own.astype(BF16)
    if plan.S > 1:
        g_seq = send(gs, gr2, far)
    tick()

    arrived(dq_group, dq_recv)
    arrived(dkv_group, dkv_recv)
    tick()
    lane = lax.broadcasted_iota(jnp.int32, (ROWS, 128), 1)
    left = lane < 64
    cols = [[], []]
    for i in range(HEADS // 2):
        a = dkv_recv[2 * i].astype(F32)
        b = dkv_recv[2 * i + 1].astype(F32)
        cols[0].append(jnp.where(left, a, pltpu.roll(b, 64, 1)))
        cols[1].append(jnp.where(left, pltpu.roll(a, 64, 1), b))
    kv_cols = jnp.concatenate(cols[0] + cols[1], axis=1).astype(BF16)
    grad_normed = mm(kv_cols, wq[:, D:], 1, 1) + mm(dq_recv[...].reshape(D, ROWS), wq[:, :D], 0, 1)
    n_one, r_one = row_norm(tok[h].astype(F32))
    scatter_row(v1, 0, jnp.sum(grad_normed * n_one, axis=0, keepdims=True))
    scatter_row(v1, 1, jnp.sum(grad_normed, axis=0, keepdims=True))
    v1_sib = {k: send(v1, v1r.at[k - 1], sib_dev[k]) for k in range(1, G)}
    e1 = grad_normed * gain1
    out_dx[...] = mid[...] + r_one * (
        e1 - jnp.mean(e1, axis=1, keepdims=True) - n_one * jnp.mean(e1 * n_one, axis=1, keepdims=True))
    tick()
    for k in range(1, G):
        v1_sib[k].wait_recv()
    acc1 = v1[...]
    for k in range(1, G):
        acc1 = acc1 + v1r[k - 1]
    v1s[...] = acc1
    if plan.S > 1:
        v1_seq = send(v1s, v1r2, far)
    tick()
    if plan.S > 1:
        g_seq.wait_recv()
        gt[...] = (gs[...].astype(F32) + gr2[...].astype(F32)).astype(BF16)
    else:
        gt[...] = gs[...]
    gr[h] = gt[fs // Gm]
    g_in = {}
    for k in range(1, HEADS):
        there = (head_idx[k] * G + g) % F
        g_in[k] = send(gt.at[there // Gm], gr.at[h], head_dev[k])
        if k % 2 == 0:
            tick()
    if plan.S > 1:
        v1_seq.wait_recv()
        v1t[...] = v1s[...] + v1r2[...]
    else:
        v1t[...] = v1s[...]
    v1_in = {}
    for k in range(1, HEADS):
        there = (head_idx[k] * G + g) % F
        v1_in[k] = send(v1t.at[there], v1r3.at[h], head_dev[k])
    v1r3[h] = v1t[fs]
    step_parts(len(events) - LAST)

    for k in range(1, HEADS):
        g_in[k].wait_recv()
    for i in range(HEADS // 2):
        for part_no in range(3):
            lo, hi = 64 * part_no, 64 * (part_no + 1)
            x = jnp.concatenate([gr[2 * i, lo:hi, :], gr[2 * i + 1, lo:hi, :]], axis=0)
            out_dq[:, D * part_no + 128 * i : D * part_no + 128 * (i + 1)] = x.astype(F32).T
    step_parts(len(events))
    while not all(p.done for p in parts):
        for p in parts:
            p.pump()
    out_v[...] = vacc[len(parts[-1].steps) - 1, fs]
    for k in range(1, HEADS):
        v1_in[k].wait_recv()
    out_v1[...] = jnp.sum(v1r3[...], axis=0)
    for copy in sent:
        copy.wait_send()
    for to, copy in posted:
        @pl.when(h != to)
        def _(copy=copy):
            copy.wait_send()


def layer(plan, lengths, vectors, tokens, cotangent, qkv_weight, out_weight, up_weight, down_weight):
    G, F, N = plan.G, plan.F, plan.N
    Gm = min(G, F)
    D = tokens.shape[1]
    FF = up_weight.shape[1]
    span = FF // F
    nv = 3 + len(plan.bits)
    shard = span + 4 * 128 + 128
    hbm = pl.BlockSpec(memory_space=pltpu.HBM)
    vm = pl.BlockSpec(memory_space=pltpu.VMEM)
    V = pltpu.VMEM
    sib = max(G - 1, 1)
    nsem = 192 + 8 * G
    heads = lambda: V((HEADS, HEAD_DIM, ROWS), BF16)
    scratch = [
        V((5, 1, 128), BF16), V((span // 128, 128), BF16), V((F, 16, 128), F32),
        V((HEADS, ROWS, D), BF16),
        V((D, 3 * D), BF16), V((D, D), BF16), V((D, FF), BF16), V((FF, D), BF16),
        V((3, HEADS, HEAD_DIM, ROWS), BF16),
        V((HEADS, G, 128, ROWS), BF16),
        V((N * ROWS, 128), BF16), V((128, N * ROWS), BF16),
        heads(), heads(), V((2, HEADS, HEAD_DIM, ROWS), BF16),
        V((HEADS // 2, HEAD_DIM, 2 * ROWS), F32), V((HEADS // 2, 1, 2 * ROWS), F32),
        heads(), heads(),
        V((N * ROWS, 128), F32),
        V((sib, HEADS, ROWS, 128), BF16), V((sib, HEADS, ROWS, 128), BF16),
        V((HEADS, ROWS, 128), BF16), V((HEADS, ROWS, 128), BF16),
        heads(), heads(),
        V((HEADS, ROWS, D), BF16),
        V((F // Gm, Gm, 192, 128), BF16), V((sib, F // Gm, 192, 128), BF16),
        V((F // Gm, 192, 128), BF16), V((F // Gm, 192, 128), BF16), V((F // Gm, 192, 128), BF16),
        V((HEADS, 192, 128), BF16),
        V((F, 8, 128), F32), V((sib, F, 8, 128), F32), V((F, 8, 128), F32), V((F, 8, 128), F32),
        V((F, 8, 128), F32), V((HEADS, 8, 128), F32),
        V((F, 8, 128), F32), V((nv, 4, F, 8, 128), F32), V((nv, F, 8, 128), F32),
        V((ROWS, D), F32),
        V((F, ROWS, span), F32), V((shard, D), BF16),
        V((2, 2, ROWS, span), BF16), V((2, ROWS, span), BF16),
        V((2, ROWS, D), BF16), V((2, ROWS, D), BF16), V((2, ROWS, FF), BF16), V((2, ROWS, D), BF16),
        V((2, shard, D), BF16),
        V((5 * shard // 2, D), BF16), V((5 * shard // 2, D), BF16),
        pltpu.SemaphoreType.DMA((16,)), pltpu.SemaphoreType.DMA((nsem,)), pltpu.SemaphoreType.DMA((nsem,)),
    ]
    S = jax.ShapeDtypeStruct
    return pl.pallas_call(
        partial(body, plan),
        out_shape=(S((ROWS, D), BF16), S((ROWS, D), F32), S((ROWS, 3 * D), F32),
                   S((span, D), F32), S((128, FF), F32), S((128, D), F32), S((8, 128), F32), S((8, 128), F32)),
        in_specs=[pl.BlockSpec(memory_space=pltpu.SMEM)] + [hbm] * 12,
        out_specs=(vm,) * 8,
        scratch_shapes=scratch,
        compiler_params=pltpu.CompilerParams(
            collective_id=0, has_side_effects=True, vmem_limit_bytes=(36 << 20) + 12 * N * ROWS * 128),
    )(lengths, *(pltpu.with_memory_space_constraint(x, pltpu.HBM) for x in (
        *vectors, tokens, cotangent, qkv_weight, out_weight, up_weight, down_weight)))


def finish(y, dx, dq, down, up, out, v, v1, o_y, o_dx, o_g1, o_b1, o_dq, o_out, o_g2, o_b2, o_up, o_ub, o_down, o_db,
           o_rms, sem):
    D = dx.shape[1]
    n = down.shape[0] // 128
    pairs = ((up, o_up), (down, o_down), (dq, o_dq), (dx, o_dx), (out, o_out), (y, o_y))
    copies = [pltpu.make_async_copy(src, dst, sem.at[i]) for i, (src, dst) in enumerate(pairs)]
    for copy in copies:
        copy.start()
    o_g1[...] = v1[0:1, :]
    o_b1[...] = v1[1:2, :]
    o_g2[...] = v[0:1, :]
    o_b2[...] = v[1:2, :]
    o_ub[...] = v[2 : 2 + n, :]
    o_db[...] = v[2 + n : 3 + n, :]
    stats = v[3 + n : 4 + n, :]
    o_rms[...] = jnp.sqrt(stats[:, 0:3] / (stats[:, 3:4] * D))
    for copy in copies:
        copy.wait()


def on_device(plan, tokens, lengths, ln1_gain, ln1_bias, qkv_weight, out_weight, ln2_gain, ln2_bias,
              up_weight, up_bias, down_weight, down_bias, cotangent):
    D = tokens.shape[1]
    F = plan.F
    span = up_weight.shape[1] // F
    vectors = [x.reshape(-1, 128) for x in (ln1_gain, ln1_bias, ln2_gain, ln2_bias, up_bias, down_bias)]
    results = layer(
        plan, lengths, vectors, tokens, cotangent, qkv_weight, out_weight, up_weight, down_weight)
    S = jax.ShapeDtypeStruct
    vec = S((1, 128), F32)
    vm = pl.BlockSpec(memory_space=pltpu.VMEM)
    hbm = pl.BlockSpec(memory_space=pltpu.HBM)
    outs = pl.pallas_call(
        finish,
        out_shape=(S((ROWS, D), BF16), S((ROWS, D), F32), vec, vec, S((ROWS, 3 * D), F32), S((128, D), F32),
                   vec, vec, S((128, F * span), F32), S((span // 128, 128), F32), S((span, D), F32), vec,
                   S((1, 3), F32)),
        in_specs=[vm] * 8,
        out_specs=(hbm, hbm, vm, vm, hbm, hbm, vm, vm, hbm, vm, hbm, vm, vm),
        scratch_shapes=[pltpu.SemaphoreType.DMA((6,))],
        compiler_params=pltpu.CompilerParams(vmem_limit_bytes=16 << 20),
    )(*results)
    outs = list(outs)
    for i in (2, 3, 6, 7, 9, 11, 12):
        outs[i] = outs[i].reshape(-1)
    return tuple(outs)


def solution(mesh):
    plan = Plan(mesh.shape["seq"], mesh.shape["ctx"], mesh.shape["fsdp"])
    rows = P(("seq", "ctx", "fsdp"), None)
    f1, f2 = P("fsdp"), P("fsdp", None)
    return jax.shard_map(
        partial(on_device, plan),
        mesh=mesh,
        in_specs=(rows, P("seq"), f1, f1, f2, f2, f1, f1, f2, f1, f2, f1, rows),
        out_specs=(rows, rows, f1, f1, f2, f2, f1, f1, f2, f1, f2, f1, P()),
        check_vma=False,
    )
```

```python
from functools import partial
import itertools

import jax
import jax.numpy as jnp
from jax import lax
from jax.experimental import pallas as pl
from jax.experimental.pallas import tpu as pltpu
from jax.sharding import PartitionSpec as P

HEADS = 8
HEAD_DIM = 64
EPS = 1e-05
NEG = -1e30
F32 = jnp.float32
BF16 = jnp.bfloat16
MESH = pl.DeviceIdType.MESH
ROWS = 128
KEYS = 512
KEYS_BACK = 512
LAST = 3
PARTS = [(0, 256, False, False), (256, 256, False, False), (512, 128, False, False), (640, 128, False, False), (768, 128, True, False), (896, 128, False, True), (1024, 128, False, False)]
EVENTS = [0, 1, 2, 3, 4, 5, 6, 0, 7, 7, 4, 1, 0, 2, 7, 1, 3, 0, 7, 2, 5, 1, 6, 2, 3, 4, 0, 5, 7, 3, 6, 4, 1, 2, 0, 6, 5, 3, 4, 1, 2, 0, 6, 5, 3, 4, 1, 2, 0, 6, 5, 3, 4, 6, 1, 2, 3, 4, 6]
TICKS = [1, 1, 4, 1, 1, 1, 3, 3, 0, 6, 8, 0, 5, 0, 5, 4, 0, 7, 3, 0, 0, 0]

ERF_TOP = (
    0.00022905065861350646,
    0.0034082910107109506,
    0.050955695062380861,
    0.18520832239976145,
    1.128379143519084,
)
ERF_LOW = (
    -1.1791602954361697e-7,
    0.000023547966471313185,
    0.0010179625278914885,
    0.014070470171167667,
    0.11098505178285362,
    0.49746925110067538,
    1.0,
)


def mm(a, b, ca=1, cb=0):
    return lax.dot_general(a, b, (((ca,), (cb,)), ((), ())), preferred_element_type=F32)


def erf(x):
    x = jnp.clip(x, -3.832506856900711, 3.832506856900711)
    s = x * x
    top = jnp.full_like(s, ERF_TOP[0])
    for c in ERF_TOP[1:]:
        top = top * s + c
    low = jnp.full_like(s, ERF_LOW[0])
    for c in ERF_LOW[1:]:
        low = low * s + c
    return x * top / low


def row_norm(x):
    center = jnp.mean(x, axis=1, keepdims=True)
    shifted = x - center
    spread = jnp.mean(shifted * shifted, axis=1, keepdims=True)
    r = lax.rsqrt(spread + EPS)
    return shifted * r, r


class Plan:
    def __init__(self, seqs, ctx, fsdp):
        self.S, self.C, self.F = seqs, ctx, fsdp
        self.N = ctx * fsdp
        self.G = self.N // HEADS
        self.bits = []
        b = 1
        while b < ctx:
            self.bits.append(b)
            b *= 2

    def split(self, dev):
        s, c, f = dev
        p = c * self.F + f
        return p // self.G, p % self.G

    def at(self, s, p):
        return (s, p // self.F, p % self.F)

    def head_peer(self, dev, k):
        h, g = self.split(dev)
        return self.at(dev[0], ((h + k) % HEADS) * self.G + g)

    def flip_peer(self, dev):
        h, g = self.split(dev)
        return self.at(dev[0], (h + 1 - 2 * (h % 2)) * self.G + g)

    def sibling(self, dev, k):
        h, g = self.split(dev)
        return self.at(dev[0], h * self.G + (g + k) % self.G)

    def fsdp_low(self, dev):
        s, c, f = dev
        return (s, c, f + 1 - 2 * (f % 2))

    def fsdp_high(self, dev):
        s, c, f = dev
        return (s, c, (f + 2) % self.F)

    def seq_peer(self, dev):
        s, c, f = dev
        return ((s + 1) % self.S, c, f)

    def ctx_peer(self, dev, b):
        s, c, f = dev
        return (s, c + b - 2 * b * ((c // b) % 2), f)

    def quad_peer(self, dev, b, k):
        s, c, f = dev
        return (s, (c // (4 * b)) * (4 * b) + ((c // b + k) % 4) * b + c % b, f)

    def greeted(self):
        base = [partial(self._head, k) for k in range(1, HEADS)]
        base += [partial(self._sib, k) for k in range(1, self.G)]
        base += [self.seq_peer]
        more = [self.fsdp_low, self.fsdp_high] + [partial(self._ctx, b) for b in self.bits]
        more += [partial(self._quad, b, k) for b in self.bits[:-1:2] for k in (1, 2, 3)]
        devs = list(itertools.product(range(self.S), range(self.C), range(self.F)))
        for extra in more:
            if not all(extra(d) in [p(d) for p in base] for d in devs):
                base.append(extra)
        return base

    def _head(self, k, dev):
        return self.head_peer(dev, k)

    def _sib(self, k, dev):
        return self.sibling(dev, k)

    def _quad(self, b, k, dev):
        return self.quad_peer(dev, b, k)

    def _ctx(self, b, dev):
        return self.ctx_peer(dev, b)


def body(plan, lens, g1_in, b1_in, g2_in, b2_in, ub_in, db_in, tok_in, cot_in, wq_in, wo_in, wu_in, wd_in,
         out_y, out_dx, out_dq, out_down, out_up, out_out, out_v, out_v1,
         raw, rawu, small, tok, wq, wo, wu, wd,
         msg, kvb, kvn, kvw, qb, o_send, at2, ot, lse, do_send, do_recv,
         dkv, dkvs, dkvr, dkv_red, dkv_recv, dq_send, dq_recv, nall,
         gp, gr1, gs, gr2, gt, gr,
         v1, v1r, v1s, v1r2, v1t, v1r3, v0, vrecv, vacc,
         mid, slope, out_r, actb, xa, c2, n2, g2, gb2, sa, into, sums, lsem, ssem, rsem):
    G, F, N = plan.G, plan.F, plan.N
    Gm = min(G, F)
    seq, ctx, fs = (lax.axis_index(a) for a in ("seq", "ctx", "fsdp"))
    me = (seq, ctx, fs)
    h, g = plan.split(me)
    fl, fh = fs % 2, fs // 2
    D = tok.shape[2]
    FF = wu.shape[1]
    span = FF // F
    valid = lens[0]
    counter = itertools.count()
    locals_ = itertools.count()

    def local(src, dst):
        copy = pltpu.make_async_copy(src, dst, lsem.at[next(locals_)])
        copy.start()
        return copy

    l_raw = [local(x, raw.at[i]) for i, x in enumerate((g1_in, b1_in, g2_in, b2_in, db_in))]
    l_raw.append(local(ub_in, rawu))
    l_tok = local(tok_in, tok.at[h])
    greet = plan.greeted()
    bar = pltpu.get_barrier_semaphore()
    for peer in greet:
        pl.semaphore_signal(bar, inc=1, device_id=peer(me), device_id_type=MESH)
    for copy in l_raw:
        copy.wait()
    own = [raw[i].astype(F32) for i in range(4)] + [rawu[...].astype(F32), raw[4].astype(F32)]
    used = 5 + span // 128
    small[fs] = jnp.concatenate(own + [jnp.zeros((16 - used, 128), F32)], axis=0)
    pl.semaphore_wait(bar, len(greet))

    sent = []

    def send(src, dst, dev):
        n = next(counter)
        copy = pltpu.make_async_remote_copy(
            src_ref=src, dst_ref=dst, send_sem=ssem.at[n], recv_sem=rsem.at[n],
            device_id=dev, device_id_type=MESH)
        copy.start()
        sent.append(copy)
        return copy

    posted = []

    def new_group():
        first = next(counter)
        for _ in range(HEADS - 1):
            next(counter)
        return first

    def post(group, to, src, dst):
        copy = pltpu.make_async_remote_copy(
            src_ref=src, dst_ref=dst, send_sem=ssem.at[group + to], recv_sem=rsem.at[group + h],
            device_id=plan.at(seq, to * G + g), device_id_type=MESH)

        @pl.when(h != to)
        def _():
            copy.start()

        posted.append((to, copy))

    def arrived(group, ref):
        for source in range(HEADS):
            copy = pltpu.make_async_remote_copy(
                src_ref=ref.at[source], dst_ref=ref.at[source], send_sem=ssem.at[group + source],
                recv_sem=rsem.at[group + source], device_id=plan.at(seq, source * G + g), device_id_type=MESH)

            @pl.when(h != source)
            def _():
                copy.wait_recv()

    low, high = plan.fsdp_low(me), plan.fsdp_high(me)
    fhigh = (fs + 2) % F
    head_dev = {k: plan.head_peer(me, k) for k in range(1, HEADS)}
    head_idx = {k: (h + k) % HEADS for k in range(1, HEADS)}
    sib_dev = {k: plan.sibling(me, k) for k in range(1, G)}
    sib_idx = {k: (g + k) % G for k in range(1, G)}

    far = plan.seq_peer(me)
    sm_low = send(small.at[fs], small.at[fs], low)
    sm_high = send(small.at[fs], small.at[fs], high)
    shards = ((wq_in, wq, 128), (wo_in, wo, 128), (wu_in, wu, 128), (wd_in, wd, span))

    def rows_of(w, first, count):
        return w.at[pl.ds(pl.multiple_of(first, count), count), :]

    def group_of(ref, which, c):
        return ref.at[pl.ds(pl.multiple_of(which * 128, 128), 128), c * D : (c + 1) * D]

    order = (1, 2, 0)
    q_high = {c: send(wq_in.at[:, c * D : (c + 1) * D], group_of(wq, fs, c), high) for c in order}
    q_low = {c: send(wq_in.at[:, c * D : (c + 1) * D], group_of(wq, fs, c), low) for c in order}
    half_rows = ROWS // 2

    def tokens_out(part):
        rows = slice(part * half_rows, (part + 1) * half_rows)
        return [send(tok_in.at[rows, :], tok.at[h, rows, :], head_dev[k]) for k in (2, 4, 6)]

    tok_copies = tokens_out(0)
    w_high, w_low = {}, {}
    for q in range(1, 4):
        src, dst, step = shards[q]
        w_low[q] = send(src, rows_of(dst, fs * step, step), low)
    l_w = [local(src, rows_of(dst, fs * step, step)) for src, dst, step in shards]
    l_cot = local(cot_in, c2.at[0])

    crossed, passed = {}, {}
    cuts = {1: 1, 2: 2, 3: 2}

    def slice_of(q, owner, p):
        count = shards[q][2] // (2 * cuts[q])
        first = (seq * cuts[q] + p) * count
        return count, first, owner * shards[q][2] + first

    def fetch(q):
        src, dst, step = shards[q]
        for p in range(cuts[q]):
            count, first, at = slice_of(q, fs, p)
            w_high[q, p] = send(rows_of(src, first, count), rows_of(dst, at, count), high)

    def cross(q, p):
        w_high[q, p].wait_recv()
        count, _, at = slice_of(q, fhigh, p)
        piece = rows_of(shards[q][1], at, count)
        crossed[q, p] = send(piece, piece, far)

    def hand_on(q):
        for p in range(cuts[q]):
            crossed[q, p].wait_recv()
        _, dst, step = shards[q]
        piece = rows_of(dst, fhigh * step, step)
        passed[q] = send(piece, piece, low)

    sm_low.wait_recv()
    sm_high.wait_recv()
    sm_fwd = send(small.at[fhigh], small.at[fhigh], low)
    l_tok.wait()
    inputs = tok[h].astype(F32)
    n_one, r_one = row_norm(inputs)
    sm_fwd.wait_recv()

    def vec(first, many=1):
        return jnp.concatenate(
            [small[q, first + r : first + r + 1, :] for q in range(F) for r in range(many)], axis=1)

    gain1, bias1, gain2, bias2 = vec(0), vec(1), vec(2), vec(3)
    down_bias = vec(4 + span // 128)
    normed = (n_one * gain1 + bias1).astype(BF16)
    nall[h] = normed
    l_w[0].wait()
    qkv_in = {}
    for c in order:
        q_low[c].wait_recv()
        q_high[c].wait_recv()
        piece = group_of(wq, fhigh, c)
        handed = send(piece, piece, low)
        handed.wait_recv()
        proj = mm(normed, wq[:, c * D : (c + 1) * D])
        if c == 0:
            proj = proj * (HEAD_DIM ** -0.5)
        msg[c] = proj.T.astype(BF16).reshape(HEADS, HEAD_DIM, ROWS)
        for k in range(1, HEADS):
            dst = qb.at[h] if c == 0 else kvb.at[h, g, (c - 1) * 64 : c * 64]
            qkv_in[c, k] = send(msg.at[c, head_idx[k]], dst, head_dev[k])
        if c == 0:
            qb[h] = msg[c, h]
        else:
            kvb[h, g, (c - 1) * 64 : c * 64] = msg[c, h]
    fetch(1)
    fetch(2)
    fetch(3)
    for c in (1, 2):
        for k in range(1, HEADS):
            qkv_in[c, k].wait_recv()
    tok_copies += tokens_out(1)
    kv_sib = {k: send(kvb.at[:, g], kvb.at[:, g], sib_dev[k]) for k in range(1, G)}

    def spread_block(hp, gg):
        at = pl.multiple_of((hp * G + gg) * ROWS, ROWS)
        block = kvb[hp, gg]
        kvw[:, pl.ds(at, ROWS)] = block
        kvn[pl.ds(at, ROWS), :] = block.astype(F32).T.astype(BF16)

    @pl.loop(0, HEADS)
    def _(hp):
        spread_block(hp, g)

    for k in range(1, G):
        kv_sib[k].wait_recv()
    for k in range(1, G):
        @pl.loop(0, HEADS)
        def _(hp, k=k):
            spread_block(hp, sib_idx[k])
    cross(1, 0)
    for k in range(1, HEADS):
        qkv_in[0, k].wait_recv()

    tiles = HEADS // 2

    def span_of(i, most):
        keys = (i + 1) * 2 * G * ROWS
        count = 1
        while keys % count or keys // count > most:
            count += 1
        return keys // count, count

    def over(count, step, start):
        return step(0, start) if count == 1 else lax.fori_loop(0, count, step, start)

    def keys_at(kc, size):
        return pl.ds(pl.multiple_of(kc * size, size), size) if not isinstance(kc, int) else slice(0, size)

    def key_iota(size):
        return lax.broadcasted_iota(jnp.int32, (size, 2 * ROWS), 0)

    def limits(i):
        col = lax.broadcasted_iota(jnp.int32, (1, 2 * ROWS), 1)
        pos = ((2 * i + col // ROWS) * G + g) * ROWS + col % ROWS
        return jnp.minimum(pos + 1, valid)

    nothing = jnp.zeros((HEAD_DIM, 2 * ROWS), BF16)

    def attend(i):
        qt = jnp.concatenate([qb[2 * i], qb[2 * i + 1]], axis=1)
        stacked = jnp.concatenate([qt, nothing], axis=0)
        limit = limits(i)

        size, count = span_of(i, KEYS)

        def step(kc, carry):
            at = keys_at(kc, size)
            st = mm(kvn[at, :], stacked)
            st = jnp.where(key_iota(size) < limit - kc * size, st, NEG)
            mn = jnp.max(st, axis=0, keepdims=True)
            if carry is not None:
                m, l, acc = carry
                mn = jnp.maximum(m, mn)
            e = jnp.exp(st - mn)
            total_e = jnp.sum(e, axis=0, keepdims=True)
            out = mm(kvw[64:128, at], e.astype(BF16))
            if carry is not None:
                al = jnp.exp(m - mn)
                total_e, out = l * al + total_e, acc * al + out
            return mn, total_e, out

        first = None if count == 1 else (
            jnp.full((1, 2 * ROWS), NEG, F32), jnp.zeros((1, 2 * ROWS), F32),
            jnp.zeros((HEAD_DIM, 2 * ROWS), F32))
        m, l, acc = over(count, step, first)
        o = acc / l
        ot[i] = o
        lse[i] = m + jnp.log(l)
        for p in range(2):
            o_send[2 * i + p] = o[:, p * ROWS : (p + 1) * ROWS].astype(BF16)
            post(o_group, 2 * i + p, o_send.at[2 * i + p], at2.at[0, h])

    o_group = new_group()
    for i in range(tiles):
        attend(i)
        if i == 1:
            cross(2, 0)
        if i == 2:
            cross(2, 1)
            hand_on(1)
    at2[0, h] = o_send[h]
    cross(3, 0)
    parity = h % 2
    flip = plan.flip_peer(me)
    for copy in tok_copies:
        copy.wait_recv()
    l_cot.wait()
    sib_c = send(c2.at[0], c2.at[1], low)
    tok4 = tok.reshape(HEADS // 2, 2, ROWS, D)
    tok_flip = send(tok4.at[:, parity], tok4.at[:, parity], flip)
    hand_on(2)
    cross(3, 1)
    arrived(o_group, at2.at[0])
    sib_at = send(at2.at[0], at2.at[1], low)

    def add_rows(dst, refs, rows):
        block = max(b for b in (16, 32, 64) if rows % b == 0)

        @pl.loop(0, rows // block)
        def _(t):
            at = pl.ds(pl.multiple_of(t * block, block), block)
            if len(refs) == 2:
                dst[at, :] = refs[0][at, :] + refs[1][at, :]
            else:
                x = refs[0][at, :].astype(F32)
                for ref in refs[1:]:
                    x = x + ref[at, :].astype(F32)
                dst[at, :] = x.astype(BF16)

    pool = {"into": 0, "sums": 0}

    def take(name, rows):
        first = pool[name]
        pool[name] += rows
        ref = {"into": into, "sums": sums}[name]
        return ref.at[pl.ds(first, rows), :]

    class Part:
        def __init__(self, first, rows, y_first, quads):
            self.first, self.rows = first, rows
            self.off, self.n = first, rows
            self.pair = sa.at[:, pl.ds(first, rows), :]
            self.piece = None
            x = ("cut", [far], 2, seq)
            y = ("pick", [high], 2, fh)
            self.steps = [y, x] if y_first else [x, y]
            n, bits = rows // 2, list(plan.bits)
            while bits:
                b = bits[0]
                if quads and len(bits) > 1 and n % 64 == 0:
                    peers = [plan.quad_peer(me, b, k) for k in (1, 2, 3)]
                    self.steps.append(("cut", peers, 4, (ctx // b) % 4))
                    bits, n = bits[2:], n // 4
                else:
                    kind = "cut" if n % 32 == 0 else "whole"
                    self.steps.append((kind, [plan.ctx_peer(me, b)], 2, (ctx // b) % 2))
                    bits, n = bits[1:], n // 2 if kind == "cut" else n
            self.trail = []
            self.t = -1
            self.done = False

        def pump(self):
            if self.done:
                return
            if self.t >= 0:
                for copy in self.copies:
                    copy.wait_recv()
                if self.t < len(self.steps):
                    self.finish()
                else:
                    self.off, self.n = self.region
            self.t += 1
            if self.t < len(self.steps):
                self.begin()
            elif self.trail:
                peers, off, n = self.trail.pop()
                region = out_r.at[pl.ds(pl.multiple_of(self.off, 16), self.n), :]
                self.copies = [send(region, region, dev) for dev in peers]
                self.region = off, n
            else:
                self.done = True
                self.store()

        def store(self):
            for row in range(self.first, self.first + self.rows, 128):
                x = out_r[row : row + 128, :].astype(F32)
                if row < span:
                    out_down[row : row + 128, :] = x
                elif row < span + 512:
                    q = (row - span) // 128
                    out_up[:, q * span : (q + 1) * span] = x
                else:
                    out_out[...] = x

        def slot(self, ref, which, size):
            return ref.at[pl.ds(pl.multiple_of(which * size, 16), size), :]

        def begin(self):
            kind, peers, ways, mine = self.steps[self.t]
            self.size = self.n // ways if kind == "cut" else self.n
            self.got, self.copies = [], []
            for k, dev in enumerate(peers):
                there = (mine + k + 1) % ways
                if self.piece is None and kind == "cut":
                    got = take("into", 2 * self.size).reshape(2, self.size, D)
                    src = self.pair.at[:, pl.ds(pl.multiple_of(there * self.size, 16), self.size), :]
                else:
                    got = take("into", self.size)
                    if kind == "pick":
                        src = self.pair.at[there]
                    elif kind == "cut":
                        src = self.slot(self.piece, there, self.size)
                    else:
                        src = self.piece
                self.got.append(got)
                self.copies.append(send(src, got, dev))

        def finish(self):
            kind, peers, ways, mine = self.steps[self.t]
            size = self.size
            if kind == "cut":
                self.trail.append((peers, self.off, self.n))
                self.off = self.off + mine * size
            if self.piece is None and kind == "cut":
                dst = take("sums", 2 * size).reshape(2, size, D)
                for y in range(2):
                    add_rows(dst.at[y], [self.slot(self.pair.at[y], mine, size)] + [got.at[y] for got in self.got], size)
                self.pair = dst
            else:
                if self.t + 1 == len(self.steps):
                    dst = out_r.at[pl.ds(pl.multiple_of(self.off, 16), size), :]
                else:
                    dst = take("sums", size)
                if kind == "pick":
                    own = self.pair.at[mine]
                elif kind == "cut":
                    own = self.slot(self.piece, mine, size)
                else:
                    own = self.piece
                add_rows(dst, [own] + self.got, size)
                self.piece = dst
            self.n = size

    class Vectors:
        def __init__(self):
            self.steps = [([p], 2, None) for p in (low, high)]
            bits = list(plan.bits)
            while bits:
                b = bits[0]
                if len(bits) > 1:
                    self.steps.append(([plan.quad_peer(me, b, k) for k in (1, 2, 3)], 4, (ctx // b) % 4))
                    bits = bits[2:]
                else:
                    self.steps.append(([plan.ctx_peer(me, b)], 2, None))
                    bits = bits[1:]
            self.steps.append(([far], 2, None))
            self.t = -1
            self.done = False

        def begin(self, src):
            peers, ways, mine = self.steps[self.t]
            if ways == 2:
                self.copies = [send(src, vrecv.at[self.t, 0], peers[0])]
            else:
                vrecv[self.t, mine] = src[...]
                self.copies = [send(src, vrecv.at[self.t, mine], dev) for dev in peers]

        def pump(self):
            if self.done:
                return
            t = self.t
            if t < 0:
                self.t = 0
                self.begin(v0)
                return
            for copy in self.copies:
                copy.wait_recv()
            if self.steps[t][1] == 2:
                vacc[t] = (v0[...] if t == 0 else vacc[t - 1]) + vrecv[t, 0]
            else:
                vacc[t] = (vrecv[t, 0] + vrecv[t, 1]) + (vrecv[t, 2] + vrecv[t, 3])
            self.t += 1
            if self.t < len(self.steps):
                self.begin(vacc.at[t])
            else:
                self.done = True

    events, parts = [], []

    turns = iter(TICKS)

    def step_parts(count):
        for _ in range(min(count, len(events))):
            parts[events.pop(0)].pump()

    def tick():
        step_parts(next(turns))

    for q in range(1, 4):
        l_w[q].wait()
        w_low[q].wait_recv()
    passed[1].wait_recv()
    at_t = at2[0].reshape(D, ROWS)
    attention_out = mm(at_t, wo[...], 0, 0)
    middle = tok[h].astype(F32) + attention_out
    n_two, r_two = row_norm(middle)
    normed_two = (n_two * gain2 + bias2).astype(BF16)
    n2[0] = normed_two
    sib_n = send(n2.at[0], n2.at[1], low)
    passed[2].wait_recv()
    sib_a = []
    half = span // 2
    for p in range(2):
        mine = slice(p * half, (p + 1) * half)
        for q in range(F):
            rows = range(4 + p * half // 128, 4 + (p + 1) * half // 128)
            bias = jnp.concatenate([small[q, r : r + 1, :] for r in rows], axis=1)
            raised = mm(normed_two, wu[:, q * span + p * half : q * span + (p + 1) * half]) + bias
            cdf = 0.5 * (1.0 + erf(raised * (0.5 ** 0.5)))
            pdf = jnp.exp(-0.5 * raised * raised) * 0.3989422804014327
            actb[q // 2, q % 2, :, mine] = (raised * cdf).astype(BF16)
            slope[q, :, mine] = cdf + raised * pdf
        sib_a.append(send(actb.at[:, 1 - fl, :, mine], xa.at[:, :, mine], low))
    sib_c.wait_recv()
    both_c = c2[...].reshape(2 * ROWS, D)
    cots = c2[0]
    gnt = jnp.zeros((ROWS, D), F32)

    def back_block(step, gnt):
        q = (2 * fh + step) % F
        cols = pl.ds(pl.multiple_of(q * span, span), span)
        grad = (mm(cots, wd[cols, :], 1, 1) * slope[q]).astype(BF16)
        g2[0, :, cols] = grad
        return gnt + mm(grad, wu[:, cols], 1, 1)

    def share_blocks(y):
        cols = pl.ds(pl.multiple_of(y * 2 * span, 2 * span), 2 * span)
        return send(g2.at[0, :, cols], g2.at[1, :, cols], low)

    parts += [Part(*p) for p in PARTS]
    events += EVENTS
    for p in range(2):
        mine = slice(p * half, (p + 1) * half)
        sib_a[p].wait_recv()
        for y in range(2):
            a = jnp.concatenate([actb[y, fl, :, mine], xa[y, :, mine]], axis=0)
            sa[y, mine, :] = mm(a, both_c, 0, 0).astype(BF16)
        tick()
        gnt = back_block(p, gnt)
    sib_g = [share_blocks(fh)]
    hand_on(3)
    passed[3].wait_recv()
    for step in range(F // 2, F):
        gnt = back_block(step, gnt)
    sib_g.append(share_blocks(1 - fh))

    def scatter_row(ref, row, x):
        for q in range(F):
            ref[q, row : row + 1, :] = x[:, 128 * q : 128 * (q + 1)]

    grad_final = cots.astype(F32)
    e2 = gnt * gain2
    grad_middle = grad_final + r_two * (
        e2 - jnp.mean(e2, axis=1, keepdims=True) - n_two * jnp.mean(e2 * n_two, axis=1, keepdims=True))
    mid[...] = grad_middle
    gb = grad_middle.astype(BF16)
    gb2[0] = gb
    sib_b = send(gb2.at[0], gb2.at[1], low)
    ga = mm(wo[...], gb, 1, 1).astype(BF16)
    do_send[...] = ga.reshape(HEADS, HEAD_DIM, ROWS)
    do_in = {k: send(do_send.at[head_idx[k]], do_recv.at[h], head_dev[k]) for k in (4, 3, 5, 2, 6, 1, 7)}
    do_recv[h] = do_send[h]

    sib_n.wait_recv()
    for copy in sib_g:
        copy.wait_recv()
    for y in range(2):
        spot = pl.ds(pl.multiple_of((2 * y + fl) * 128, 128), 128)
        a = n2[:, :, spot].reshape(2 * ROWS, 128)
        for q in range(F):
            cols = slice(q * span, (q + 1) * span)
            sa[y, span + 128 * q : span + 128 * (q + 1), :] = mm(
                a, g2[:, :, cols].reshape(2 * ROWS, span), 0, 0).astype(BF16)
    tick()
    sib_at.wait_recv()
    sib_b.wait_recv()
    for y in range(2):
        x = jnp.zeros((128, D), F32)
        for p in range(2):
            rows = at2[p, pl.ds(pl.multiple_of((2 * y + fl) * 2, 2), 2)].reshape(128, ROWS)
            x = x + mm(rows, gb2[p])
        sa[y, span + 512 : span + 640, :] = x.astype(BF16)

    tick()

    feed_out = down_bias
    for q in range(F):
        cols = slice(q * span, (q + 1) * span)
        feed_out = feed_out + mm(actb[q // 2, q % 2], wd[cols, :])
        grad = g2[0, :, cols].astype(F32)
        v0[q, 2 : 2 + span // 128, :] = jnp.concatenate(
            [jnp.sum(grad[:, 128 * r : 128 * (r + 1)], axis=0, keepdims=True)
             for r in range(span // 128)], axis=0)
    final = middle + feed_out
    out_y[...] = final.astype(BF16)
    scatter_row(v0, 0, jnp.sum(gnt * n_two, axis=0, keepdims=True))
    scatter_row(v0, 1, jnp.sum(gnt, axis=0, keepdims=True))
    scatter_row(v0, 2 + span // 128, jnp.sum(grad_final, axis=0, keepdims=True))
    place = (ctx * F + fs) * ROWS
    row = lax.broadcasted_iota(jnp.int32, (ROWS, 1), 0) + place
    live = (row < valid).astype(F32)

    def total(x):
        return jnp.sum(jnp.sum(x, axis=1, keepdims=True) * live, axis=0, keepdims=True)

    lane1 = lax.broadcasted_iota(jnp.int32, (1, 128), 1)
    stats = jnp.where(lane1 == 0, total(final * final), 0.0)
    stats = jnp.where(lane1 == 1, total(attention_out * attention_out), stats)
    stats = jnp.where(lane1 == 2, total(feed_out * feed_out), stats)
    stats = jnp.where(lane1 == 3, jnp.sum(live, axis=0, keepdims=True), stats)
    for q in range(F):
        v0[q, 3 + span // 128 : 4 + span // 128, :] = stats

    parts.append(Vectors())
    tick()
    tok_flip.wait_recv()

    @pl.loop(0, HEADS)
    def _(j):
        n, _ = row_norm(tok[j].astype(F32))
        nall[j] = (n * gain1 + bias1).astype(BF16)

    for k in range(1, HEADS):
        do_in[k].wait_recv()
    tick()

    dq_group, dkv_group = new_group(), new_group()
    dkv_sib = {}

    def attend_back(i):
        qt = jnp.concatenate([qb[2 * i], qb[2 * i + 1]], axis=1)
        dt = jnp.concatenate([do_recv[2 * i], do_recv[2 * i + 1]], axis=1)
        stacked = jnp.concatenate(
            [jnp.concatenate([qt, nothing], axis=1), jnp.concatenate([nothing, dt], axis=1)], axis=0)
        delta = jnp.sum(dt.astype(F32) * ot[i], axis=0, keepdims=True)
        level = lse[i]
        limit = limits(i)

        size, count = span_of(i, KEYS_BACK)

        def step(kc, acc):
            at = keys_at(kc, size)
            both = mm(kvn[at, :], stacked)
            st = jnp.where(key_iota(size) < limit - kc * size, both[:, : 2 * ROWS], NEG)
            p = jnp.exp(st - level)
            ds = (p * (both[:, 2 * ROWS :] - delta)).astype(BF16)
            pair = jnp.concatenate([ds, p.astype(BF16)], axis=1)
            more = mm(pair, stacked, 1, 1)
            if i == tiles - 1:
                dkv[at, :] = more
            else:
                dkv[at, :] += more
            out = mm(kvw[0:64, at], ds)
            return out if acc is None else acc + out

        acc = over(count, step, None if count == 1 else jnp.zeros((HEAD_DIM, 2 * ROWS), F32))
        low_dq = (acc.astype(BF16).astype(F32) * (HEAD_DIM ** -0.5)).astype(BF16)
        for p in range(2):
            j = 2 * i + p
            dq_send[j] = low_dq[:, p * ROWS : (p + 1) * ROWS]
            post(dq_group, j, dq_send.at[j], dq_recv.at[h])
            for k in range(1, G):
                spot = pl.multiple_of((j * G + sib_idx[k]) * ROWS, ROWS)
                dkvs[k - 1, j] = dkv[pl.ds(spot, ROWS), :].astype(BF16)
        for k in range(1, G):
            pairs = slice(2 * i, 2 * i + 2)
            dkv_sib[i, k] = send(dkvs.at[k - 1, pairs], dkvr.at[k - 1, pairs], sib_dev[k])

    def give_back(i):
        for k in range(1, G):
            dkv_sib[i, k].wait_recv()
        for j in (2 * i, 2 * i + 1):
            x = dkv[pl.ds(pl.multiple_of((j * G + g) * ROWS, ROWS), ROWS), :]
            for k in range(1, G):
                x = x + dkvr[k - 1, j].astype(F32)
            dkv_red[j] = x.astype(BF16)
            post(dkv_group, j, dkv_red.at[j], dkv_recv.at[h])

    for i in reversed(range(tiles)):
        attend_back(i)
        if i < tiles - 1:
            give_back(i + 1)
        tick()
    give_back(0)
    dq_recv[h] = dq_send[h]
    dkv_recv[h] = dkv_red[h]
    tick()

    dq_cat = jnp.concatenate([dq_send[j] for j in range(HEADS)], axis=1)
    dkv_cat = jnp.concatenate([dkv_red[j].astype(F32).T.astype(BF16) for j in range(HEADS)], axis=1)
    heads_t = jnp.concatenate([dq_cat, dkv_cat], axis=0)
    gw = mm(heads_t, nall[...].reshape(HEADS * ROWS, D)).astype(BF16)
    for q in range(F):
        gp[q // Gm, q % Gm] = gw[:, 128 * q : 128 * (q + 1)]
    g_sib = {k: send(gp.at[:, sib_idx[k] % Gm], gr1.at[k - 1], sib_dev[k]) for k in range(1, G)}
    tick()
    for k in range(1, G):
        g_sib[k].wait_recv()
    own = gp[:, g % Gm].astype(F32)
    for k in range(1, G):
        own = own + gr1[k - 1].astype(F32)
    gs[...] = own.astype(BF16)
    if plan.S > 1:
        g_seq = send(gs, gr2, far)
    tick()

    arrived(dq_group, dq_recv)
    arrived(dkv_group, dkv_recv)
    tick()
    lane = lax.broadcasted_iota(jnp.int32, (ROWS, 128), 1)
    left = lane < 64
    cols = [[], []]
    for i in range(HEADS // 2):
        a = dkv_recv[2 * i].astype(F32)
        b = dkv_recv[2 * i + 1].astype(F32)
        cols[0].append(jnp.where(left, a, pltpu.roll(b, 64, 1)))
        cols[1].append(jnp.where(left, pltpu.roll(a, 64, 1), b))
    kv_cols = jnp.concatenate(cols[0] + cols[1], axis=1).astype(BF16)
    grad_normed = mm(kv_cols, wq[:, D:], 1, 1) + mm(dq_recv[...].reshape(D, ROWS), wq[:, :D], 0, 1)
    n_one, r_one = row_norm(tok[h].astype(F32))
    scatter_row(v1, 0, jnp.sum(grad_normed * n_one, axis=0, keepdims=True))
    scatter_row(v1, 1, jnp.sum(grad_normed, axis=0, keepdims=True))
    v1_sib = {k: send(v1, v1r.at[k - 1], sib_dev[k]) for k in range(1, G)}
    e1 = grad_normed * gain1
    out_dx[...] = mid[...] + r_one * (
        e1 - jnp.mean(e1, axis=1, keepdims=True) - n_one * jnp.mean(e1 * n_one, axis=1, keepdims=True))
    tick()
    for k in range(1, G):
        v1_sib[k].wait_recv()
    acc1 = v1[...]
    for k in range(1, G):
        acc1 = acc1 + v1r[k - 1]
    v1s[...] = acc1
    if plan.S > 1:
        v1_seq = send(v1s, v1r2, far)
    tick()
    if plan.S > 1:
        g_seq.wait_recv()
        gt[...] = (gs[...].astype(F32) + gr2[...].astype(F32)).astype(BF16)
    else:
        gt[...] = gs[...]
    gr[h] = gt[fs // Gm]
    g_in = {}
    for n, k in enumerate((4, 3, 5, 2, 6, 1, 7), 1):
        there = (head_idx[k] * G + g) % F
        g_in[k] = send(gt.at[there // Gm], gr.at[h], head_dev[k])
        if n % 2 == 0:
            tick()
    if plan.S > 1:
        v1_seq.wait_recv()
        v1t[...] = v1s[...] + v1r2[...]
    else:
        v1t[...] = v1s[...]
    v1_in = {}
    for k in range(1, HEADS):
        there = (head_idx[k] * G + g) % F
        v1_in[k] = send(v1t.at[there], v1r3.at[h], head_dev[k])
    v1r3[h] = v1t[fs]
    step_parts(len(events) - LAST)

    for k in range(1, HEADS):
        g_in[k].wait_recv()
    for i in range(HEADS // 2):
        for part_no in range(3):
            lo, hi = 64 * part_no, 64 * (part_no + 1)
            x = jnp.concatenate([gr[2 * i, lo:hi, :], gr[2 * i + 1, lo:hi, :]], axis=0)
            out_dq[:, D * part_no + 128 * i : D * part_no + 128 * (i + 1)] = x.astype(F32).T
    step_parts(len(events))
    while not all(p.done for p in parts):
        for p in parts:
            p.pump()
    out_v[...] = vacc[len(parts[-1].steps) - 1, fs]
    for k in range(1, HEADS):
        v1_in[k].wait_recv()
    out_v1[...] = jnp.sum(v1r3[...], axis=0)
    for copy in sent:
        copy.wait_send()
    for to, copy in posted:
        @pl.when(h != to)
        def _(copy=copy):
            copy.wait_send()


def layer(plan, lengths, vectors, tokens, cotangent, qkv_weight, out_weight, up_weight, down_weight):
    G, F, N = plan.G, plan.F, plan.N
    Gm = min(G, F)
    D = tokens.shape[1]
    FF = up_weight.shape[1]
    span = FF // F
    nv = 3 + len(plan.bits)
    shard = span + 4 * 128 + 128
    hbm = pl.BlockSpec(memory_space=pltpu.HBM)
    vm = pl.BlockSpec(memory_space=pltpu.VMEM)
    V = pltpu.VMEM
    sib = max(G - 1, 1)
    nsem = 192 + 8 * G
    heads = lambda: V((HEADS, HEAD_DIM, ROWS), BF16)
    scratch = [
        V((5, 1, 128), BF16), V((span // 128, 128), BF16), V((F, 16, 128), F32),
        V((HEADS, ROWS, D), BF16),
        V((D, 3 * D), BF16), V((D, D), BF16), V((D, FF), BF16), V((FF, D), BF16),
        V((3, HEADS, HEAD_DIM, ROWS), BF16),
        V((HEADS, G, 128, ROWS), BF16),
        V((N * ROWS, 128), BF16), V((128, N * ROWS), BF16),
        heads(), heads(), V((2, HEADS, HEAD_DIM, ROWS), BF16),
        V((HEADS // 2, HEAD_DIM, 2 * ROWS), F32), V((HEADS // 2, 1, 2 * ROWS), F32),
        heads(), heads(),
        V((N * ROWS, 128), F32),
        V((sib, HEADS, ROWS, 128), BF16), V((sib, HEADS, ROWS, 128), BF16),
        V((HEADS, ROWS, 128), BF16), V((HEADS, ROWS, 128), BF16),
        heads(), heads(),
        V((HEADS, ROWS, D), BF16),
        V((F // Gm, Gm, 192, 128), BF16), V((sib, F // Gm, 192, 128), BF16),
        V((F // Gm, 192, 128), BF16), V((F // Gm, 192, 128), BF16), V((F // Gm, 192, 128), BF16),
        V((HEADS, 192, 128), BF16),
        V((F, 8, 128), F32), V((sib, F, 8, 128), F32), V((F, 8, 128), F32), V((F, 8, 128), F32),
        V((F, 8, 128), F32), V((HEADS, 8, 128), F32),
        V((F, 8, 128), F32), V((nv, 4, F, 8, 128), F32), V((nv, F, 8, 128), F32),
        V((ROWS, D), F32),
        V((F, ROWS, span), F32), V((shard, D), BF16),
        V((2, 2, ROWS, span), BF16), V((2, ROWS, span), BF16),
        V((2, ROWS, D), BF16), V((2, ROWS, D), BF16), V((2, ROWS, FF), BF16), V((2, ROWS, D), BF16),
        V((2, shard, D), BF16),
        V((5 * shard // 2, D), BF16), V((5 * shard // 2, D), BF16),
        pltpu.SemaphoreType.DMA((16,)), pltpu.SemaphoreType.DMA((nsem,)), pltpu.SemaphoreType.DMA((nsem,)),
    ]
    S = jax.ShapeDtypeStruct
    return pl.pallas_call(
        partial(body, plan),
        out_shape=(S((ROWS, D), BF16), S((ROWS, D), F32), S((ROWS, 3 * D), F32),
                   S((span, D), F32), S((128, FF), F32), S((128, D), F32), S((8, 128), F32), S((8, 128), F32)),
        in_specs=[pl.BlockSpec(memory_space=pltpu.SMEM)] + [hbm] * 12,
        out_specs=(vm,) * 8,
        scratch_shapes=scratch,
        compiler_params=pltpu.CompilerParams(
            collective_id=0, has_side_effects=True, vmem_limit_bytes=(36 << 20) + 12 * N * ROWS * 128),
    )(lengths, *(pltpu.with_memory_space_constraint(x, pltpu.HBM) for x in (
        *vectors, tokens, cotangent, qkv_weight, out_weight, up_weight, down_weight)))


def finish(y, dx, dq, down, up, out, v, v1, o_y, o_dx, o_g1, o_b1, o_dq, o_out, o_g2, o_b2, o_up, o_ub, o_down, o_db,
           o_rms, sem):
    D = dx.shape[1]
    n = down.shape[0] // 128
    pairs = ((up, o_up), (down, o_down), (dq, o_dq), (dx, o_dx), (out, o_out), (y, o_y))
    copies = [pltpu.make_async_copy(src, dst, sem.at[i]) for i, (src, dst) in enumerate(pairs)]
    for copy in copies:
        copy.start()
    o_g1[...] = v1[0:1, :]
    o_b1[...] = v1[1:2, :]
    o_g2[...] = v[0:1, :]
    o_b2[...] = v[1:2, :]
    o_ub[...] = v[2 : 2 + n, :]
    o_db[...] = v[2 + n : 3 + n, :]
    stats = v[3 + n : 4 + n, :]
    o_rms[...] = jnp.sqrt(stats[:, 0:3] / (stats[:, 3:4] * D))
    for copy in copies:
        copy.wait()


def on_device(plan, tokens, lengths, ln1_gain, ln1_bias, qkv_weight, out_weight, ln2_gain, ln2_bias,
              up_weight, up_bias, down_weight, down_bias, cotangent):
    D = tokens.shape[1]
    F = plan.F
    span = up_weight.shape[1] // F
    vectors = [x.reshape(-1, 128) for x in (ln1_gain, ln1_bias, ln2_gain, ln2_bias, up_bias, down_bias)]
    results = layer(
        plan, lengths, vectors, tokens, cotangent, qkv_weight, out_weight, up_weight, down_weight)
    S = jax.ShapeDtypeStruct
    vec = S((1, 128), F32)
    vm = pl.BlockSpec(memory_space=pltpu.VMEM)
    hbm = pl.BlockSpec(memory_space=pltpu.HBM)
    outs = pl.pallas_call(
        finish,
        out_shape=(S((ROWS, D), BF16), S((ROWS, D), F32), vec, vec, S((ROWS, 3 * D), F32), S((128, D), F32),
                   vec, vec, S((128, F * span), F32), S((span // 128, 128), F32), S((span, D), F32), vec,
                   S((1, 3), F32)),
        in_specs=[vm] * 8,
        out_specs=(hbm, hbm, vm, vm, hbm, hbm, vm, vm, hbm, vm, hbm, vm, vm),
        scratch_shapes=[pltpu.SemaphoreType.DMA((6,))],
        compiler_params=pltpu.CompilerParams(vmem_limit_bytes=16 << 20),
    )(*results)
    outs = list(outs)
    for i in (2, 3, 6, 7, 9, 11, 12):
        outs[i] = outs[i].reshape(-1)
    return tuple(outs)


def solution(mesh):
    plan = Plan(mesh.shape["seq"], mesh.shape["ctx"], mesh.shape["fsdp"])
    rows = P(("seq", "ctx", "fsdp"), None)
    f1, f2 = P("fsdp"), P("fsdp", None)
    return jax.shard_map(
        partial(on_device, plan),
        mesh=mesh,
        in_specs=(rows, P("seq"), f1, f1, f2, f2, f1, f1, f2, f1, f2, f1, rows),
        out_specs=(rows, rows, f1, f1, f2, f2, f1, f1, f2, f1, f2, f1, P()),
        check_vma=False,
    )
```
